128 devices in a mesh: grid: 32 (over y_lo, x, z), ch: 4 (over y_hi, core).
Axes of the slice: x: 4, y: 4 (y_hi: 2, y_lo: 2; y = y_hi * 2 + y_lo), z: 4, core: 2. Of those that a mesh axis runs over, the one named last changes fastest.
Arguments:
- inputs: bfloat16 [128, 1024, 512], P('grid', None, 'ch'), may hold values from -6 to 6
- w_gate: bfloat16 [512, 512], P(None, 'ch'), may hold values from -0.25 to 0.25
- w_value: bfloat16 [512, 512], P(None, 'ch'), may hold values from -0.25 to 0.25
- short_filter: bfloat16 [2, 3, 3, 512], P(None, None, None, 'ch'), may hold values from -2 to 2
- row_filter: bfloat16 [1024, 512], P(None, 'ch'), may hold values from -0.1875 to 0.1875
- column_filter: bfloat16 [128, 512], P(None, 'ch'), may hold values from -0.5 to 0.5
- cotangent: bfloat16 [128, 1024, 512], P('grid', None, 'ch'), may hold values from -6 to 6
Outputs:
- gated: bfloat16 [128, 1024, 512], P('grid', None, 'ch')
- input_grad: bfloat16 [128, 1024, 512], P('grid', None, 'ch')
- gate_grad: float32 [512, 512], P('grid', 'ch')
- value_grad: float32 [512, 512], P('grid', 'ch')
- short_grad: float32 [2, 3, 3, 512], P(None, None, None, 'ch')
- row_grad: float32 [1024, 512], P('grid', 'ch')
- column_grad: float32 [128, 512], P('grid', 'ch')
The draws below stay inside these ranges and needn't reach their ends.
All inputs are finite; a program needn't handle non-finite values.
Results may differ from the reference program's by a relative error of at most 0.025.
Values may be sent and summed in bfloat16 or wider, within the bound.
No kernel may reach another device: no remote copies, remote signals or barrier semaphores. Data moves between devices by JAX's collectives and lax.ppermute only.
A program may use at most 128 MiB of HBM per device.

```python
import math
import jax
import jax.numpy as jnp
from jax import lax

D = 512
W = 1024
H = 128


def level_of(own_key, shape, pieces, low, largest):
    loudness, own = 1.0, jax.random.fold_in(own_key, 6)
    for position, blocks in pieces:
        draws = jnp.exp(jax.random.uniform(jax.random.fold_in(own, position), (blocks,), jnp.float32, low / len(pieces), largest / len(pieces)))
        loudness = loudness * jnp.repeat(draws, shape[position] // blocks).reshape([-1 if axis == position else 1 for axis in range(len(shape))])
    return loudness


def noise(own_key, shape, width, bound, cuts=(), dtype=jnp.bfloat16):
    entries = jax.random.normal(own_key, shape, jnp.float32) * width
    if len(cuts) > 0:
        entries = level_of(own_key, shape, cuts, -0.22, 0.18) * entries
    return jnp.clip(entries, min=-bound, max=bound).astype(dtype)


def setup_inputs(seed: int = 0) -> dict:
    splits = jax.random.split(jax.random.key(seed), 8)
    return {
        "inputs": noise(splits[0], (H, W, D), 1.0, 6.0, ((0, 32), (2, 4))),
        "w_gate": noise(splits[1], (D, D), D ** -0.5, 0.25, ((1, 4),)),
        "w_value": noise(splits[2], (D, D), D ** -0.5, 0.25, ((1, 4),)),
        "short_filter": noise(splits[3], (2, 3, 3, D), 9 ** -0.5, 2.0, ((3, 4),)),
        "row_filter": noise(splits[4], (W, D), W ** -0.5, 0.1875, ((1, 4),)),
        "column_filter": noise(splits[5], (H, D), H ** -0.5, 0.5, ((1, 4),)),
        "cotangent": noise(splits[6], (H, W, D), 1.0, 6.0, ((0, 32), (2, 4))),
    }


def featurize(field, kernel):
    height, breadth = (field.shape[0], field.shape[1])
    padded = jnp.pad(field, ((1, 1), (1, 1), (0, 0)))
    total = jnp.zeros_like(field)
    for row_shift in range(3):
        for col_shift in range(3):
            total = total + kernel[row_shift, col_shift] * padded[row_shift:row_shift + height, col_shift:col_shift + breadth]
    return total

def featurize_back(field, kernel):
    height, breadth = (field.shape[0], field.shape[1])
    padded = jnp.pad(field, ((1, 1), (1, 1), (0, 0)))
    total = jnp.zeros_like(field)
    for row_shift in range(3):
        for col_shift in range(3):
            total = total + kernel[row_shift, col_shift] * padded[2 - row_shift:2 - row_shift + height, 2 - col_shift:2 - col_shift + breadth]
    return total

def filter_terms(grad_field, source):
    height, breadth = (grad_field.shape[0], grad_field.shape[1])
    padded = jnp.pad(source, ((1, 1), (1, 1), (0, 0)))
    outer = []
    for row_shift in range(3):
        inner = []
        for col_shift in range(3):
            inner.append(lax.optimization_barrier(jnp.sum(grad_field * padded[row_shift:row_shift + height, col_shift:col_shift + breadth], axis=(0, 1))))
        outer.append(jnp.stack(inner))
    return jnp.stack(outer)

def reference(inputs, w_gate, w_value, short_filter, row_filter, column_filter, cotangent):
    height, breadth, depth = inputs.shape
    scale = 1.0 / math.sqrt(height * breadth)
    flat = inputs.reshape(height * breadth, depth)
    proj_a = jnp.dot(flat, w_gate, preferred_element_type=jnp.float32).astype(jnp.bfloat16).reshape(height, breadth, depth)
    proj_b = jnp.dot(flat, w_value, preferred_element_type=jnp.float32).astype(jnp.bfloat16).reshape(height, breadth, depth)
    kernel = short_filter.astype(jnp.float32)
    pa32 = proj_a.astype(jnp.float32)
    pb32 = proj_b.astype(jnp.float32)
    feat_a = featurize(pa32, kernel[0]).astype(jnp.bfloat16)
    feat_b = featurize(pb32, kernel[1]).astype(jnp.bfloat16)
    fa32 = feat_a.astype(jnp.float32)
    fb32 = feat_b.astype(jnp.float32)
    row_spec = jnp.fft.rfft(row_filter.astype(jnp.float32), axis=0)
    col_spec = jnp.fft.rfft(column_filter.astype(jnp.float32), axis=0)
    spec_b = jnp.fft.rfft(fb32, axis=1)
    mix_row = jnp.fft.irfft(spec_b * row_spec[None], n=breadth, axis=1)
    spec_row = jnp.fft.rfft(mix_row, axis=0)
    mix_col = jnp.fft.irfft(spec_row * col_spec[:, None], n=height, axis=0)
    gated = (fa32 * mix_col).astype(jnp.bfloat16)
    grad_out = cotangent.astype(jnp.float32)
    grad_a = grad_out * mix_col
    grad_col = grad_out * fa32
    spec_gc = jnp.fft.rfft(grad_col, axis=0)
    grad_row = jnp.fft.irfft(spec_gc * jnp.conj(col_spec)[:, None], n=height, axis=0)
    column_grad = jnp.fft.irfft(lax.optimization_barrier(jnp.sum(spec_gc * jnp.conj(spec_row), axis=1)), n=height, axis=0) * scale
    spec_gr = jnp.fft.rfft(grad_row, axis=1)
    grad_b = jnp.fft.irfft(spec_gr * jnp.conj(row_spec)[None], n=breadth, axis=1)
    row_grad = jnp.fft.irfft(lax.optimization_barrier(jnp.sum(spec_gr * jnp.conj(spec_b), axis=0)), n=breadth, axis=0) * scale
    back_a = featurize_back(grad_a, kernel[0]).astype(jnp.bfloat16)
    back_b = featurize_back(grad_b, kernel[1]).astype(jnp.bfloat16)
    short_grad = jnp.stack([filter_terms(grad_a, pa32), filter_terms(grad_b, pb32)]) * scale
    flat_a = back_a.reshape(height * breadth, depth)
    flat_b = back_b.reshape(height * breadth, depth)
    summed = jnp.dot(flat_a, w_gate.T, preferred_element_type=jnp.float32) + jnp.dot(flat_b, w_value.T, preferred_element_type=jnp.float32)
    input_grad = summed.astype(jnp.bfloat16).reshape(height, breadth, depth)
    gate_grad = jnp.dot(flat.T, flat_a, preferred_element_type=jnp.float32) * scale
    value_grad = jnp.dot(flat.T, flat_b, preferred_element_type=jnp.float32) * scale
    return (gated, input_grad, gate_grad, value_grad, short_grad.astype(jnp.float32), row_grad.astype(jnp.float32), column_grad.astype(jnp.float32))
```

```python
import functools
import math

import jax
import jax.numpy as jnp
from jax import lax
from jax.experimental import pallas as pl
from jax.experimental.pallas import tpu as pltpu
from jax.sharding import PartitionSpec as P


BF = jnp.bfloat16
F32 = jnp.float32
EDGE = 8
STEP = 32


def cosine(phase, period):
    folded = phase & (period - 1)
    folded = jnp.minimum(folded, period - folded)
    y = (folded - period // 4).astype(F32) * (2.0 * math.pi / period)
    z = y * y
    series = 1.0 + z * (-1 / 6 + z * (1 / 120 + z * (-1 / 5040 + z * (1 / 362880 - z / 39916800))))
    return -(y * series)


def frequencies(slots, width, owners):
    per_owner = width // owners
    half = per_owner // 2
    place = slots % per_owner
    top = slots == half
    freq = (slots // per_owner) * half + place % half
    freq = jnp.where(top, width // 2, freq)
    offset = jnp.where((place >= half) & ~top, width // 4, 0)
    return freq, offset


def row_matrix(width, owners, slot_dim):
    shape = (width, width)
    freq, offset = frequencies(lax.broadcasted_iota(jnp.int32, shape, slot_dim), width, owners)
    token = lax.broadcasted_iota(jnp.int32, shape, 1 - slot_dim)
    return cosine(freq * token + offset, width).astype(BF)


def column_matrix(height, sign):
    shape = (2 * height, 2 * height)
    i = lax.broadcasted_iota(jnp.int32, shape, 0)
    j = lax.broadcasted_iota(jnp.int32, shape, 1)
    turn = (j // height - i // height) * (-sign * (height // 4))
    return cosine((i % height) * (j % height) + turn + height, height)


def fill_framed(framed, rows_of, channels):
    width = rows_of[0][0].shape[1]
    zeros = jnp.zeros((EDGE, channels), F32)
    for branch in range(2):
        for r in range(len(rows_of)):
            framed[branch, r, pl.ds(0, EDGE), :] = zeros
            framed[branch, r, pl.ds(EDGE + width, EDGE), :] = zeros

    def body(t, _):
        at = pl.multiple_of(t * 32, 32)
        for r, (ref, row) in enumerate(rows_of):
            for branch in range(2):
                v = ref[row, pl.ds(at, 32), pl.ds(branch * channels, channels)]
                framed[branch, r, pl.ds(EDGE + at, 32), :] = v.astype(F32)
        return 0

    lax.fori_loop(0, width // 32, body, 0)


def taps_of(kern, branch, channels):
    return [jnp.broadcast_to(kern[pl.ds(branch * 9 + k, 1), :], (8, channels)) for k in range(9)]


def projected(xs, w):
    size = 2 * xs[0].shape[1]
    total = None
    for n in range(len(xs) // 2):
        pair = jnp.concatenate([xs[2 * n][...], xs[2 * n + 1][...]], axis=1)
        part = jnp.dot(pair, w[pl.ds(n * size, size), :], preferred_element_type=F32)
        total = part if total is None else total + part
    return total.astype(BF)


def project_edge_kernel(x0, x1, x2, x3, w, first, last):
    width = first.shape[1]
    both = projected((x0, x1, x2, x3), w)
    first[0] = both[:width]
    last[0] = both[width:]


def project_mid_kernel(x0, x1, x2, x3, w, middle):
    middle[...] = projected((x0, x1, x2, x3), w).reshape(middle.shape)


def forward_kernel(up, first, middle, last, down, cot, kern, mat, send, feat, framed, cols):
    rows, width, channels = cot.shape
    owners, _, per_owner, _ = send.shape
    inner = [(middle, r) for r in range(rows - 2)]
    fill_framed(framed, [(up, 0), (first, 0), *inner, (last, 0), (down, 0)], channels)
    for branch in range(2):
        taps = taps_of(kern, branch, channels)

        def body(t, _, branch=branch, taps=taps):
            base = pl.multiple_of(t * STEP, STEP)
            done = [[] for _ in range(rows)]
            for p in range(STEP // 8):
                acc = [None] * rows
                for r in range(rows + 2):
                    for j in range(3):
                        v = framed[branch, r, pl.ds(base + 8 * p + EDGE + j - 1, 8), :]
                        for i in range(3):
                            o = r - i
                            if 0 <= o < rows:
                                term = taps[i * 3 + j] * v
                                acc[o] = term if acc[o] is None else acc[o] + term
                for o in range(rows):
                    done[o].append(acc[o])
            for o in range(rows):
                f = jnp.concatenate(done[o], axis=0).astype(BF)
                if branch == 0:
                    feat[o, pl.ds(base, STEP), :] = f
                    g = cot[o, pl.ds(base, STEP), :].astype(F32) * f.astype(F32)
                    cols[pl.ds(base, STEP), pl.ds((rows + o) * channels, channels)] = g.astype(BF)
                else:
                    cols[pl.ds(base, STEP), pl.ds(o * channels, channels)] = f
            return 0

        lax.fori_loop(0, width // STEP, body, 0)
    for n in range(rows):
        spec = jnp.dot(
            mat[...], cols[:, pl.ds(2 * n * channels, 2 * channels)], preferred_element_type=F32
        ).astype(BF)
        for e in range(2):
            send[:, 2 * n + e] = spec[:, e * channels : (e + 1) * channels].reshape(
                owners, per_owner, channels
            )


def column_kernel(
    recv, coef, keep, colr, coli, fwd, inv, send, rowq, colp, stacked, spectra, er, ei
):
    owners, twice, per_owner, channels = recv.shape
    rows = twice // 2
    height = owners * rows
    half = per_owner // 2
    wide = half * channels
    group = 16 // rows

    def place(value, at, offset):
        turned = jnp.swapaxes(value, 0, 1)
        for k in range(half):
            lanes = pl.ds(k * channels + offset, channels)
            stacked[pl.ds(at, 16), lanes] = turned[k]
            stacked[pl.ds(at + height, 16), lanes] = turned[k + half]

    def unpack(n, _):
        at = pl.multiple_of(n * 16, 16)
        mixed = []
        for r in range(16):
            v = recv[n * group + r // rows, r % rows].astype(F32)
            br, bi = v[:half], v[half:]
            both = [br * coef[0] + bi * coef[1], br * coef[2] + bi * coef[3]]
            mixed.append(jnp.concatenate(both, axis=0).astype(BF))
        place(jnp.stack(mixed), at, 0)
        raw = [recv[n * group + r // rows, rows + r % rows] for r in range(16)]
        place(jnp.stack(raw), at, wide)
        return 0

    lax.fori_loop(0, height // 16, unpack, 0)
    for n in range(2 * wide // 512):
        lanes = pl.ds(n * 512, 512)
        spectra[:, lanes] = jnp.dot(fwd[...], stacked[:, lanes], preferred_element_type=F32)

    def products(n, _):
        at = pl.multiple_of(n * 16, 16)
        low, high = pl.ds(at, 16), pl.ds(at + height, 16)
        cr, ci = colr[low, :], coli[low, :]
        sr = jnp.zeros((16, channels), F32)
        si = jnp.zeros((16, channels), F32)
        for k in range(half):
            lanes = pl.ds(k * channels, channels)
            more = pl.ds(k * channels + wide, channels)
            tr, ti = spectra[low, lanes], spectra[high, lanes]
            fr, fi = spectra[low, more], spectra[high, more]
            sr = sr + (fr * tr + fi * ti)
            si = si + (fi * tr - fr * ti)
            stacked[low, lanes] = (tr * cr - ti * ci).astype(BF)
            stacked[high, lanes] = (tr * ci + ti * cr).astype(BF)
            stacked[low, more] = (fr * cr + fi * ci).astype(BF)
            stacked[high, more] = (fi * cr - fr * ci).astype(BF)
        er[low, :] = sr
        ei[low, :] = si
        return 0

    lax.fori_loop(0, height // 16, products, 0)
    for n in range(2 * wide // 512):
        lanes = pl.ds(n * 512, 512)
        spectra[:, lanes] = jnp.dot(inv[...], stacked[:, lanes], preferred_element_type=F32)

    e = jnp.concatenate([er[...], ei[...]], axis=0) * (1.0 / height)
    high = e.astype(BF)
    low = (e - high.astype(F32)).astype(BF)
    top = inv[pl.ds(0, height), :]
    colp[...] = jnp.dot(top, high, preferred_element_type=F32) + jnp.dot(
        top, low, preferred_element_type=F32
    )

    def pack(n, sums):
        p1, p2, p3 = sums
        at = pl.multiple_of(n * 16, 16)

        def taken(offset):
            slots = []
            for part in range(2):
                for k in range(half):
                    lanes = pl.ds(k * channels + offset, channels)
                    slots.append(spectra[pl.ds(at + part * height, 16), lanes])
            return jnp.stack(slots)

        mixed = jnp.swapaxes(taken(0).astype(BF), 0, 1)
        for r in range(16):
            send[n * group + r // rows, r % rows] = mixed[r]
        turned = jnp.swapaxes(taken(wide), 0, 1)
        for r in range(16):
            ar, ai = turned[r, :half], turned[r, half:]
            v = recv[n * group + r // rows, r % rows].astype(F32)
            br, bi = v[:half], v[half:]
            p1 = p1 + ar * br
            p2 = p2 + ai * bi
            p3 = p3 + (ai * br - ar * bi)
            both = [ar * coef[0] + ai * coef[2], ar * coef[1] + ai * coef[3]]
            send[n * group + r // rows, rows + r % rows] = jnp.concatenate(both, axis=0).astype(BF)
        return p1, p2, p3

    none = jnp.zeros((half, channels), F32)
    p1, p2, p3 = lax.fori_loop(0, height // 16, pack, (none, none, none))
    kept = keep[0]
    rowq[pl.ds(0, half), :] = p1 + kept * p2
    rowq[pl.ds(half, half), :] = kept * p3 + (1.0 - kept) * p2


def inverse_kernel(recv, mat, feat, cot, gated, first, middle, last):
    rows, width, channels = cot.shape
    for n in range(rows):
        spec = jnp.concatenate(
            [recv[:, 2 * n + e].reshape(width, channels) for e in range(2)], axis=1
        )
        back = jnp.dot(mat[...], spec, preferred_element_type=F32)
        for e in range(2):
            r = (2 * n + e) % rows
            value = back[:, e * channels : (e + 1) * channels]
            to, row = ((first, 0), *((middle, i) for i in range(rows - 2)), (last, 0))[r]
            if n < rows // 2:
                gated[r] = (feat[r].astype(F32) * value).astype(BF)
                to[row, :, pl.ds(0, channels)] = (cot[r].astype(F32) * value).astype(BF)
            else:
                to[row, :, pl.ds(channels, channels)] = value.astype(BF)


def spread_back(framed, kern, outs, width, channels):
    for branch in range(2):
        taps = taps_of(kern, branch, channels)

        def body(t, _, branch=branch, taps=taps):
            base = pl.multiple_of(t * STEP, STEP)
            done = [[] for _ in outs]
            for p in range(STEP // 8):
                acc = [None] * len(outs)
                needed = sorted({c + 1 - i for _, _, c in outs for i in range(3)})
                for r in needed:
                    for j in range(3):
                        v = framed[branch, r, pl.ds(base + 8 * p + EDGE + 1 - j, 8), :]
                        for n, (_, _, c) in enumerate(outs):
                            i = c + 1 - r
                            if 0 <= i < 3:
                                term = taps[i * 3 + j] * v
                                acc[n] = term if acc[n] is None else acc[n] + term
                for n in range(len(outs)):
                    done[n].append(acc[n])
            for n, (ref, row, _) in enumerate(outs):
                value = jnp.concatenate(done[n], axis=0).astype(BF)
                ref[row, pl.ds(base, STEP), pl.ds(branch * channels, channels)] = value
            return 0

        lax.fori_loop(0, width // STEP, body, 0)


def backward_mid_kernel(gfirst, gmiddle, glast, kern, back, gframed):
    width = gfirst.shape[1]
    channels = kern.shape[1]
    inner = gmiddle.shape[0]
    fill_framed(
        gframed, [(gfirst, 0), *((gmiddle, r) for r in range(inner)), (glast, 0)], channels
    )
    spread_back(gframed, kern, [(back, r, r + 1) for r in range(inner)], width, channels)


def short_kernel(up, first, middle, last, down, gfirst, gmiddle, glast, short, framed):
    width = first.shape[1]
    channels = short.shape[1]
    inner = middle.shape[0]
    rows = inner + 2
    fill_framed(
        framed,
        [(up, 0), (first, 0), *((middle, r) for r in range(inner)), (last, 0), (down, 0)],
        channels,
    )
    grads = [(gfirst, 0), *((gmiddle, r) for r in range(inner)), (glast, 0)]
    for branch in range(2):
        lanes = pl.ds(branch * channels, channels)

        def terms(t, sums, branch=branch, lanes=lanes):
            base = pl.multiple_of(t * 16, 16)
            sums = list(sums)
            both = [ref[row, pl.ds(base, 16), lanes].astype(F32) for ref, row in grads]
            for p in range(2):
                at = base + 8 * p + EDGE
                g = [v[8 * p : 8 * p + 8] for v in both]
                for r in range(rows + 2):
                    for j in range(3):
                        v = framed[branch, r, pl.ds(at + j - 1, 8), :]
                        for i in range(3):
                            o = r - i
                            if 0 <= o < rows:
                                sums[i * 3 + j] = sums[i * 3 + j] + g[o] * v
            return tuple(sums)

        sums = lax.fori_loop(
            0, width // 16, terms, tuple(jnp.zeros((8, channels), F32) for _ in range(9))
        )
        for k in range(9):
            short[pl.ds(branch * 9 + k, 1), :] = jnp.sum(sums[k], axis=0, keepdims=True)


def backward_edge_kernel(gup, gfirst, gmiddle, glast, gdown, kern, back, gframed):
    width = gfirst.shape[1]
    channels = kern.shape[1]
    inner = gmiddle.shape[0]
    fill_framed(
        gframed,
        [(gup, 0), (gfirst, 0), (gmiddle, 0), (gmiddle, inner - 1), (glast, 0), (gdown, 0)],
        channels,
    )
    spread_back(gframed, kern, [(back, 0, 1), (back, 1, 4)], width, channels)


def finish_kernel(kept_edge, edge, kept_mid, mid, grad):
    width = grad.shape[1]
    inner = grad.shape[0] - 2
    for r in range(inner):
        at = pl.ds(r * width, width)
        grad[r + 1] = (kept_mid[at, :] + mid[at, :].astype(F32)).astype(BF)
    for r in range(2):
        at = pl.ds(r * width, width)
        grad[r * (inner + 1)] = (kept_edge[at, :] + edge[at, :].astype(F32)).astype(BF)


def sum_kernel(parts, *outs, scale):
    total = parts[0].astype(F32)
    for n in range(1, parts.shape[0]):
        total = total + parts[n].astype(F32)
    total = total * scale
    at = 0
    for out in outs:
        out[...] = total[at : at + out.shape[0]]
        at += out.shape[0]


def pack_kernel(ch, grad_w, row_part, small, packed):
    owners, _, channels = packed.shape
    parts = 4
    size = grad_w.shape[0] // parts
    each = owners // parts
    deep = size // each
    for k in range(parts):
        at = pl.ds((ch[0] ^ k) * each, each)
        for branch in range(2):
            v = grad_w[pl.ds(k * size, size), pl.ds(branch * channels, channels)].astype(BF)
            packed[at, pl.ds(branch * deep, deep), :] = v.reshape(each, deep, channels)
    per_owner = row_part.shape[0] // owners
    packed[:, pl.ds(2 * deep, per_owner), :] = (
        row_part[...].astype(BF).reshape(owners, per_owner, channels)
    )
    packed[:, pl.ds(2 * deep + per_owner, small.shape[1]), :] = small[...]


def kernel_call(body, outs, scratch, limit, scalars=0, operands=0):
    specs = {}
    if scalars:
        whole = [pl.BlockSpec(memory_space=pltpu.SMEM)] * scalars
        specs["in_specs"] = whole + [pl.BlockSpec(memory_space=pltpu.VMEM)] * operands
    return pl.pallas_call(
        body,
        out_shape=[jax.ShapeDtypeStruct(s, d) for s, d in outs],
        scratch_shapes=[pltpu.VMEM(s, d) for s, d in scratch],
        compiler_params=pltpu.CompilerParams(vmem_limit_bytes=limit << 20),
        **specs,
    )


def local(inputs, w_gate, w_value, short_filter, row_filter, column_filter, cotangent):
    rows, width, channels = inputs.shape
    owners = lax.axis_size("grid")
    parts = lax.axis_size("ch")
    height = column_filter.shape[0]
    per_owner = width // owners
    half = per_owner // 2
    inner = rows - 2
    scale = 1.0 / math.sqrt(height * width)
    ch = lax.axis_index("ch")
    place = lax.axis_index("grid")

    def flipped(value, bit):
        return lax.ppermute(value, "ch", [(i, i ^ bit) for i in range(parts)])

    def halos(first, last):
        up = lax.ppermute(last, "grid", [(i, i + 1) for i in range(owners - 1)])
        down = lax.ppermute(first, "grid", [(i + 1, i) for i in range(owners - 1)])
        return up, down

    def blocks(value):
        size = value.shape[0] // parts
        return [lax.dynamic_slice_in_dim(value, (ch ^ k) * size, size, axis=0) for k in range(parts)]

    edge = jnp.concatenate([inputs[0], inputs[rows - 1]], axis=0)
    mid = inputs[1 : rows - 1].reshape(inner * width, channels)
    edge_across = flipped(edge, 2)
    mid_across = flipped(mid, 2)
    edge_beside = flipped(edge, 1)
    mid_beside = flipped(mid, 1)
    edge_corner = flipped(edge_across, 1)

    w_blocks = blocks(jnp.concatenate([w_gate, w_value], axis=1))
    w_all = jnp.concatenate(w_blocks, axis=0)

    mat = row_matrix(width, owners, 0)
    mat_t = row_matrix(width, owners, 1)
    fwd = column_matrix(height, 1).astype(BF)
    inv = column_matrix(height, -1).astype(BF)
    mine = lax.dynamic_slice_in_dim(mat, place * per_owner, per_owner, axis=0)
    rspec = jnp.dot(mine, row_filter, preferred_element_type=F32)
    is_top = (place == 0) & (jnp.arange(half)[:, None] == 0)
    weight = jnp.where(is_top, 1.0, 2.0) / width
    rre, rim = rspec[:half] * weight, rspec[half:] * weight
    coef = jnp.stack(
        [rre, jnp.where(is_top, 0.0, -rim), jnp.where(is_top, 0.0, rim), jnp.where(is_top, rim, rre)]
    )
    keep = jnp.broadcast_to(jnp.where(is_top, 0.0, 1.0), (1, half, channels))
    cspec = jnp.dot(fwd[:, :height], column_filter, preferred_element_type=F32) / height
    colr, coli = cspec[:height], cspec[height:]
    kern = short_filter.reshape(18, channels).astype(F32)

    line = ((1, width, 2 * channels), BF)
    lines = ((inner, width, 2 * channels), BF)
    edge_blocks = (edge, edge_beside, edge_across, edge_corner)
    first, last = kernel_call(project_edge_kernel, [line, line], [], 12)(*edge_blocks, w_all)
    up, down = halos(first, last)
    mid_across, mat, mat_t, fwd, inv, mine, coef, keep, colr, coli, kern = lax.optimization_barrier(
        (mid_across, mat, mat_t, fwd, inv, mine, coef, keep, colr, coli, kern)
    )
    mid_corner = flipped(mid_across, 1)
    mid_blocks = (mid, mid_beside, mid_across, mid_corner)
    middle = kernel_call(project_mid_kernel, [lines], [], 12)(*mid_blocks, w_all)[0]
    middle, edge_blocks, mid_blocks = lax.optimization_barrier((middle, edge_blocks, mid_blocks))
    gathered_edge = jnp.concatenate(edge_blocks, axis=1)
    gathered_mid = jnp.concatenate(mid_blocks, axis=1)

    def framed(count):
        return ((2, count, width + 2 * EDGE, channels), F32)

    spread = ((owners, 2 * rows, per_owner, channels), BF)
    tile = ((rows, width, channels), BF)
    send, feat = kernel_call(
        forward_kernel, [spread, tile], [framed(rows + 2), ((width, 2 * rows * channels), BF)], 24
    )(up, first, middle, last, down, cotangent, kern, mat)
    recv = lax.all_to_all(send, "grid", split_axis=0, concat_axis=0, tiled=True)
    tall = (2 * height, 2 * half * channels)
    turned, rowq, colp = kernel_call(
        column_kernel,
        [spread, ((per_owner, channels), F32), ((height, channels), F32)],
        [(tall, BF), (tall, F32), ((height, channels), F32), ((height, channels), F32)],
        20,
    )(recv, coef, keep, colr, coli, fwd, inv)
    returned = lax.all_to_all(turned, "grid", split_axis=0, concat_axis=0, tiled=True)
    gated, gfirst, gmiddle, glast = kernel_call(
        inverse_kernel, [tile, line, lines, line], [], 20
    )(returned, mat_t, feat, cotangent)
    gup, gdown = halos(gfirst, glast)
    back_mid = kernel_call(backward_mid_kernel, [lines], [framed(rows)], 16)(
        gfirst, gmiddle, glast, kern
    )[0]
    short = kernel_call(
        short_kernel, [((18, channels), F32)], [framed(rows + 2)], 20
    )(up, first, middle, last, down, gfirst, gmiddle, glast)[0]
    back_edge = kernel_call(backward_edge_kernel, [lines], [framed(6)], 16)(
        gup, gfirst, gmiddle, glast, gdown, kern
    )[0]

    contract = (((1,), (1,)), ((), ()))
    over_tokens = (((0,), (0,)), ((), ()))

    def collected(back):
        def share(k):
            return lax.dot_general(back, w_blocks[k], contract, preferred_element_type=F32)

        beside = flipped(share(3).astype(BF), 1)
        theirs = (share(2) + beside.astype(F32)).astype(BF)
        across = flipped(theirs, 2)
        kept = share(0) + flipped(share(1).astype(BF), 1).astype(F32)
        return kept, across

    back_mid = back_mid.reshape(inner * width, 2 * channels)
    back_edge = back_edge.reshape(2 * width, 2 * channels)
    kept_mid, across_mid = collected(back_mid)
    kept_edge, across_edge = collected(back_edge)
    input_grad = kernel_call(finish_kernel, [tile], [], 12)(
        kept_edge, across_edge, kept_mid, across_mid
    )[0]

    grad_w = lax.dot_general(gathered_mid, back_mid, over_tokens, preferred_element_type=F32)
    grad_w = lax.optimization_barrier(grad_w)
    grad_w = grad_w + lax.dot_general(
        gathered_edge, back_edge, over_tokens, preferred_element_type=F32
    )
    tops = jnp.where(
        (place == 0) & (jnp.arange(per_owner)[:, None] % half == 0), 1.0, 2.0
    ) / width
    row_part = lax.dot_general(mine, (rowq * tops).astype(BF), over_tokens, preferred_element_type=F32)
    small = jnp.concatenate(
        [
            colp.astype(BF).reshape(owners, -1, channels),
            jnp.broadcast_to(short.astype(BF), (owners, 18, channels)),
            jnp.zeros((owners, 2, channels), BF),
        ],
        axis=1,
    )
    small = lax.optimization_barrier(small)
    deep = parts * channels // owners
    packed = kernel_call(
        pack_kernel,
        [((owners, 2 * deep + per_owner + small.shape[1], channels), BF)],
        [],
        16,
        scalars=1,
        operands=3,
    )(ch.reshape(1), grad_w, row_part, small)[0]
    total = lax.all_to_all(packed, "grid", split_axis=0, concat_axis=0, tiled=True)
    sizes = (deep, deep, per_owner, height // owners, 18)
    gate_grad, value_grad, row_share, col_share, short_sum = kernel_call(
        functools.partial(sum_kernel, scale=scale),
        [((size, channels), F32) for size in sizes],
        [],
        12,
    )(total)
    short_grad = short_sum.reshape(2, 3, 3, channels)
    return (gated, input_grad, gate_grad, value_grad, short_grad, row_share, col_share)


def solution(mesh):
    return jax.shard_map(
        local,
        mesh=mesh,
        in_specs=(
            P("grid", None, "ch"),
            P(None, "ch"),
            P(None, "ch"),
            P(None, None, None, "ch"),
            P(None, "ch"),
            P(None, "ch"),
            P("grid", None, "ch"),
        ),
        out_specs=(
            P("grid", None, "ch"),
            P("grid", None, "ch"),
            P("grid", "ch"),
            P("grid", "ch"),
            P(None, None, None, "ch"),
            P("grid", "ch"),
            P("grid", "ch"),
        ),
        check_vma=False,
    )
```

```python
import functools
import math

import jax
import jax.numpy as jnp
from jax import lax
from jax.experimental import pallas as pl
from jax.experimental.pallas import tpu as pltpu
from jax.sharding import PartitionSpec as P


BF = jnp.bfloat16
F32 = jnp.float32
EDGE = 8
STEP = 32


def cosine(phase, period):
    folded = phase & (period - 1)
    folded = jnp.minimum(folded, period - folded)
    y = (folded - period // 4).astype(F32) * (2.0 * math.pi / period)
    z = y * y
    series = 1.0 + z * (-1 / 6 + z * (1 / 120 + z * (-1 / 5040 + z * (1 / 362880 - z / 39916800))))
    return -(y * series)


def frequencies(slots, width, owners):
    per_owner = width // owners
    half = per_owner // 2
    place = slots & (per_owner - 1)
    top = slots == half
    freq = (slots // per_owner) * half + (place & (half - 1))
    freq = jnp.where(top, width // 2, freq)
    offset = jnp.where((place >= half) & ~top, width // 4, 0)
    return freq, offset


def turning(store, phase, step, period, count):
    quarter = period - period // 4
    c, s = cosine(phase, period), cosine(phase + quarter, period)
    dc, ds = cosine(step, period), cosine(step + quarter, period)
    for n in range(count):
        store(n, c)
        c, s = c * dc - s * ds, s * dc + c * ds


def column_matrix(height, sign):
    shape = (2 * height, 2 * height)
    i = lax.broadcasted_iota(jnp.int32, shape, 0)
    j = lax.broadcasted_iota(jnp.int32, shape, 1)
    turn = (jnp.where(j >= height, 1, 0) - jnp.where(i >= height, 1, 0)) * (-sign * (height // 4))
    return cosine((i & (height - 1)) * (j & (height - 1)) + turn + height, height)


def tables_kernel(
    where, w_gate, w_value, short_filter, row_filter, column_filter,
    mat, mat_t, mine, fwd, inv, coef, keep, colr, coli, kern, w_all,
):
    ch, place = where[0], where[1]
    width, channels = row_filter.shape
    height = column_filter.shape[0]
    _, half, _ = coef.shape
    per_owner = 2 * half
    owners = width // per_owner
    shape = (16, 128)
    lane = lax.broadcasted_iota(jnp.int32, shape, 1)
    row = lax.broadcasted_iota(jnp.int32, shape, 0)

    def build(n, _):
        at = pl.multiple_of(n * 16, 16)
        freq, offset = frequencies(row + at, width, owners)

        def along(m, value):
            mat[pl.ds(at, 16), pl.ds(m * 128, 128)] = value.astype(BF)

        turning(along, freq * lane + offset, freq * 128, width, width // 128)
        token = row + at
        per_block = 128 // per_owner * half
        freq, offset = frequencies(lane + 128, width, owners)
        freq = freq - per_block
        highest = 1.0 - 2.0 * (token & 1).astype(F32)

        def across(m, value):
            if m == 0:
                value = jnp.where(lane == half, highest, value)
            mat_t[pl.ds(at, 16), pl.ds(m * 128, 128)] = value.astype(BF)

        turning(across, freq * token + offset, token * per_block, width, width // 128)
        return 0

    lax.fori_loop(0, width // 16, build, 0)
    fwd[...] = column_matrix(height, 1).astype(BF)
    inv[...] = column_matrix(height, -1).astype(BF)
    mine[...] = mat[pl.ds(pl.multiple_of(place * per_owner, per_owner), per_owner), :]
    rspec = jnp.dot(mine[...], row_filter[...], preferred_element_type=F32)
    first = lax.broadcasted_iota(jnp.int32, (half, channels), 0) == 0
    top = jnp.where(first, jnp.where(place == 0, 1.0, 0.0), 0.0)
    weight = (2.0 - top) * (1.0 / width)
    rre, rim = rspec[:half] * weight, rspec[half:] * weight
    rest = 1.0 - top
    coef[0] = rre
    coef[1] = -rim * rest
    coef[2] = rim * rest
    coef[3] = rre * rest + rim * top
    keep[0] = rest
    cspec = jnp.dot(fwd[:, pl.ds(0, height)], column_filter[...], preferred_element_type=F32)
    cspec = cspec * (1.0 / height)
    colr[...] = cspec[:height]
    coli[...] = cspec[height:]
    for b in range(2):
        for i in range(3):
            kern[pl.ds(b * 9 + i * 3, 3), :] = short_filter[b, i].astype(F32)
    parts = w_gate.shape[0] // channels
    for k in range(parts):
        at = pl.ds(pl.multiple_of((ch ^ k) * channels, channels), channels)
        to = pl.ds(k * channels, channels)
        w_all[to, pl.ds(0, channels)] = w_gate[at, :]
        w_all[to, pl.ds(channels, channels)] = w_value[at, :]


def fill_framed(framed, rows_of, channels):
    width = rows_of[0][0].shape[1]
    zeros = jnp.zeros((EDGE, channels), F32)
    for branch in range(2):
        for r in range(len(rows_of)):
            framed[branch, r, pl.ds(0, EDGE), :] = zeros
            framed[branch, r, pl.ds(EDGE + width, EDGE), :] = zeros

    def body(t, _):
        at = pl.multiple_of(t * 32, 32)
        for r, (ref, row) in enumerate(rows_of):
            for branch in range(2):
                v = ref[row, pl.ds(at, 32), pl.ds(branch * channels, channels)]
                framed[branch, r, pl.ds(EDGE + at, 32), :] = v.astype(F32)
        return 0

    lax.fori_loop(0, width // 32, body, 0)


def taps_of(kern, branch, channels):
    return [jnp.broadcast_to(kern[pl.ds(branch * 9 + k, 1), :], (8, channels)) for k in range(9)]


def projected(xs, w):
    size = 2 * xs[0].shape[1]
    total = None
    for n in range(len(xs) // 2):
        pair = jnp.concatenate([xs[2 * n][...], xs[2 * n + 1][...]], axis=1)
        part = jnp.dot(pair, w[pl.ds(n * size, size), :], preferred_element_type=F32)
        total = part if total is None else total + part
    return total.astype(BF)


def project_edge_kernel(x0, x1, x2, x3, w, first, last):
    width = first.shape[1]
    both = projected((x0, x1, x2, x3), w)
    first[0] = both[:width]
    last[0] = both[width:]


def project_mid_kernel(x0, x1, x2, x3, w, middle):
    middle[...] = projected((x0, x1, x2, x3), w).reshape(middle.shape)


def forward_kernel(up, first, middle, last, down, cot, kern, mat, send, feat, framed, cols):
    rows, width, channels = cot.shape
    owners, _, per_owner, _ = send.shape
    inner = [(middle, r) for r in range(rows - 2)]
    fill_framed(framed, [(up, 0), (first, 0), *inner, (last, 0), (down, 0)], channels)
    for branch in range(2):
        taps = taps_of(kern, branch, channels)

        def body(t, _, branch=branch, taps=taps):
            base = pl.multiple_of(t * STEP, STEP)
            done = [[] for _ in range(rows)]
            for p in range(STEP // 8):
                acc = [None] * rows
                for r in range(rows + 2):
                    for j in range(3):
                        v = framed[branch, r, pl.ds(base + 8 * p + EDGE + j - 1, 8), :]
                        for i in range(3):
                            o = r - i
                            if 0 <= o < rows:
                                term = taps[i * 3 + j] * v
                                acc[o] = term if acc[o] is None else acc[o] + term
                for o in range(rows):
                    done[o].append(acc[o])
            for o in range(rows):
                f = jnp.concatenate(done[o], axis=0).astype(BF)
                if branch == 0:
                    feat[o, pl.ds(base, STEP), :] = f
                    g = cot[o, pl.ds(base, STEP), :].astype(F32) * f.astype(F32)
                    cols[pl.ds(base, STEP), pl.ds((rows + o) * channels, channels)] = g.astype(BF)
                else:
                    cols[pl.ds(base, STEP), pl.ds(o * channels, channels)] = f
            return 0

        lax.fori_loop(0, width // STEP, body, 0)
    for n in range(rows):
        spec = jnp.dot(
            mat[...], cols[:, pl.ds(2 * n * channels, 2 * channels)], preferred_element_type=F32
        ).astype(BF)
        for e in range(2):
            send[:, 2 * n + e] = spec[:, e * channels : (e + 1) * channels].reshape(
                owners, per_owner, channels
            )


def column_kernel(
    recv, coef, keep, colr, coli, fwd, inv, mine, send, rowp, colp, stacked, spectra, er, ei
):
    owners, twice, per_owner, channels = recv.shape
    rows = twice // 2
    height = owners * rows
    half = per_owner // 2
    wide = half * channels
    group = 16 // rows

    def place(value, at, offset):
        turned = jnp.swapaxes(value, 0, 1)
        for k in range(half):
            lanes = pl.ds(k * channels + offset, channels)
            stacked[pl.ds(at, 16), lanes] = turned[k]
            stacked[pl.ds(at + height, 16), lanes] = turned[k + half]

    def unpack(n, _):
        at = pl.multiple_of(n * 16, 16)
        mixed = []
        for r in range(16):
            v = recv[n * group + r // rows, r % rows].astype(F32)
            br, bi = v[:half], v[half:]
            both = [br * coef[0] + bi * coef[1], br * coef[2] + bi * coef[3]]
            mixed.append(jnp.concatenate(both, axis=0).astype(BF))
        place(jnp.stack(mixed), at, 0)
        raw = [recv[n * group + r // rows, rows + r % rows] for r in range(16)]
        place(jnp.stack(raw), at, wide)
        return 0

    lax.fori_loop(0, height // 16, unpack, 0)
    for n in range(2 * wide // 512):
        lanes = pl.ds(n * 512, 512)
        spectra[:, lanes] = jnp.dot(fwd[...], stacked[:, lanes], preferred_element_type=F32)

    def products(n, _):
        at = pl.multiple_of(n * 16, 16)
        low, high = pl.ds(at, 16), pl.ds(at + height, 16)
        cr, ci = colr[low, :], coli[low, :]
        sr = jnp.zeros((16, channels), F32)
        si = jnp.zeros((16, channels), F32)
        for k in range(half):
            lanes = pl.ds(k * channels, channels)
            more = pl.ds(k * channels + wide, channels)
            tr, ti = spectra[low, lanes], spectra[high, lanes]
            fr, fi = spectra[low, more], spectra[high, more]
            sr = sr + (fr * tr + fi * ti)
            si = si + (fi * tr - fr * ti)
            stacked[low, lanes] = (tr * cr - ti * ci).astype(BF)
            stacked[high, lanes] = (tr * ci + ti * cr).astype(BF)
            stacked[low, more] = (fr * cr + fi * ci).astype(BF)
            stacked[high, more] = (fi * cr - fr * ci).astype(BF)
        er[low, :] = sr
        ei[low, :] = si
        return 0

    lax.fori_loop(0, height // 16, products, 0)
    for n in range(2 * wide // 512):
        lanes = pl.ds(n * 512, 512)
        spectra[:, lanes] = jnp.dot(inv[...], stacked[:, lanes], preferred_element_type=F32)

    e = jnp.concatenate([er[...], ei[...]], axis=0) * (1.0 / height)
    high = e.astype(BF)
    low = (e - high.astype(F32)).astype(BF)
    top = inv[pl.ds(0, height), :]
    colp[...] = jnp.dot(top, high, preferred_element_type=F32) + jnp.dot(
        top, low, preferred_element_type=F32
    )

    def pack(n, sums):
        p1, p2, p3 = sums
        at = pl.multiple_of(n * 16, 16)

        def taken(offset):
            slots = []
            for part in range(2):
                for k in range(half):
                    lanes = pl.ds(k * channels + offset, channels)
                    slots.append(spectra[pl.ds(at + part * height, 16), lanes])
            return jnp.stack(slots)

        mixed = jnp.swapaxes(taken(0).astype(BF), 0, 1)
        for r in range(16):
            send[n * group + r // rows, r % rows] = mixed[r]
        turned = jnp.swapaxes(taken(wide), 0, 1)
        for r in range(16):
            ar, ai = turned[r, :half], turned[r, half:]
            v = recv[n * group + r // rows, r % rows].astype(F32)
            br, bi = v[:half], v[half:]
            p1 = p1 + ar * br
            p2 = p2 + ai * bi
            p3 = p3 + (ai * br - ar * bi)
            both = [ar * coef[0] + ai * coef[2], ar * coef[1] + ai * coef[3]]
            send[n * group + r // rows, rows + r % rows] = jnp.concatenate(both, axis=0).astype(BF)
        return p1, p2, p3

    none = jnp.zeros((half, channels), F32)
    p1, p2, p3 = lax.fori_loop(0, height // 16, pack, (none, none, none))
    width = owners * per_owner
    kept = keep[0]
    twofold = (1.0 + kept) * (1.0 / width)
    qr = (p1 + kept * p2) * twofold
    qi = (kept * p3 + (1.0 - kept) * p2) * twofold
    rowp[...] = lax.dot_general(
        mine[...],
        jnp.concatenate([qr, qi], axis=0).astype(BF),
        (((0,), (0,)), ((), ())),
        preferred_element_type=F32,
    ).astype(BF)


def inverse_kernel(recv, mat, feat, cot, gated, first, middle, last):
    rows, width, channels = cot.shape
    for n in range(rows):
        spec = jnp.concatenate(
            [recv[:, 2 * n + e].reshape(width, channels) for e in range(2)], axis=1
        )
        back = jnp.dot(mat[...], spec, preferred_element_type=F32)
        for e in range(2):
            r = (2 * n + e) % rows
            value = back[:, e * channels : (e + 1) * channels]
            to, row = ((first, 0), *((middle, i) for i in range(rows - 2)), (last, 0))[r]
            if n < rows // 2:
                gated[r] = (feat[r].astype(F32) * value).astype(BF)
                to[row, :, pl.ds(0, channels)] = (cot[r].astype(F32) * value).astype(BF)
            else:
                to[row, :, pl.ds(channels, channels)] = value.astype(BF)


def spread_back(framed, kern, outs, width, channels):
    for branch in range(2):
        taps = taps_of(kern, branch, channels)

        def body(t, _, branch=branch, taps=taps):
            base = pl.multiple_of(t * STEP, STEP)
            done = [[] for _ in outs]
            for p in range(STEP // 8):
                acc = [None] * len(outs)
                needed = sorted({c + 1 - i for _, _, c in outs for i in range(3)})
                for r in needed:
                    for j in range(3):
                        v = framed[branch, r, pl.ds(base + 8 * p + EDGE + 1 - j, 8), :]
                        for n, (_, _, c) in enumerate(outs):
                            i = c + 1 - r
                            if 0 <= i < 3:
                                term = taps[i * 3 + j] * v
                                acc[n] = term if acc[n] is None else acc[n] + term
                for n in range(len(outs)):
                    done[n].append(acc[n])
            for n, (ref, row, _) in enumerate(outs):
                value = jnp.concatenate(done[n], axis=0).astype(BF)
                ref[row, pl.ds(base, STEP), pl.ds(branch * channels, channels)] = value
            return 0

        lax.fori_loop(0, width // STEP, body, 0)


def backward_mid_kernel(gfirst, gmiddle, glast, kern, back, gframed):
    width = gfirst.shape[1]
    channels = kern.shape[1]
    inner = gmiddle.shape[0]
    fill_framed(
        gframed, [(gfirst, 0), *((gmiddle, r) for r in range(inner)), (glast, 0)], channels
    )
    spread_back(gframed, kern, [(back, r, r + 1) for r in range(inner)], width, channels)


def short_kernel(up, first, middle, last, down, gfirst, gmiddle, glast, short, framed, *, branch):
    width = first.shape[1]
    channels = short.shape[1]
    inner = middle.shape[0]
    rows = inner + 2
    lanes = pl.ds(branch * channels, channels)
    tokens = [(up, 0), (first, 0), *((middle, r) for r in range(inner)), (last, 0), (down, 0)]
    grads = [(gfirst, 0), *((gmiddle, r) for r in range(inner)), (glast, 0)]
    zeros = jnp.zeros((EDGE, channels), F32)
    for r in range(rows + 2):
        framed[r, pl.ds(0, EDGE), :] = zeros
        framed[r, pl.ds(EDGE + width, EDGE), :] = zeros

    def fill(t, _):
        at = pl.multiple_of(t * 32, 32)
        for r, (ref, row) in enumerate(tokens):
            framed[r, pl.ds(EDGE + at, 32), :] = ref[row, pl.ds(at, 32), lanes].astype(F32)
        return 0

    lax.fori_loop(0, width // 32, fill, 0)

    def terms(t, sums):
        base = pl.multiple_of(t * 16, 16)
        sums = list(sums)
        both = [ref[row, pl.ds(base, 16), lanes].astype(F32) for ref, row in grads]
        for p in range(2):
            at = base + 8 * p + EDGE
            g = [v[8 * p : 8 * p + 8] for v in both]
            for r in range(rows + 2):
                for j in range(3):
                    v = framed[r, pl.ds(at + j - 1, 8), :]
                    for i in range(3):
                        o = r - i
                        if 0 <= o < rows:
                            sums[i * 3 + j] = sums[i * 3 + j] + g[o] * v
        return tuple(sums)

    sums = lax.fori_loop(
        0, width // 16, terms, tuple(jnp.zeros((8, channels), F32) for _ in range(9))
    )
    for k in range(9):
        short[pl.ds(k, 1), :] = jnp.sum(sums[k], axis=0, keepdims=True)


def backward_edge_kernel(gup, gfirst, gmiddle, glast, gdown, kern, back, gframed):
    width = gfirst.shape[1]
    channels = kern.shape[1]
    inner = gmiddle.shape[0]
    fill_framed(
        gframed,
        [(gup, 0), (gfirst, 0), (gmiddle, 0), (gmiddle, inner - 1), (glast, 0), (gdown, 0)],
        channels,
    )
    spread_back(gframed, kern, [(back, 0, 1), (back, 1, 4)], width, channels)


def finish_kernel(kept_edge, edge, kept_mid, mid, grad):
    width = grad.shape[1]
    inner = grad.shape[0] - 2
    for r in range(inner):
        at = pl.ds(r * width, width)
        grad[r + 1] = (kept_mid[at, :] + mid[at, :].astype(F32)).astype(BF)
    for r in range(2):
        at = pl.ds(r * width, width)
        grad[r * (inner + 1)] = (kept_edge[at, :] + edge[at, :].astype(F32)).astype(BF)


def sum_kernel(parts, *outs, scale):
    total = parts[0].astype(F32)
    for n in range(1, parts.shape[0]):
        total = total + parts[n].astype(F32)
    total = total * scale
    at = 0
    for out in outs:
        out[...] = total[at : at + out.shape[0]]
        at += out.shape[0]


def pack_kernel(ch, grad_w, row_part, small, packed):
    owners, _, channels = packed.shape
    parts = 4
    size = grad_w.shape[0] // parts
    each = owners // parts
    deep = size // each
    for k in range(parts):
        at = pl.ds((ch[0] ^ k) * each, each)
        for branch in range(2):
            v = grad_w[pl.ds(k * size, size), pl.ds(branch * channels, channels)].astype(BF)
            packed[at, pl.ds(branch * deep, deep), :] = v.reshape(each, deep, channels)
    per_owner = row_part.shape[0] // owners
    packed[:, pl.ds(2 * deep, per_owner), :] = (
        row_part[...].reshape(owners, per_owner, channels)
    )
    packed[:, pl.ds(2 * deep + per_owner, small.shape[1]), :] = small[...]


def kernel_call(body, outs, scratch, limit, scalars=0, operands=0):
    specs = {}
    if scalars:
        whole = [pl.BlockSpec(memory_space=pltpu.SMEM)] * scalars
        specs["in_specs"] = whole + [pl.BlockSpec(memory_space=pltpu.VMEM)] * operands
    return pl.pallas_call(
        body,
        out_shape=[jax.ShapeDtypeStruct(s, d) for s, d in outs],
        scratch_shapes=[pltpu.VMEM(s, d) for s, d in scratch],
        compiler_params=pltpu.CompilerParams(vmem_limit_bytes=limit << 20),
        **specs,
    )


def local(inputs, w_gate, w_value, short_filter, row_filter, column_filter, cotangent):
    rows, width, channels = inputs.shape
    owners = lax.axis_size("grid")
    parts = lax.axis_size("ch")
    height = column_filter.shape[0]
    per_owner = width // owners
    half = per_owner // 2
    inner = rows - 2
    scale = 1.0 / math.sqrt(height * width)
    ch = lax.axis_index("ch")
    place = lax.axis_index("grid")

    def flipped(value, bit):
        return lax.ppermute(value, "ch", [(i, i ^ bit) for i in range(parts)])

    def halos(first, last):
        up = lax.ppermute(last, "grid", [(i, i + 1) for i in range(owners - 1)])
        down = lax.ppermute(first, "grid", [(i + 1, i) for i in range(owners - 1)])
        return up, down

    edge = jnp.concatenate([inputs[0], inputs[rows - 1]], axis=0)
    mid = inputs[1 : rows - 1].reshape(inner * width, channels)
    edge_across = flipped(edge, 2)
    mid_across = flipped(mid, 2)
    edge_beside = flipped(edge, 1)
    mid_beside = flipped(mid, 1)
    edge_corner = flipped(edge_across, 1)

    (mat, mat_t, mine, fwd, inv, coef, keep, colr, coli, kern, w_all) = kernel_call(
        tables_kernel,
        [
            ((width, width), BF),
            ((width, width), BF),
            ((per_owner, width), BF),
            ((2 * height, 2 * height), BF),
            ((2 * height, 2 * height), BF),
            ((4, half, channels), F32),
            ((1, half, channels), F32),
            ((height, channels), F32),
            ((height, channels), F32),
            ((18, channels), F32),
            ((parts * channels, 2 * channels), BF),
        ],
        [],
        12,
        scalars=1,
        operands=5,
    )(jnp.stack([ch, place]), w_gate, w_value, short_filter, row_filter, column_filter)
    w_blocks = [w_all[k * channels : (k + 1) * channels] for k in range(parts)]

    line = ((1, width, 2 * channels), BF)
    lines = ((inner, width, 2 * channels), BF)
    edge_blocks = (edge, edge_beside, edge_across, edge_corner)
    first, last = kernel_call(project_edge_kernel, [line, line], [], 12)(*edge_blocks, w_all)
    up, down = halos(first, last)
    mid_corner = flipped(mid_across, 1)
    mid_blocks = (mid, mid_beside, mid_across, mid_corner)
    middle = kernel_call(project_mid_kernel, [lines], [], 12)(*mid_blocks, w_all)[0]
    middle, edge_blocks, mid_blocks = lax.optimization_barrier((middle, edge_blocks, mid_blocks))
    gathered_edge = jnp.concatenate(edge_blocks, axis=1)
    gathered_mid = jnp.concatenate(mid_blocks, axis=1)

    def framed(count):
        return ((2, count, width + 2 * EDGE, channels), F32)

    spread = ((owners, 2 * rows, per_owner, channels), BF)
    tile = ((rows, width, channels), BF)
    send, feat = kernel_call(
        forward_kernel, [spread, tile], [framed(rows + 2), ((width, 2 * rows * channels), BF)], 24
    )(up, first, middle, last, down, cotangent, kern, mat)
    recv = lax.all_to_all(send, "grid", split_axis=0, concat_axis=0, tiled=True)
    tall = (2 * height, 2 * half * channels)
    turned, row_part, colp = kernel_call(
        column_kernel,
        [spread, ((width, channels), BF), ((height, channels), F32)],
        [(tall, BF), (tall, F32), ((height, channels), F32), ((height, channels), F32)],
        20,
    )(recv, coef, keep, colr, coli, fwd, inv, mine)
    returned = lax.all_to_all(turned, "grid", split_axis=0, concat_axis=0, tiled=True)
    gated, gfirst, gmiddle, glast = kernel_call(
        inverse_kernel, [tile, line, lines, line], [], 20
    )(returned, mat_t, feat, cotangent)
    gup, gdown = halos(gfirst, glast)
    back_mid = kernel_call(backward_mid_kernel, [lines], [framed(rows)], 16)(
        gfirst, gmiddle, glast, kern
    )[0]
    shorts = [
        kernel_call(
            functools.partial(short_kernel, branch=n),
            [((9, channels), F32)],
            [((rows + 2, width + 2 * EDGE, channels), F32)],
            12,
        )(up, first, middle, last, down, gfirst, gmiddle, glast)[0]
        for n in range(2)
    ]
    back_edge = kernel_call(backward_edge_kernel, [lines], [framed(6)], 16)(
        gup, gfirst, gmiddle, glast, gdown, kern
    )[0]

    contract = (((1,), (1,)), ((), ()))
    over_tokens = (((0,), (0,)), ((), ()))

    def collected(back):
        def share(k):
            return lax.dot_general(back, w_blocks[k], contract, preferred_element_type=F32)

        beside = flipped(share(3).astype(BF), 1)
        theirs = (share(2) + beside.astype(F32)).astype(BF)
        across = flipped(theirs, 2)
        back, _ = lax.optimization_barrier((back, theirs))
        kept = share(0) + flipped(share(1).astype(BF), 1).astype(F32)
        return kept, across

    back_mid = back_mid.reshape(inner * width, 2 * channels)
    back_edge = back_edge.reshape(2 * width, 2 * channels)
    kept_mid, across_mid = collected(back_mid)
    kept_edge, across_edge = collected(back_edge)
    input_grad = kernel_call(finish_kernel, [tile], [], 12)(
        kept_edge, across_edge, kept_mid, across_mid
    )[0]

    grad_w = lax.dot_general(gathered_mid, back_mid, over_tokens, preferred_element_type=F32)
    grad_w = lax.optimization_barrier(grad_w)
    grad_w = grad_w + lax.dot_general(
        gathered_edge, back_edge, over_tokens, preferred_element_type=F32
    )
    small = jnp.concatenate(
        [
            colp.astype(BF).reshape(owners, -1, channels),
            *(jnp.broadcast_to(v.astype(BF), (owners, 9, channels)) for v in shorts),
            jnp.zeros((owners, 2, channels), BF),
        ],
        axis=1,
    )
    small = lax.optimization_barrier(small)
    deep = parts * channels // owners
    packed = kernel_call(
        pack_kernel,
        [((owners, 2 * deep + per_owner + small.shape[1], channels), BF)],
        [],
        16,
        scalars=1,
        operands=3,
    )(ch.reshape(1), grad_w, row_part, small)[0]
    total = lax.all_to_all(packed, "grid", split_axis=0, concat_axis=0, tiled=True)
    sizes = (deep, deep, per_owner, height // owners, 18)
    gate_grad, value_grad, row_share, col_share, short_sum = kernel_call(
        functools.partial(sum_kernel, scale=scale),
        [((size, channels), F32) for size in sizes],
        [],
        12,
    )(total)
    short_grad = short_sum.reshape(2, 3, 3, channels)
    return (gated, input_grad, gate_grad, value_grad, short_grad, row_share, col_share)


def solution(mesh):
    return jax.shard_map(
        local,
        mesh=mesh,
        in_specs=(
            P("grid", None, "ch"),
            P(None, "ch"),
            P(None, "ch"),
            P(None, None, None, "ch"),
            P(None, "ch"),
            P(None, "ch"),
            P("grid", None, "ch"),
        ),
        out_specs=(
            P("grid", None, "ch"),
            P("grid", None, "ch"),
            P("grid", "ch"),
            P("grid", "ch"),
            P(None, None, None, "ch"),
            P("grid", "ch"),
            P("grid", "ch"),
        ),
        check_vma=False,
    )
```

```python
import functools
import math

import jax
import jax.numpy as jnp
from jax import lax
from jax.experimental import pallas as pl
from jax.experimental.pallas import tpu as pltpu
from jax.sharding import PartitionSpec as P


BF = jnp.bfloat16
F32 = jnp.float32
EDGE = 8
STEP = 32


def cosine(phase, period):
    folded = phase & (period - 1)
    folded = jnp.minimum(folded, period - folded)
    y = (folded - period // 4).astype(F32) * (2.0 * math.pi / period)
    z = y * y
    series = 1.0 + z * (-1 / 6 + z * (1 / 120 + z * (-1 / 5040 + z * (1 / 362880 - z / 39916800))))
    return -(y * series)


def frequencies(slots, width, owners):
    per_owner = width // owners
    half = per_owner // 2
    place = slots & (per_owner - 1)
    top = slots == half
    freq = (slots // per_owner) * half + (place & (half - 1))
    freq = jnp.where(top, width // 2, freq)
    offset = jnp.where((place >= half) & ~top, width // 4, 0)
    return freq, offset


def turning(store, phase, step, period, count):
    quarter = period - period // 4
    c, s = cosine(phase, period), cosine(phase + quarter, period)
    dc, ds = cosine(step, period), cosine(step + quarter, period)
    for n in range(count):
        store(n, c)
        c, s = c * dc - s * ds, s * dc + c * ds


def column_matrix(height, sign):
    shape = (2 * height, 2 * height)
    i = lax.broadcasted_iota(jnp.int32, shape, 0)
    j = lax.broadcasted_iota(jnp.int32, shape, 1)
    turn = (jnp.where(j >= height, 1, 0) - jnp.where(i >= height, 1, 0)) * (-sign * (height // 4))
    return cosine((i & (height - 1)) * (j & (height - 1)) + turn + height, height)


def tables_kernel(
    where, w_gate, w_value, short_filter, row_filter, column_filter,
    mat, mat_t, mine, fwd, inv, coef, keep, colr, coli, kern, w_all,
):
    ch, place = where[0], where[1]
    width, channels = row_filter.shape
    height = column_filter.shape[0]
    _, half, _ = coef.shape
    per_owner = 2 * half
    owners = width // per_owner
    shape = (16, 128)
    lane = lax.broadcasted_iota(jnp.int32, shape, 1)
    row = lax.broadcasted_iota(jnp.int32, shape, 0)

    def build(n, _):
        at = pl.multiple_of(n * 16, 16)
        freq, offset = frequencies(row + at, width, owners)

        def along(m, value):
            mat[pl.ds(at, 16), pl.ds(m * 128, 128)] = value.astype(BF)

        turning(along, freq * lane + offset, freq * 128, width, width // 128)
        token = row + at
        per_block = 128 // per_owner * half
        freq, offset = frequencies(lane + 128, width, owners)
        freq = freq - per_block
        highest = 1.0 - 2.0 * (token & 1).astype(F32)

        def across(m, value):
            if m == 0:
                value = jnp.where(lane == half, highest, value)
            mat_t[pl.ds(at, 16), pl.ds(m * 128, 128)] = value.astype(BF)

        turning(across, freq * token + offset, token * per_block, width, width // 128)
        return 0

    lax.fori_loop(0, width // 16, build, 0)
    fwd[...] = column_matrix(height, 1).astype(BF)
    inv[...] = column_matrix(height, -1).astype(BF)
    mine[...] = mat[pl.ds(pl.multiple_of(place * per_owner, per_owner), per_owner), :]
    rspec = jnp.dot(mine[...], row_filter[...], preferred_element_type=F32)
    first = lax.broadcasted_iota(jnp.int32, (half, channels), 0) == 0
    top = jnp.where(first, jnp.where(place == 0, 1.0, 0.0), 0.0)
    weight = (2.0 - top) * (1.0 / width)
    rre, rim = rspec[:half] * weight, rspec[half:] * weight
    rest = 1.0 - top
    coef[0] = rre
    coef[1] = -rim * rest
    coef[2] = rim * rest
    coef[3] = rre * rest + rim * top
    keep[0] = rest
    cspec = jnp.dot(fwd[:, pl.ds(0, height)], column_filter[...], preferred_element_type=F32)
    cspec = cspec * (1.0 / height)
    colr[...] = cspec[:height]
    coli[...] = cspec[height:]
    for b in range(2):
        for i in range(3):
            kern[pl.ds(b * 9 + i * 3, 3), :] = short_filter[b, i].astype(F32)
    parts = w_gate.shape[0] // channels
    for k in range(parts):
        at = pl.ds(pl.multiple_of((ch ^ k) * channels, channels), channels)
        to = pl.ds(k * channels, channels)
        w_all[to, pl.ds(0, channels)] = w_gate[at, :]
        w_all[to, pl.ds(channels, channels)] = w_value[at, :]


def fill_framed(framed, rows_of, channels, branches=(0, 1)):
    width = sum(ref.shape[-2] for ref, _ in rows_of[-2])
    zeros = jnp.zeros((EDGE, channels), F32)
    for n in range(len(branches)):
        for r in range(len(rows_of)):
            framed[n, r, pl.ds(0, EDGE), :] = zeros
            framed[n, r, pl.ds(EDGE + width, EDGE), :] = zeros

    def body(t, _):
        at = pl.multiple_of(t * 16, 16)
        for r, pieces in enumerate(rows_of):
            for side in range(2):
                ref, row = pieces[side % len(pieces)]
                start = at + (side * width // 2 if len(pieces) == 1 else 0)
                for n, branch in enumerate(branches):
                    v = ref[row, pl.ds(start, 16), pl.ds(branch * channels, channels)]
                    framed[n, r, pl.ds(EDGE + at + side * width // 2, 16), :] = v.astype(F32)
        return 0

    lax.fori_loop(0, width // 32, body, 0)


def taps_of(kern, branch, channels):
    return [jnp.broadcast_to(kern[pl.ds(branch * 9 + k, 1), :], (8, channels)) for k in range(9)]


def projected(xs, w):
    size = 2 * xs[0].shape[1]
    total = None
    for n in range(len(xs) // 2):
        pair = jnp.concatenate([xs[2 * n][...], xs[2 * n + 1][...]], axis=1)
        part = jnp.dot(pair, w[pl.ds(n * size, size), :], preferred_element_type=F32)
        total = part if total is None else total + part
    return total.astype(BF)


def project_edge_kernel(x0, x1, x2, x3, w, first, last):
    width = first.shape[1]
    both = projected((x0, x1, x2, x3), w)
    first[0] = both[:width]
    last[0] = both[width:]


def project_mid_kernel(x0, x1, x2, x3, w, middle):
    middle[...] = projected((x0, x1, x2, x3), w).reshape(middle.shape)


def forward_rows(framed, outs, cot, kern, mat, feat, cols, put):
    _, width, channels = cot.shape
    for branch in range(2):
        taps = taps_of(kern, branch, channels)

        def body(t, _, branch=branch, taps=taps):
            base = pl.multiple_of(t * STEP, STEP)
            done = [[] for _ in outs]
            for p in range(STEP // 8):
                acc = [None] * len(outs)
                for r in sorted({c + i - 1 for _, c in outs for i in range(3)}):
                    for j in range(3):
                        v = framed[branch, r, pl.ds(base + 8 * p + EDGE + j - 1, 8), :]
                        for n, (_, c) in enumerate(outs):
                            i = r - c + 1
                            if 0 <= i < 3:
                                term = taps[i * 3 + j] * v
                                acc[n] = term if acc[n] is None else acc[n] + term
                for n in range(len(outs)):
                    done[n].append(acc[n])
            for n, (row, _) in enumerate(outs):
                f = jnp.concatenate(done[n], axis=0).astype(BF)
                if branch == 0:
                    feat[n, pl.ds(base, STEP), :] = f
                    g = cot[row, pl.ds(base, STEP), :].astype(F32) * f.astype(F32)
                    lanes = pl.ds((len(outs) + n) * channels, channels)
                    cols[pl.ds(base, STEP), lanes] = g.astype(BF)
                else:
                    cols[pl.ds(base, STEP), pl.ds(n * channels, channels)] = f
            return 0

        lax.fori_loop(0, width // STEP, body, 0)
    for n in range(len(outs)):
        spec = jnp.dot(
            mat[...], cols[:, pl.ds(2 * n * channels, 2 * channels)], preferred_element_type=F32
        ).astype(BF)
        for e in range(2):
            put(2 * n + e, spec[:, e * channels : (e + 1) * channels])


def forward_mid_kernel(f0, f1, middle, l0, l1, cot, kern, mat, part, feat, framed, cols):
    channels = cot.shape[2]
    inner = middle.shape[0]
    owners, _, per_owner, _ = part.shape
    whole = [((middle, r),) for r in range(inner)]
    fill_framed(framed, [((f0, 0), (f1, 0)), *whole, ((l0, 0), (l1, 0))], channels)

    def put(block, spec):
        part[:, block] = spec.reshape(owners, per_owner, channels)

    outs = [(r + 1, r + 1) for r in range(inner)]
    forward_rows(framed, outs, cot, kern, mat, feat, cols, put)


def forward_edge_kernel(
    u0, u1, f0, f1, middle, l0, l1, d0, d1, cot, kern, mat, part, send, feat, framed, cols
):
    rows, _, channels = cot.shape
    inner = rows - 2
    owners, _, per_owner, _ = send.shape
    for r in range(inner):
        send[:, r + 1] = part[:, r]
        send[:, rows + r + 1] = part[:, inner + r]
    fill_framed(
        framed,
        [
            ((u0, 0), (u1, 0)),
            ((f0, 0), (f1, 0)),
            ((middle, 0),),
            ((middle, inner - 1),),
            ((l0, 0), (l1, 0)),
            ((d0, 0), (d1, 0)),
        ],
        channels,
    )

    def put(block, spec):
        to = (block // 2) * rows + (block % 2) * (rows - 1)
        send[:, to] = spec.reshape(owners, per_owner, channels)

    forward_rows(framed, [(0, 1), (rows - 1, 4)], cot, kern, mat, feat, cols, put)


def column_kernel(
    recv, coef, keep, colr, coli, fwd, inv, mine, send, rowp, colp, stacked, spectra, er, ei
):
    owners, twice, per_owner, channels = recv.shape
    rows = twice // 2
    height = owners * rows
    half = per_owner // 2
    wide = half * channels
    group = 16 // rows

    def place(value, at, offset):
        turned = jnp.swapaxes(value, 0, 1)
        for k in range(half):
            lanes = pl.ds(k * channels + offset, channels)
            stacked[pl.ds(at, 16), lanes] = turned[k]
            stacked[pl.ds(at + height, 16), lanes] = turned[k + half]

    def unpack(n, _):
        at = pl.multiple_of(n * 16, 16)
        mixed = []
        for r in range(16):
            v = recv[n * group + r // rows, r % rows].astype(F32)
            br, bi = v[:half], v[half:]
            both = [br * coef[0] + bi * coef[1], br * coef[2] + bi * coef[3]]
            mixed.append(jnp.concatenate(both, axis=0).astype(BF))
        place(jnp.stack(mixed), at, 0)
        raw = [recv[n * group + r // rows, rows + r % rows] for r in range(16)]
        place(jnp.stack(raw), at, wide)
        return 0

    lax.fori_loop(0, height // 16, unpack, 0)
    for n in range(2 * wide // 512):
        lanes = pl.ds(n * 512, 512)
        spectra[:, lanes] = jnp.dot(fwd[...], stacked[:, lanes], preferred_element_type=F32)

    def products(n, _):
        at = pl.multiple_of(n * 16, 16)
        low, high = pl.ds(at, 16), pl.ds(at + height, 16)
        cr, ci = colr[low, :], coli[low, :]
        sr = jnp.zeros((16, channels), F32)
        si = jnp.zeros((16, channels), F32)
        for k in range(half):
            lanes = pl.ds(k * channels, channels)
            more = pl.ds(k * channels + wide, channels)
            tr, ti = spectra[low, lanes], spectra[high, lanes]
            fr, fi = spectra[low, more], spectra[high, more]
            sr = sr + (fr * tr + fi * ti)
            si = si + (fi * tr - fr * ti)
            stacked[low, lanes] = (tr * cr - ti * ci).astype(BF)
            stacked[high, lanes] = (tr * ci + ti * cr).astype(BF)
            stacked[low, more] = (fr * cr + fi * ci).astype(BF)
            stacked[high, more] = (fi * cr - fr * ci).astype(BF)
        er[low, :] = sr
        ei[low, :] = si
        return 0

    lax.fori_loop(0, height // 16, products, 0)
    for n in range(2 * wide // 512):
        lanes = pl.ds(n * 512, 512)
        spectra[:, lanes] = jnp.dot(inv[...], stacked[:, lanes], preferred_element_type=F32)

    e = jnp.concatenate([er[...], ei[...]], axis=0) * (1.0 / height)
    high = e.astype(BF)
    low = (e - high.astype(F32)).astype(BF)
    top = inv[pl.ds(0, height), :]
    colp[...] = jnp.dot(top, high, preferred_element_type=F32) + jnp.dot(
        top, low, preferred_element_type=F32
    )

    def pack(n, sums):
        p1, p2, p3 = sums
        at = pl.multiple_of(n * 16, 16)

        def taken(offset):
            slots = []
            for part in range(2):
                for k in range(half):
                    lanes = pl.ds(k * channels + offset, channels)
                    slots.append(spectra[pl.ds(at + part * height, 16), lanes])
            return jnp.stack(slots)

        mixed = jnp.swapaxes(taken(0).astype(BF), 0, 1)
        for r in range(16):
            send[n * group + r // rows, r % rows] = mixed[r]
        turned = jnp.swapaxes(taken(wide), 0, 1)
        for r in range(16):
            ar, ai = turned[r, :half], turned[r, half:]
            v = recv[n * group + r // rows, r % rows].astype(F32)
            br, bi = v[:half], v[half:]
            p1 = p1 + ar * br
            p2 = p2 + ai * bi
            p3 = p3 + (ai * br - ar * bi)
            both = [ar * coef[0] + ai * coef[2], ar * coef[1] + ai * coef[3]]
            send[n * group + r // rows, rows + r % rows] = jnp.concatenate(both, axis=0).astype(BF)
        return p1, p2, p3

    none = jnp.zeros((half, channels), F32)
    p1, p2, p3 = lax.fori_loop(0, height // 16, pack, (none, none, none))
    width = owners * per_owner
    kept = keep[0]
    twofold = (1.0 + kept) * (1.0 / width)
    qr = (p1 + kept * p2) * twofold
    qi = (kept * p3 + (1.0 - kept) * p2) * twofold
    rowp[...] = lax.dot_general(
        mine[...],
        jnp.concatenate([qr, qi], axis=0).astype(BF),
        (((0,), (0,)), ((), ())),
        preferred_element_type=F32,
    ).astype(BF)


def inverse_kernel(recv, mat, feat_edge, feat_mid, cot, gated, first, middle, last):
    rows, width, channels = cot.shape
    for n in range(rows):
        spec = jnp.concatenate(
            [recv[:, 2 * n + e].reshape(width, channels) for e in range(2)], axis=1
        )
        back = jnp.dot(mat[...], spec, preferred_element_type=F32)
        for e in range(2):
            r = (2 * n + e) % rows
            value = back[:, e * channels : (e + 1) * channels]
            to, row = ((first, 0), *((middle, i) for i in range(rows - 2)), (last, 0))[r]
            if n < rows // 2:
                feat = feat_mid[r - 1] if 0 < r < rows - 1 else feat_edge[r // (rows - 1)]
                gated[r] = (feat.astype(F32) * value).astype(BF)
                to[row, :, pl.ds(0, channels)] = (cot[r].astype(F32) * value).astype(BF)
            else:
                to[row, :, pl.ds(channels, channels)] = value.astype(BF)


def spread_back(framed, kern, outs, width, channels, skip=0):
    for branch in range(2):
        taps = taps_of(kern, branch, channels)

        def body(t, _, branch=branch, taps=taps):
            base = pl.multiple_of(t * STEP, STEP)
            done = [[] for _ in outs]
            for p in range(STEP // 8):
                acc = [None] * len(outs)
                needed = sorted({c + 1 - i for _, _, c in outs for i in range(3)})
                for r in needed:
                    for j in range(3):
                        v = framed[branch, r, pl.ds(base + skip + 8 * p + EDGE + 1 - j, 8), :]
                        for n, (_, _, c) in enumerate(outs):
                            i = c + 1 - r
                            if 0 <= i < 3:
                                term = taps[i * 3 + j] * v
                                acc[n] = term if acc[n] is None else acc[n] + term
                for n in range(len(outs)):
                    done[n].append(acc[n])
            for n, (ref, row, _) in enumerate(outs):
                value = jnp.concatenate(done[n], axis=0).astype(BF)
                ref[row, pl.ds(base, STEP), pl.ds(branch * channels, channels)] = value
            return 0

        lax.fori_loop(0, width // STEP, body, 0)


def backward_mid_kernel(gfirst, gmiddle, glast, kern, back, gframed):
    width = gfirst.shape[1]
    channels = kern.shape[1]
    inner = gmiddle.shape[0]
    whole = [((gmiddle, r),) for r in range(inner)]
    fill_framed(gframed, [((gfirst, 0),), *whole, ((glast, 0),)], channels)
    spread_back(gframed, kern, [(back, r, r + 1) for r in range(inner)], width, channels)


def short_kernel(
    u0, u1, f0, f1, middle, l0, l1, d0, d1, gfirst, gmiddle, glast, short, framed, *, branch
):
    width = gfirst.shape[1]
    channels = short.shape[1]
    inner = middle.shape[0]
    rows = inner + 2
    lanes = pl.ds(branch * channels, channels)
    whole = [((middle, r),) for r in range(inner)]
    halves = [((u0, 0), (u1, 0)), ((f0, 0), (f1, 0))], [((l0, 0), (l1, 0)), ((d0, 0), (d1, 0))]
    fill_framed(framed, [*halves[0], *whole, *halves[1]], channels, (branch,))
    grads = [(gfirst, 0), *((gmiddle, r) for r in range(inner)), (glast, 0)]

    def terms(t, sums):
        base = pl.multiple_of(t * 16, 16)
        sums = list(sums)
        both = [ref[row, pl.ds(base, 16), lanes].astype(F32) for ref, row in grads]
        for p in range(2):
            at = base + 8 * p + EDGE
            g = [v[8 * p : 8 * p + 8] for v in both]
            for r in range(rows + 2):
                for j in range(3):
                    v = framed[0, r, pl.ds(at + j - 1, 8), :]
                    for i in range(3):
                        o = r - i
                        if 0 <= o < rows:
                            sums[i * 3 + j] = sums[i * 3 + j] + g[o] * v
        return tuple(sums)

    sums = lax.fori_loop(
        0, width // 16, terms, tuple(jnp.zeros((8, channels), F32) for _ in range(9))
    )
    for k in range(9):
        short[pl.ds(k, 1), :] = jnp.sum(sums[k], axis=0, keepdims=True)


def backward_edge_kernel(gup, gfirst, gmiddle, glast, gdown, kern, back, gframed):
    channels = kern.shape[1]
    inner = gmiddle.shape[0]
    fill_framed(
        gframed,
        [
            ((gup, 0),),
            ((gfirst, 0),),
            ((gmiddle, 0),),
            ((gmiddle, inner - 1),),
            ((glast, 0),),
            ((gdown, 0),),
        ],
        channels,
    )
    size = back.shape[2]
    for side in range(2):
        to = back.at[side]
        spread_back(gframed, kern, [(to, 0, 1), (to, 1, 4)], size, channels, side * size)


def finish_kernel(kept_edge, edge, kept_mid, mid, grad):
    width = grad.shape[1]
    inner = grad.shape[0] - 2
    for r in range(inner):
        at = pl.ds(r * width, width)
        grad[r + 1] = (kept_mid[at, :] + mid[at, :].astype(F32)).astype(BF)
    size = width // 2
    for side in range(2):
        for r in range(2):
            at = pl.ds(side * width + r * size, size)
            value = (kept_edge[at, :] + edge[at, :].astype(F32)).astype(BF)
            grad[r * (inner + 1), pl.ds(side * size, size), :] = value


def sum_kernel(parts, *outs, scale):
    total = parts[0].astype(F32)
    for n in range(1, parts.shape[0]):
        total = total + parts[n].astype(F32)
    total = total * scale
    at = 0
    for out in outs:
        out[...] = total[at : at + out.shape[0]]
        at += out.shape[0]


def pack_kernel(ch, grad_w, row_part, small, packed):
    owners, _, channels = packed.shape
    parts = 4
    size = grad_w.shape[0] // parts
    each = owners // parts
    deep = size // each
    for k in range(parts):
        at = pl.ds((ch[0] ^ k) * each, each)
        for branch in range(2):
            v = grad_w[pl.ds(k * size, size), pl.ds(branch * channels, channels)].astype(BF)
            packed[at, pl.ds(branch * deep, deep), :] = v.reshape(each, deep, channels)
    per_owner = row_part.shape[0] // owners
    packed[:, pl.ds(2 * deep, per_owner), :] = (
        row_part[...].reshape(owners, per_owner, channels)
    )
    packed[:, pl.ds(2 * deep + per_owner, small.shape[1]), :] = small[...]


def kernel_call(body, outs, scratch, limit, scalars=0, operands=0):
    specs = {}
    if scalars:
        whole = [pl.BlockSpec(memory_space=pltpu.SMEM)] * scalars
        specs["in_specs"] = whole + [pl.BlockSpec(memory_space=pltpu.VMEM)] * operands
    return pl.pallas_call(
        body,
        out_shape=[jax.ShapeDtypeStruct(s, d) for s, d in outs],
        scratch_shapes=[pltpu.VMEM(s, d) for s, d in scratch],
        compiler_params=pltpu.CompilerParams(vmem_limit_bytes=limit << 20),
        **specs,
    )


def local(inputs, w_gate, w_value, short_filter, row_filter, column_filter, cotangent):
    rows, width, channels = inputs.shape
    owners = lax.axis_size("grid")
    parts = lax.axis_size("ch")
    height = column_filter.shape[0]
    per_owner = width // owners
    half = per_owner // 2
    inner = rows - 2
    scale = 1.0 / math.sqrt(height * width)
    ch = lax.axis_index("ch")
    place = lax.axis_index("grid")

    def flipped(value, bit):
        return lax.ppermute(value, "ch", [(i, i ^ bit) for i in range(parts)])

    def halos(first, last):
        up = lax.ppermute(last, "grid", [(i, i + 1) for i in range(owners - 1)])
        down = lax.ppermute(first, "grid", [(i + 1, i) for i in range(owners - 1)])
        return up, down

    size = width // 2
    edges, edges_across, edges_beside = [], [], []
    for n in range(2):
        lines_of = [inputs[r, n * size : (n + 1) * size] for r in (0, rows - 1)]
        edges.append(jnp.concatenate(lines_of, axis=0))
        edges_across.append(flipped(edges[n], 2))
    mid = inputs[1 : rows - 1].reshape(inner * width, channels)
    mid_across = flipped(mid, 2)
    edges_beside = [flipped(edge, 1) for edge in edges]
    mid_beside = flipped(mid, 1)

    (mat, mat_t, mine, fwd, inv, coef, keep, colr, coli, kern, w_all) = kernel_call(
        tables_kernel,
        [
            ((width, width), BF),
            ((width, width), BF),
            ((per_owner, width), BF),
            ((2 * height, 2 * height), BF),
            ((2 * height, 2 * height), BF),
            ((4, half, channels), F32),
            ((1, half, channels), F32),
            ((height, channels), F32),
            ((height, channels), F32),
            ((18, channels), F32),
            ((parts * channels, 2 * channels), BF),
        ],
        [],
        12,
        scalars=1,
        operands=5,
    )(jnp.stack([ch, place]), w_gate, w_value, short_filter, row_filter, column_filter)
    w_blocks = [w_all[k * channels : (k + 1) * channels] for k in range(parts)]

    line = ((1, width, 2 * channels), BF)
    lines = ((inner, width, 2 * channels), BF)
    side = ((1, size, 2 * channels), BF)
    edge_blocks, ends, around = [], [], []
    for n in range(2):
        corner = flipped(edges_across[n], 1)
        edge_blocks.append((edges[n], edges_beside[n], edges_across[n], corner))
        ends.append(kernel_call(project_edge_kernel, [side, side], [], 12)(*edge_blocks[n], w_all))
        around.append(halos(*ends[n]))
    firsts, lasts = zip(*ends)
    ups, downs = zip(*around)
    mid_corner = flipped(mid_across, 1)
    mid_blocks = (mid, mid_beside, mid_across, mid_corner)
    middle = kernel_call(project_mid_kernel, [lines], [], 12)(*mid_blocks, w_all)[0]
    middle, edge_blocks, mid_blocks = lax.optimization_barrier((middle, edge_blocks, mid_blocks))
    gathered_edge = jnp.concatenate([jnp.concatenate(b, axis=1) for b in edge_blocks], axis=0)
    gathered_mid = jnp.concatenate(mid_blocks, axis=1)

    def framed(count):
        return ((2, count, width + 2 * EDGE, channels), F32)

    spread = ((owners, 2 * rows, per_owner, channels), BF)
    tile = ((rows, width, channels), BF)
    pair = ((2, width, channels), BF)
    cols = ((width, 4 * channels), BF)
    part, feat_mid = kernel_call(
        forward_mid_kernel,
        [((owners, rows, per_owner, channels), BF), pair],
        [framed(rows), cols],
        16,
    )(*firsts, middle, *lasts, cotangent, kern, mat)
    send, feat_edge = kernel_call(
        forward_edge_kernel, [spread, pair], [framed(6), cols], 20
    )(*ups, *firsts, middle, *lasts, *downs, cotangent, kern, mat, part)
    recv = lax.all_to_all(send, "grid", split_axis=0, concat_axis=0, tiled=True)
    tall = (2 * height, 2 * half * channels)
    turned, row_part, colp = kernel_call(
        column_kernel,
        [spread, ((width, channels), BF), ((height, channels), F32)],
        [(tall, BF), (tall, F32), ((height, channels), F32), ((height, channels), F32)],
        20,
    )(recv, coef, keep, colr, coli, fwd, inv, mine)
    returned = lax.all_to_all(turned, "grid", split_axis=0, concat_axis=0, tiled=True)
    gated, gfirst, gmiddle, glast = kernel_call(
        inverse_kernel, [tile, line, lines, line], [], 20
    )(returned, mat_t, feat_edge, feat_mid, cotangent)
    gup, gdown = halos(gfirst, glast)
    back_mid = kernel_call(backward_mid_kernel, [lines], [framed(rows)], 16)(
        gfirst, gmiddle, glast, kern
    )[0]
    shorts = [
        kernel_call(
            functools.partial(short_kernel, branch=n),
            [((9, channels), F32)],
            [((1, rows + 2, width + 2 * EDGE, channels), F32)],
            12,
        )(*ups, *firsts, middle, *lasts, *downs, gfirst, gmiddle, glast)[0]
        for n in range(2)
    ]
    halved = ((2, 2, size, 2 * channels), BF)
    back_edge = kernel_call(backward_edge_kernel, [halved], [framed(6)], 16)(
        gup, gfirst, gmiddle, glast, gdown, kern
    )[0]

    contract = (((1,), (1,)), ((), ()))
    over_tokens = (((0,), (0,)), ((), ()))

    def collected(back):
        def share(k):
            return lax.dot_general(back, w_blocks[k], contract, preferred_element_type=F32)

        beside = flipped(share(3).astype(BF), 1)
        theirs = (share(2) + beside.astype(F32)).astype(BF)
        across = flipped(theirs, 2)
        back, _ = lax.optimization_barrier((back, theirs))
        kept = share(0) + flipped(share(1).astype(BF), 1).astype(F32)
        return kept, across

    back_mid = back_mid.reshape(inner * width, 2 * channels)
    back_edge = back_edge.reshape(2 * width, 2 * channels)
    kept_mid, across_mid = collected(back_mid)
    kept_edge, across_edge = collected(back_edge)
    input_grad = kernel_call(finish_kernel, [tile], [], 12)(
        kept_edge, across_edge, kept_mid, across_mid
    )[0]

    grad_w = lax.dot_general(gathered_mid, back_mid, over_tokens, preferred_element_type=F32)
    grad_w = lax.optimization_barrier(grad_w)
    grad_w = grad_w + lax.dot_general(
        gathered_edge, back_edge, over_tokens, preferred_element_type=F32
    )
    small = jnp.concatenate(
        [
            colp.astype(BF).reshape(owners, -1, channels),
            *(jnp.broadcast_to(v.astype(BF), (owners, 9, channels)) for v in shorts),
            jnp.zeros((owners, 2, channels), BF),
        ],
        axis=1,
    )
    small = lax.optimization_barrier(small)
    deep = parts * channels // owners
    packed = kernel_call(
        pack_kernel,
        [((owners, 2 * deep + per_owner + small.shape[1], channels), BF)],
        [],
        16,
        scalars=1,
        operands=3,
    )(ch.reshape(1), grad_w, row_part, small)[0]
    total = lax.all_to_all(packed, "grid", split_axis=0, concat_axis=0, tiled=True)
    sizes = (deep, deep, per_owner, height // owners, 18)
    gate_grad, value_grad, row_share, col_share, short_sum = kernel_call(
        functools.partial(sum_kernel, scale=scale),
        [((size, channels), F32) for size in sizes],
        [],
        12,
    )(total)
    short_grad = short_sum.reshape(2, 3, 3, channels)
    return (gated, input_grad, gate_grad, value_grad, short_grad, row_share, col_share)


def solution(mesh):
    return jax.shard_map(
        local,
        mesh=mesh,
        in_specs=(
            P("grid", None, "ch"),
            P(None, "ch"),
            P(None, "ch"),
            P(None, None, None, "ch"),
            P(None, "ch"),
            P(None, "ch"),
            P("grid", None, "ch"),
        ),
        out_specs=(
            P("grid", None, "ch"),
            P("grid", None, "ch"),
            P("grid", "ch"),
            P("grid", "ch"),
            P(None, None, None, "ch"),
            P("grid", "ch"),
            P("grid", "ch"),
        ),
        check_vma=False,
    )
```

```python
import functools
import math

import jax
import jax.numpy as jnp
from jax import lax
from jax.experimental import pallas as pl
from jax.experimental.pallas import tpu as pltpu
from jax.sharding import PartitionSpec as P


BF = jnp.bfloat16
F32 = jnp.float32
EDGE = 8
STEP = 32


def cosine(phase, period):
    folded = phase & (period - 1)
    folded = jnp.minimum(folded, period - folded)
    y = (folded - period // 4).astype(F32) * (2.0 * math.pi / period)
    z = y * y
    series = 1.0 + z * (-1 / 6 + z * (1 / 120 + z * (-1 / 5040 + z * (1 / 362880 - z / 39916800))))
    return -(y * series)


def frequencies(slots, width, owners):
    per_owner = width // owners
    half = per_owner // 2
    place = slots & (per_owner - 1)
    top = slots == half
    freq = (slots // per_owner) * half + (place & (half - 1))
    freq = jnp.where(top, width // 2, freq)
    offset = jnp.where((place >= half) & ~top, width // 4, 0)
    return freq, offset


def turning(store, phase, step, period, count):
    quarter = period - period // 4
    c, s = cosine(phase, period), cosine(phase + quarter, period)
    dc, ds = cosine(step, period), cosine(step + quarter, period)
    for n in range(count):
        store(n, c)
        c, s = c * dc - s * ds, s * dc + c * ds


def column_matrix(height, sign):
    shape = (2 * height, 2 * height)
    i = lax.broadcasted_iota(jnp.int32, shape, 0)
    j = lax.broadcasted_iota(jnp.int32, shape, 1)
    turn = (jnp.where(j >= height, 1, 0) - jnp.where(i >= height, 1, 0)) * (-sign * (height // 4))
    return cosine((i & (height - 1)) * (j & (height - 1)) + turn + height, height)


def tables_kernel(
    where, w_gate, w_value, short_filter, row_filter, column_filter,
    mat, mat_t, mine, fwd, inv, coef, keep, colr, coli, kern, w_all,
):
    ch, place = where[0], where[1]
    width, channels = row_filter.shape
    height = column_filter.shape[0]
    _, half, _ = coef.shape
    per_owner = 2 * half
    owners = width // per_owner
    shape = (16, 128)
    lane = lax.broadcasted_iota(jnp.int32, shape, 1)
    row = lax.broadcasted_iota(jnp.int32, shape, 0)

    def build(n, _):
        at = pl.multiple_of(n * 16, 16)
        freq, offset = frequencies(row + at, width, owners)

        def along(m, value):
            mat[pl.ds(at, 16), pl.ds(m * 128, 128)] = value.astype(BF)

        turning(along, freq * lane + offset, freq * 128, width, width // 128)
        token = row + at
        per_block = 128 // per_owner * half
        freq, offset = frequencies(lane + 128, width, owners)
        freq = freq - per_block
        highest = 1.0 - 2.0 * (token & 1).astype(F32)

        def across(m, value):
            if m == 0:
                value = jnp.where(lane == half, highest, value)
            mat_t[pl.ds(at, 16), pl.ds(m * 128, 128)] = value.astype(BF)

        turning(across, freq * token + offset, token * per_block, width, width // 128)
        return 0

    lax.fori_loop(0, width // 16, build, 0)
    fwd[...] = column_matrix(height, 1).astype(BF)
    inv[...] = column_matrix(height, -1).astype(BF)
    mine[...] = mat[pl.ds(pl.multiple_of(place * per_owner, per_owner), per_owner), :]
    rspec = jnp.dot(mine[...], row_filter[...], preferred_element_type=F32)
    first = lax.broadcasted_iota(jnp.int32, (half, channels), 0) == 0
    top = jnp.where(first, jnp.where(place == 0, 1.0, 0.0), 0.0)
    weight = (2.0 - top) * (1.0 / width)
    rre, rim = rspec[:half] * weight, rspec[half:] * weight
    rest = 1.0 - top
    coef[0] = rre
    coef[1] = -rim * rest
    coef[2] = rim * rest
    coef[3] = rre * rest + rim * top
    keep[0] = rest
    cspec = jnp.dot(fwd[:, pl.ds(0, height)], column_filter[...], preferred_element_type=F32)
    cspec = cspec * (1.0 / height)
    colr[...] = cspec[:height]
    coli[...] = cspec[height:]
    for b in range(2):
        for i in range(3):
            kern[pl.ds(b * 9 + i * 3, 3), :] = short_filter[b, i].astype(F32)
    parts = w_gate.shape[0] // channels
    for k in range(parts):
        at = pl.ds(pl.multiple_of((ch ^ k) * channels, channels), channels)
        to = pl.ds(k * channels, channels)
        w_all[to, pl.ds(0, channels)] = w_gate[at, :]
        w_all[to, pl.ds(channels, channels)] = w_value[at, :]


def fill_framed(framed, rows_of, channels):
    width = rows_of[0][0].shape[1]
    zeros = jnp.zeros((EDGE, channels), F32)
    for branch in range(2):
        for r in range(len(rows_of)):
            framed[branch, r, pl.ds(0, EDGE), :] = zeros
            framed[branch, r, pl.ds(EDGE + width, EDGE), :] = zeros

    def body(t, _):
        at = pl.multiple_of(t * 32, 32)
        for r, (ref, row) in enumerate(rows_of):
            for branch in range(2):
                v = ref[row, pl.ds(at, 32), pl.ds(branch * channels, channels)]
                framed[branch, r, pl.ds(EDGE + at, 32), :] = v.astype(F32)
        return 0

    lax.fori_loop(0, width // 32, body, 0)


def taps_of(kern, branch, channels):
    return [jnp.broadcast_to(kern[pl.ds(branch * 9 + k, 1), :], (8, channels)) for k in range(9)]


def projected(xs, w):
    size = 2 * xs[0].shape[1]
    total = None
    for n in range(len(xs) // 2):
        pair = jnp.concatenate([xs[2 * n][...], xs[2 * n + 1][...]], axis=1)
        part = jnp.dot(pair, w[pl.ds(n * size, size), :], preferred_element_type=F32)
        total = part if total is None else total + part
    return total.astype(BF)


def project_edge_kernel(x0, x1, x2, x3, w, first, last):
    width = first.shape[1]
    both = projected((x0, x1, x2, x3), w)
    first[0] = both[:width]
    last[0] = both[width:]


def project_mid_kernel(x0, x1, x2, x3, w, middle):
    middle[...] = projected((x0, x1, x2, x3), w).reshape(middle.shape)


def forward_kernel(up, first, middle, last, down, cot, kern, mat, send, feat, framed, cols):
    rows, width, channels = cot.shape
    owners, _, per_owner, _ = send.shape
    inner = [(middle, r) for r in range(rows - 2)]
    fill_framed(framed, [(up, 0), (first, 0), *inner, (last, 0), (down, 0)], channels)
    for branch in range(2):
        taps = taps_of(kern, branch, channels)

        def body(t, _, branch=branch, taps=taps):
            base = pl.multiple_of(t * STEP, STEP)
            done = [[] for _ in range(rows)]
            for p in range(STEP // 8):
                acc = [None] * rows
                for r in range(rows + 2):
                    for j in range(3):
                        v = framed[branch, r, pl.ds(base + 8 * p + EDGE + j - 1, 8), :]
                        for i in range(3):
                            o = r - i
                            if 0 <= o < rows:
                                term = taps[i * 3 + j] * v
                                acc[o] = term if acc[o] is None else acc[o] + term
                for o in range(rows):
                    done[o].append(acc[o])
            for o in range(rows):
                f = jnp.concatenate(done[o], axis=0).astype(BF)
                if branch == 0:
                    feat[o, pl.ds(base, STEP), :] = f
                    g = cot[o, pl.ds(base, STEP), :].astype(F32) * f.astype(F32)
                    cols[pl.ds(base, STEP), pl.ds((rows + o) * channels, channels)] = g.astype(BF)
                else:
                    cols[pl.ds(base, STEP), pl.ds(o * channels, channels)] = f
            return 0

        lax.fori_loop(0, width // STEP, body, 0)
    for n in range(rows):
        spec = jnp.dot(
            mat[...], cols[:, pl.ds(2 * n * channels, 2 * channels)], preferred_element_type=F32
        ).astype(BF)
        for e in range(2):
            send[:, 2 * n + e] = spec[:, e * channels : (e + 1) * channels].reshape(
                owners, per_owner, channels
            )


def column_kernel(
    recv, coef, keep, colr, coli, fwd, inv, mine, send, rowp, colp, stacked, spectra, er, ei
):
    owners, twice, per_owner, channels = recv.shape
    rows = twice // 2
    height = owners * rows
    half = per_owner // 2
    wide = half * channels
    group = 16 // rows

    def place(value, at, offset):
        turned = jnp.swapaxes(value, 0, 1)
        for k in range(half):
            lanes = pl.ds(k * channels + offset, channels)
            stacked[pl.ds(at, 16), lanes] = turned[k]
            stacked[pl.ds(at + height, 16), lanes] = turned[k + half]

    def unpack(n, _):
        at = pl.multiple_of(n * 16, 16)
        mixed = []
        for r in range(16):
            v = recv[n * group + r // rows, r % rows].astype(F32)
            br, bi = v[:half], v[half:]
            both = [br * coef[0] + bi * coef[1], br * coef[2] + bi * coef[3]]
            mixed.append(jnp.concatenate(both, axis=0).astype(BF))
        place(jnp.stack(mixed), at, 0)
        raw = [recv[n * group + r // rows, rows + r % rows] for r in range(16)]
        place(jnp.stack(raw), at, wide)
        return 0

    lax.fori_loop(0, height // 16, unpack, 0)
    for n in range(2 * wide // 512):
        lanes = pl.ds(n * 512, 512)
        spectra[:, lanes] = jnp.dot(fwd[...], stacked[:, lanes], preferred_element_type=F32)

    def products(n, _):
        at = pl.multiple_of(n * 16, 16)
        low, high = pl.ds(at, 16), pl.ds(at + height, 16)
        cr, ci = colr[low, :], coli[low, :]
        sr = jnp.zeros((16, channels), F32)
        si = jnp.zeros((16, channels), F32)
        for k in range(half):
            lanes = pl.ds(k * channels, channels)
            more = pl.ds(k * channels + wide, channels)
            tr, ti = spectra[low, lanes], spectra[high, lanes]
            fr, fi = spectra[low, more], spectra[high, more]
            sr = sr + (fr * tr + fi * ti)
            si = si + (fi * tr - fr * ti)
            stacked[low, lanes] = (tr * cr - ti * ci).astype(BF)
            stacked[high, lanes] = (tr * ci + ti * cr).astype(BF)
            stacked[low, more] = (fr * cr + fi * ci).astype(BF)
            stacked[high, more] = (fi * cr - fr * ci).astype(BF)
        er[low, :] = sr
        ei[low, :] = si
        return 0

    lax.fori_loop(0, height // 16, products, 0)
    for n in range(2 * wide // 512):
        lanes = pl.ds(n * 512, 512)
        spectra[:, lanes] = jnp.dot(inv[...], stacked[:, lanes], preferred_element_type=F32)

    e = jnp.concatenate([er[...], ei[...]], axis=0) * (1.0 / height)
    high = e.astype(BF)
    low = (e - high.astype(F32)).astype(BF)
    top = inv[pl.ds(0, height), :]
    colp[...] = jnp.dot(top, high, preferred_element_type=F32) + jnp.dot(
        top, low, preferred_element_type=F32
    )

    def pack(n, sums):
        p1, p2, p3 = sums
        at = pl.multiple_of(n * 16, 16)

        def taken(offset):
            slots = []
            for part in range(2):
                for k in range(half):
                    lanes = pl.ds(k * channels + offset, channels)
                    slots.append(spectra[pl.ds(at + part * height, 16), lanes])
            return jnp.stack(slots)

        mixed = jnp.swapaxes(taken(0).astype(BF), 0, 1)
        for r in range(16):
            send[n * group + r // rows, r % rows] = mixed[r]
        turned = jnp.swapaxes(taken(wide), 0, 1)
        for r in range(16):
            ar, ai = turned[r, :half], turned[r, half:]
            v = recv[n * group + r // rows, r % rows].astype(F32)
            br, bi = v[:half], v[half:]
            p1 = p1 + ar * br
            p2 = p2 + ai * bi
            p3 = p3 + (ai * br - ar * bi)
            both = [ar * coef[0] + ai * coef[2], ar * coef[1] + ai * coef[3]]
            send[n * group + r // rows, rows + r % rows] = jnp.concatenate(both, axis=0).astype(BF)
        return p1, p2, p3

    none = jnp.zeros((half, channels), F32)
    p1, p2, p3 = lax.fori_loop(0, height // 16, pack, (none, none, none))
    width = owners * per_owner
    kept = keep[0]
    twofold = (1.0 + kept) * (1.0 / width)
    qr = (p1 + kept * p2) * twofold
    qi = (kept * p3 + (1.0 - kept) * p2) * twofold
    rowp[...] = lax.dot_general(
        mine[...],
        jnp.concatenate([qr, qi], axis=0).astype(BF),
        (((0,), (0,)), ((), ())),
        preferred_element_type=F32,
    ).astype(BF)


def inverse_kernel(recv, mat, feat, cot, gated, first, middle, last):
    rows, width, channels = cot.shape
    for n in range(rows):
        spec = jnp.concatenate(
            [recv[:, 2 * n + e].reshape(width, channels) for e in range(2)], axis=1
        )
        back = jnp.dot(mat[...], spec, preferred_element_type=F32)
        for e in range(2):
            r = (2 * n + e) % rows
            value = back[:, e * channels : (e + 1) * channels]
            to, row = ((first, 0), *((middle, i) for i in range(rows - 2)), (last, 0))[r]
            if n < rows // 2:
                gated[r] = (feat[r].astype(F32) * value).astype(BF)
                to[row, :, pl.ds(0, channels)] = (cot[r].astype(F32) * value).astype(BF)
            else:
                to[row, :, pl.ds(channels, channels)] = value.astype(BF)


def spread_back(framed, kern, outs, width, channels):
    for branch in range(2):
        taps = taps_of(kern, branch, channels)

        def body(t, _, branch=branch, taps=taps):
            base = pl.multiple_of(t * STEP, STEP)
            done = [[] for _ in outs]
            for p in range(STEP // 8):
                acc = [None] * len(outs)
                needed = sorted({c + 1 - i for _, _, c in outs for i in range(3)})
                for r in needed:
                    for j in range(3):
                        v = framed[branch, r, pl.ds(base + 8 * p + EDGE + 1 - j, 8), :]
                        for n, (_, _, c) in enumerate(outs):
                            i = c + 1 - r
                            if 0 <= i < 3:
                                term = taps[i * 3 + j] * v
                                acc[n] = term if acc[n] is None else acc[n] + term
                for n in range(len(outs)):
                    done[n].append(acc[n])
            for n, (ref, row, _) in enumerate(outs):
                value = jnp.concatenate(done[n], axis=0).astype(BF)
                ref[row, pl.ds(base, STEP), pl.ds(branch * channels, channels)] = value
            return 0

        lax.fori_loop(0, width // STEP, body, 0)


def backward_mid_kernel(gfirst, gmiddle, glast, kern, back, gframed):
    width = gfirst.shape[1]
    channels = kern.shape[1]
    inner = gmiddle.shape[0]
    fill_framed(
        gframed, [(gfirst, 0), *((gmiddle, r) for r in range(inner)), (glast, 0)], channels
    )
    spread_back(gframed, kern, [(back, r, r + 1) for r in range(inner)], width, channels)


def short_kernel(up, first, middle, last, down, gfirst, gmiddle, glast, short, framed, *, branch):
    width = first.shape[1]
    channels = short.shape[1]
    inner = middle.shape[0]
    rows = inner + 2
    lanes = pl.ds(branch * channels, channels)
    tokens = [(up, 0), (first, 0), *((middle, r) for r in range(inner)), (last, 0), (down, 0)]
    grads = [(gfirst, 0), *((gmiddle, r) for r in range(inner)), (glast, 0)]
    zeros = jnp.zeros((EDGE, channels), F32)
    for r in range(rows + 2):
        framed[r, pl.ds(0, EDGE), :] = zeros
        framed[r, pl.ds(EDGE + width, EDGE), :] = zeros

    def fill(t, _):
        at = pl.multiple_of(t * 32, 32)
        for r, (ref, row) in enumerate(tokens):
            framed[r, pl.ds(EDGE + at, 32), :] = ref[row, pl.ds(at, 32), lanes].astype(F32)
        return 0

    lax.fori_loop(0, width // 32, fill, 0)

    def terms(t, sums):
        base = pl.multiple_of(t * 16, 16)
        sums = list(sums)
        both = [ref[row, pl.ds(base, 16), lanes].astype(F32) for ref, row in grads]
        for p in range(2):
            at = base + 8 * p + EDGE
            g = [v[8 * p : 8 * p + 8] for v in both]
            for r in range(rows + 2):
                for j in range(3):
                    v = framed[r, pl.ds(at + j - 1, 8), :]
                    for i in range(3):
                        o = r - i
                        if 0 <= o < rows:
                            sums[i * 3 + j] = sums[i * 3 + j] + g[o] * v
        return tuple(sums)

    sums = lax.fori_loop(
        0, width // 16, terms, tuple(jnp.zeros((8, channels), F32) for _ in range(9))
    )
    for k in range(9):
        short[pl.ds(k, 1), :] = jnp.sum(sums[k], axis=0, keepdims=True)


def backward_edge_kernel(gup, gfirst, gmiddle, glast, gdown, kern, back, gframed):
    width = gfirst.shape[1]
    channels = kern.shape[1]
    inner = gmiddle.shape[0]
    fill_framed(
        gframed,
        [(gup, 0), (gfirst, 0), (gmiddle, 0), (gmiddle, inner - 1), (glast, 0), (gdown, 0)],
        channels,
    )
    spread_back(gframed, kern, [(back, 0, 1), (back, 1, 4)], width, channels)


def share_kernel(back, w, beside, out):
    part = lax.dot_general(
        back[...], w[...], (((1,), (1,)), ((), ())), preferred_element_type=F32
    )
    out[...] = (part + beside[...].astype(F32)).astype(BF)


def finish_mid_kernel(kept, across, grad, rows, sem):
    inner = grad.shape[0] - 2
    rows[...] = (kept[...] + across[...].astype(F32)).astype(BF).reshape(rows.shape)
    copy = pltpu.make_async_copy(rows, grad.at[pl.ds(1, inner)], sem)
    copy.start()
    copy.wait()


def finish_edge_kernel(kept, across, middle, grad, rows, sems):
    width = grad.shape[1]
    copies = []
    for r in range(2):
        at = pl.ds(r * width, width)
        rows[r] = (kept[at, :] + across[at, :].astype(F32)).astype(BF)
        to = r * (grad.shape[0] - 1)
        copies.append(pltpu.make_async_copy(rows.at[r], grad.at[to], sems.at[r]))
        copies[r].start()
    for copy in copies:
        copy.wait()


def sum_kernel(parts, *outs, scale):
    total = parts[0].astype(F32)
    for n in range(1, parts.shape[0]):
        total = total + parts[n].astype(F32)
    total = total * scale
    at = 0
    for out in outs[:-1]:
        out[...] = total[at : at + out.shape[0]]
        at += out.shape[0]
    short = outs[-1]
    for b in range(2):
        for k in range(9):
            row = at + 9 * b + k
            short[k // 3, k % 3, pl.ds(b, 1), :] = total[row : row + 1]


def pack_kernel(ch, grad_w, row_part, small, out, packed, sem):
    owners, _, channels = packed.shape
    parts = 4
    size = grad_w.shape[0] // parts
    each = owners // parts
    deep = size // each
    for k in range(parts):
        at = pl.ds((ch[0] ^ k) * each, each)
        for branch in range(2):
            v = grad_w[pl.ds(k * size, size), pl.ds(branch * channels, channels)].astype(BF)
            packed[at, pl.ds(branch * deep, deep), :] = v.reshape(each, deep, channels)
    per_owner = row_part.shape[0] // owners
    packed[:, pl.ds(2 * deep, per_owner), :] = row_part[...].reshape(owners, per_owner, channels)
    packed[:, pl.ds(2 * deep + per_owner, small.shape[1]), :] = small[...]
    copy = pltpu.make_async_copy(packed, out, sem)
    copy.start()
    copy.wait()


def kernel_call(
    body, outs, scratch, limit, scalars=0, operands=0, free=False, alias=None, sems=None
):
    specs = {}
    if scalars or alias is not None:
        whole = [pl.BlockSpec(memory_space=pltpu.SMEM)] * scalars
        whole += [pl.BlockSpec(memory_space=pltpu.VMEM)] * operands
        if alias is not None:
            whole += [pl.BlockSpec(memory_space=pltpu.HBM)]
            specs["input_output_aliases"] = {alias: 0}
        specs["in_specs"] = whole
    if free:
        specs["out_specs"] = [pl.BlockSpec(memory_space=pltpu.HBM)] * len(outs)
    semaphores = [] if sems is None else [pltpu.SemaphoreType.DMA(sems)]
    return pl.pallas_call(
        body,
        out_shape=[jax.ShapeDtypeStruct(s, d) for s, d in outs],
        scratch_shapes=[pltpu.VMEM(s, d) for s, d in scratch] + semaphores,
        compiler_params=pltpu.CompilerParams(vmem_limit_bytes=limit << 20),
        **specs,
    )


def local(inputs, w_gate, w_value, short_filter, row_filter, column_filter, cotangent):
    rows, width, channels = inputs.shape
    owners = lax.axis_size("grid")
    parts = lax.axis_size("ch")
    height = column_filter.shape[0]
    per_owner = width // owners
    half = per_owner // 2
    inner = rows - 2
    scale = 1.0 / math.sqrt(height * width)
    ch = lax.axis_index("ch")
    place = lax.axis_index("grid")

    def flipped(value, bit):
        return lax.ppermute(value, "ch", [(i, i ^ bit) for i in range(parts)])

    def halos(first, last):
        up = lax.ppermute(last, "grid", [(i, i + 1) for i in range(owners - 1)])
        down = lax.ppermute(first, "grid", [(i + 1, i) for i in range(owners - 1)])
        return up, down

    edge = jnp.concatenate([inputs[0], inputs[rows - 1]], axis=0)
    mid = inputs[1 : rows - 1].reshape(inner * width, channels)
    edge_across = flipped(edge, 2)
    mid_across = flipped(mid, 2)
    edge_beside = flipped(edge, 1)
    mid_beside = flipped(mid, 1)
    edge_corner = flipped(edge_across, 1)

    (mat, mat_t, mine, fwd, inv, coef, keep, colr, coli, kern, w_all) = kernel_call(
        tables_kernel,
        [
            ((width, width), BF),
            ((width, width), BF),
            ((per_owner, width), BF),
            ((2 * height, 2 * height), BF),
            ((2 * height, 2 * height), BF),
            ((4, half, channels), F32),
            ((1, half, channels), F32),
            ((height, channels), F32),
            ((height, channels), F32),
            ((18, channels), F32),
            ((parts * channels, 2 * channels), BF),
        ],
        [],
        12,
        scalars=1,
        operands=5,
    )(jnp.stack([ch, place]), w_gate, w_value, short_filter, row_filter, column_filter)
    w_blocks = [w_all[k * channels : (k + 1) * channels] for k in range(parts)]

    line = ((1, width, 2 * channels), BF)
    lines = ((inner, width, 2 * channels), BF)
    edge_blocks = (edge, edge_beside, edge_across, edge_corner)
    first, last = kernel_call(project_edge_kernel, [line, line], [], 12)(*edge_blocks, w_all)
    up, down = halos(first, last)
    mid_corner = flipped(mid_across, 1)
    mid_blocks = (mid, mid_beside, mid_across, mid_corner)
    middle = kernel_call(project_mid_kernel, [lines], [], 12)(*mid_blocks, w_all)[0]
    middle, edge_blocks, mid_blocks = lax.optimization_barrier((middle, edge_blocks, mid_blocks))
    gathered_edge = jnp.concatenate(edge_blocks, axis=1)
    gathered_mid = jnp.concatenate(mid_blocks, axis=1)

    def framed(count):
        return ((2, count, width + 2 * EDGE, channels), F32)

    spread = ((owners, 2 * rows, per_owner, channels), BF)
    tile = ((rows, width, channels), BF)
    send, feat = kernel_call(
        forward_kernel, [spread, tile], [framed(rows + 2), ((width, 2 * rows * channels), BF)], 24
    )(up, first, middle, last, down, cotangent, kern, mat)
    recv = lax.all_to_all(send, "grid", split_axis=0, concat_axis=0, tiled=True)
    tall = (2 * height, 2 * half * channels)
    turned, row_part, colp = kernel_call(
        column_kernel,
        [spread, ((width, channels), BF), ((height, channels), F32)],
        [(tall, BF), (tall, F32), ((height, channels), F32), ((height, channels), F32)],
        20,
    )(recv, coef, keep, colr, coli, fwd, inv, mine)
    returned = lax.all_to_all(turned, "grid", split_axis=0, concat_axis=0, tiled=True)
    gated, gfirst, gmiddle, glast = kernel_call(
        inverse_kernel, [tile, line, lines, line], [], 20
    )(returned, mat_t, feat, cotangent)
    gup, gdown = halos(gfirst, glast)
    back_mid = kernel_call(backward_mid_kernel, [lines], [framed(rows)], 16)(
        gfirst, gmiddle, glast, kern
    )[0]
    shorts = [
        kernel_call(
            functools.partial(short_kernel, branch=n),
            [((9, channels), F32)],
            [((rows + 2, width + 2 * EDGE, channels), F32)],
            12,
        )(up, first, middle, last, down, gfirst, gmiddle, glast)[0]
        for n in range(2)
    ]
    back_edge = kernel_call(backward_edge_kernel, [lines], [framed(6)], 16)(
        gup, gfirst, gmiddle, glast, gdown, kern
    )[0]

    contract = (((1,), (1,)), ((), ()))
    over_tokens = (((0,), (0,)), ((), ()))

    def collected(back):
        def share(k):
            return lax.dot_general(back, w_blocks[k], contract, preferred_element_type=F32)

        beside = flipped(share(3).astype(BF), 1)
        theirs = kernel_call(share_kernel, [(beside.shape, BF)], [], 10)(
            back, w_blocks[2], beside
        )[0]
        across = flipped(theirs, 2)
        back, _ = lax.optimization_barrier((back, theirs))
        kept = share(0) + flipped(share(1).astype(BF), 1).astype(F32)
        return kept, across

    back_mid = back_mid.reshape(inner * width, 2 * channels)
    back_edge = back_edge.reshape(2 * width, 2 * channels)
    kept_mid, across_mid = collected(back_mid)
    kept_edge, across_edge = collected(back_edge)
    begun = kernel_call(
        finish_mid_kernel, [tile], [((inner, width, channels), BF)], 10,
        free=True, sems=(),
    )(kept_mid, across_mid)[0]
    input_grad = kernel_call(
        finish_edge_kernel, [tile], [((2, width, channels), BF)], 10,
        operands=2, free=True, alias=2, sems=(2,),
    )(kept_edge, across_edge, begun)[0]

    grad_w = lax.dot_general(gathered_mid, back_mid, over_tokens, preferred_element_type=F32)
    grad_w = lax.optimization_barrier(grad_w)
    grad_w = grad_w + lax.dot_general(
        gathered_edge, back_edge, over_tokens, preferred_element_type=F32
    )
    small = jnp.concatenate(
        [
            colp.astype(BF).reshape(owners, -1, channels),
            *(jnp.broadcast_to(v.astype(BF), (owners, 9, channels)) for v in shorts),
            jnp.zeros((owners, 2, channels), BF),
        ],
        axis=1,
    )
    small = lax.optimization_barrier(small)
    deep = parts * channels // owners
    packed = kernel_call(
        pack_kernel,
        [((owners, 2 * deep + per_owner + small.shape[1], channels), BF)],
        [((owners, 2 * deep + per_owner + small.shape[1], channels), BF)],
        16,
        scalars=1,
        operands=3,
        free=True,
        sems=(),
    )(ch.reshape(1), grad_w, row_part, small)[0]
    total = lax.all_to_all(packed, "grid", split_axis=0, concat_axis=0, tiled=True)
    sizes = (deep, deep, per_owner, height // owners)
    gate_grad, value_grad, row_share, col_share, short_sum = kernel_call(
        functools.partial(sum_kernel, scale=scale),
        [((size, channels), F32) for size in sizes] + [((3, 3, 2, channels), F32)],
        [],
        12,
    )(total)
    short_grad = short_sum.transpose(2, 0, 1, 3)
    return (gated, input_grad, gate_grad, value_grad, short_grad, row_share, col_share)


def solution(mesh):
    return jax.shard_map(
        local,
        mesh=mesh,
        in_specs=(
            P("grid", None, "ch"),
            P(None, "ch"),
            P(None, "ch"),
            P(None, None, None, "ch"),
            P(None, "ch"),
            P(None, "ch"),
            P("grid", None, "ch"),
        ),
        out_specs=(
            P("grid", None, "ch"),
            P("grid", None, "ch"),
            P("grid", "ch"),
            P("grid", "ch"),
            P(None, None, None, "ch"),
            P("grid", "ch"),
            P("grid", "ch"),
        ),
        check_vma=False,
    )
```

```python
import functools
import math

import jax
import jax.numpy as jnp
from jax import lax
from jax.experimental import pallas as pl
from jax.experimental.pallas import tpu as pltpu
from jax.sharding import PartitionSpec as P


BF = jnp.bfloat16
F32 = jnp.float32
EDGE = 8
STEP = 128


def cosine(phase, period):
    folded = phase & (period - 1)
    folded = jnp.minimum(folded, period - folded)
    y = (folded - period // 4).astype(F32) * (2.0 * math.pi / period)
    z = y * y
    series = 1.0 + z * (-1 / 6 + z * (1 / 120 + z * (-1 / 5040 + z * (1 / 362880 - z / 39916800))))
    return -(y * series)


def frequencies(slots, width, owners):
    per_owner = width // owners
    half = per_owner // 2
    place = slots & (per_owner - 1)
    top = slots == half
    freq = (slots // per_owner) * half + (place & (half - 1))
    freq = jnp.where(top, width // 2, freq)
    offset = jnp.where((place >= half) & ~top, width // 4, 0)
    return freq, offset


def turning(store, phase, step, period, count):
    quarter = period - period // 4
    c, s = cosine(phase, period), cosine(phase + quarter, period)
    dc, ds = cosine(step, period), cosine(step + quarter, period)
    for n in range(count):
        store(n, c)
        c, s = c * dc - s * ds, s * dc + c * ds


def column_matrix(height, sign):
    shape = (2 * height, 2 * height)
    i = lax.broadcasted_iota(jnp.int32, shape, 0)
    j = lax.broadcasted_iota(jnp.int32, shape, 1)
    turn = (jnp.where(j >= height, 1, 0) - jnp.where(i >= height, 1, 0)) * (-sign * (height // 4))
    return cosine((i & (height - 1)) * (j & (height - 1)) + turn + height, height)


def tables_kernel(
    where, w_gate, w_value, short_filter, row_filter, column_filter,
    mat, mat_t, mine, fwd, inv, coef, keep, colr, coli, kern, w_all, w_turned,
):
    ch, place = where[0], where[1]
    width, channels = row_filter.shape
    height = column_filter.shape[0]
    _, half, _ = coef.shape
    per_owner = 2 * half
    owners = width // per_owner
    shape = (16, 128)
    lane = lax.broadcasted_iota(jnp.int32, shape, 1)
    row = lax.broadcasted_iota(jnp.int32, shape, 0)

    def build(n, _):
        at = pl.multiple_of(n * 16, 16)
        freq, offset = frequencies(row + at, width, owners)

        def along(m, value):
            mat[pl.ds(at, 16), pl.ds(m * 128, 128)] = value.astype(BF)

        turning(along, freq * lane + offset, freq * 128, width, width // 128)
        token = row + at
        per_block = 128 // per_owner * half
        freq, offset = frequencies(lane + 128, width, owners)
        freq = freq - per_block
        highest = 1.0 - 2.0 * (token & 1).astype(F32)

        def across(m, value):
            if m == 0:
                value = jnp.where(lane == half, highest, value)
            mat_t[pl.ds(at, 16), pl.ds(m * 128, 128)] = value.astype(BF)

        turning(across, freq * token + offset, token * per_block, width, width // 128)
        return 0

    lax.fori_loop(0, width // 16, build, 0)
    fwd[...] = column_matrix(height, 1).astype(BF)
    inv[...] = column_matrix(height, -1).astype(BF)
    mine[...] = mat[pl.ds(pl.multiple_of(place * per_owner, per_owner), per_owner), :]
    rspec = jnp.dot(mine[...], row_filter[...], preferred_element_type=F32)
    first = lax.broadcasted_iota(jnp.int32, (half, channels), 0) == 0
    top = jnp.where(first, jnp.where(place == 0, 1.0, 0.0), 0.0)
    weight = (2.0 - top) * (1.0 / width)
    rre, rim = rspec[:half] * weight, rspec[half:] * weight
    rest = 1.0 - top
    coef[0] = rre
    coef[1] = -rim * rest
    coef[2] = rim * rest
    coef[3] = rre * rest + rim * top
    keep[0] = rest
    cspec = jnp.dot(fwd[:, pl.ds(0, height)], column_filter[...], preferred_element_type=F32)
    cspec = cspec * (1.0 / height)
    colr[...] = cspec[:height]
    coli[...] = cspec[height:]
    for b in range(2):
        for i in range(3):
            kern[pl.ds(b * 9 + i * 3, 3), :] = short_filter[b, i].astype(F32)
    parts = w_gate.shape[0] // channels
    for k in range(parts):
        at = pl.ds(pl.multiple_of((ch ^ k) * channels, channels), channels)
        to = pl.ds(k * channels, channels)
        w_all[to, pl.ds(0, channels)] = w_gate[at, :]
        w_all[to, pl.ds(channels, channels)] = w_value[at, :]
    w_turned[...] = w_all[...].astype(F32).T.astype(BF)


def fill_framed(framed, rows_of, channels):
    width = rows_of[0][0].shape[1]
    zeros = jnp.zeros((EDGE, channels), F32)
    for branch in range(2):
        for r in range(len(rows_of)):
            framed[branch, r, pl.ds(0, EDGE), :] = zeros
            framed[branch, r, pl.ds(EDGE + width, EDGE), :] = zeros

    def body(t, _):
        at = pl.multiple_of(t * 32, 32)
        for r, (ref, row) in enumerate(rows_of):
            for branch in range(2):
                v = ref[row, pl.ds(at, 32), pl.ds(branch * channels, channels)]
                framed[branch, r, pl.ds(EDGE + at, 32), :] = v.astype(F32)
        return 0

    lax.fori_loop(0, width // 32, body, 0)


def taps_of(kern, branch, channels):
    return [jnp.broadcast_to(kern[pl.ds(branch * 9 + k, 1), :], (8, channels)) for k in range(9)]


def projected(xs, w):
    size = 2 * xs[0].shape[1]
    total = None
    for n in range(len(xs) // 2):
        pair = jnp.concatenate([xs[2 * n][...], xs[2 * n + 1][...]], axis=1)
        part = jnp.dot(pair, w[pl.ds(n * size, size), :], preferred_element_type=F32)
        total = part if total is None else total + part
    return total.astype(BF)


def project_edge_kernel(x0, x1, x2, x3, w, first, last):
    width = first.shape[1]
    both = projected((x0, x1, x2, x3), w)
    first[0] = both[:width]
    last[0] = both[width:]


def project_mid_kernel(x0, x1, x2, x3, w, middle):
    middle[...] = projected((x0, x1, x2, x3), w).reshape(middle.shape)


def forward_kernel(up, first, middle, last, down, cot, kern, mat, send, feat, framed, cols):
    rows, width, channels = cot.shape
    owners, _, per_owner, _ = send.shape
    inner = [(middle, r) for r in range(rows - 2)]
    fill_framed(framed, [(up, 0), (first, 0), *inner, (last, 0), (down, 0)], channels)
    for branch in range(2):
        taps = taps_of(kern, branch, channels)

        def body(t, _, branch=branch, taps=taps):
            base = pl.multiple_of(t * STEP, STEP)
            done = [[] for _ in range(rows)]
            for p in range(STEP // 8):
                acc = [None] * rows
                for r in range(rows + 2):
                    for j in range(3):
                        v = framed[branch, r, pl.ds(base + 8 * p + EDGE + j - 1, 8), :]
                        for i in range(3):
                            o = r - i
                            if 0 <= o < rows:
                                term = taps[i * 3 + j] * v
                                acc[o] = term if acc[o] is None else acc[o] + term
                for o in range(rows):
                    done[o].append(acc[o])
            for o in range(rows):
                f = jnp.concatenate(done[o], axis=0).astype(BF)
                if branch == 0:
                    feat[o, pl.ds(base, STEP), :] = f
                    g = cot[o, pl.ds(base, STEP), :].astype(F32) * f.astype(F32)
                    cols[pl.ds(base, STEP), pl.ds((rows + o) * channels, channels)] = g.astype(BF)
                else:
                    cols[pl.ds(base, STEP), pl.ds(o * channels, channels)] = f
            return 0

        lax.fori_loop(0, width // STEP, body, 0)
    for n in range(rows):
        spec = jnp.dot(
            mat[...], cols[:, pl.ds(2 * n * channels, 2 * channels)], preferred_element_type=F32
        ).astype(BF)
        for e in range(2):
            send[:, 2 * n + e] = spec[:, e * channels : (e + 1) * channels].reshape(
                owners, per_owner, channels
            )


def column_kernel(
    recv, coef, keep, colr, coli, fwd, inv, mine, send, rowp, colp, stacked, spectra, er, ei
):
    owners, twice, per_owner, channels = recv.shape
    rows = twice // 2
    height = owners * rows
    half = per_owner // 2
    wide = half * channels
    group = 16 // rows

    def place(value, at, offset):
        turned = jnp.swapaxes(value, 0, 1)
        for k in range(half):
            lanes = pl.ds(k * channels + offset, channels)
            stacked[pl.ds(at, 16), lanes] = turned[k]
            stacked[pl.ds(at + height, 16), lanes] = turned[k + half]

    def unpack(n, _):
        at = pl.multiple_of(n * 16, 16)
        mixed = []
        for r in range(16):
            v = recv[n * group + r // rows, r % rows].astype(F32)
            br, bi = v[:half], v[half:]
            both = [br * coef[0] + bi * coef[1], br * coef[2] + bi * coef[3]]
            mixed.append(jnp.concatenate(both, axis=0).astype(BF))
        place(jnp.stack(mixed), at, 0)
        raw = [recv[n * group + r // rows, rows + r % rows] for r in range(16)]
        place(jnp.stack(raw), at, wide)
        return 0

    lax.fori_loop(0, height // 16, unpack, 0)
    for n in range(2 * wide // 512):
        lanes = pl.ds(n * 512, 512)
        spectra[:, lanes] = jnp.dot(fwd[...], stacked[:, lanes], preferred_element_type=F32)

    def products(n, _):
        at = pl.multiple_of(n * 16, 16)
        low, high = pl.ds(at, 16), pl.ds(at + height, 16)
        cr, ci = colr[low, :], coli[low, :]
        sr = jnp.zeros((16, channels), F32)
        si = jnp.zeros((16, channels), F32)
        for k in range(half):
            lanes = pl.ds(k * channels, channels)
            more = pl.ds(k * channels + wide, channels)
            tr, ti = spectra[low, lanes], spectra[high, lanes]
            fr, fi = spectra[low, more], spectra[high, more]
            sr = sr + (fr * tr + fi * ti)
            si = si + (fi * tr - fr * ti)
            stacked[low, lanes] = (tr * cr - ti * ci).astype(BF)
            stacked[high, lanes] = (tr * ci + ti * cr).astype(BF)
            stacked[low, more] = (fr * cr + fi * ci).astype(BF)
            stacked[high, more] = (fi * cr - fr * ci).astype(BF)
        er[low, :] = sr
        ei[low, :] = si
        return 0

    lax.fori_loop(0, height // 16, products, 0)
    for n in range(2 * wide // 512):
        lanes = pl.ds(n * 512, 512)
        spectra[:, lanes] = jnp.dot(inv[...], stacked[:, lanes], preferred_element_type=F32)

    e = jnp.concatenate([er[...], ei[...]], axis=0) * (1.0 / height)
    high = e.astype(BF)
    low = (e - high.astype(F32)).astype(BF)
    top = inv[pl.ds(0, height), :]
    colp[...] = jnp.dot(top, high, preferred_element_type=F32) + jnp.dot(
        top, low, preferred_element_type=F32
    )

    def pack(n, sums):
        p1, p2, p3 = sums
        at = pl.multiple_of(n * 16, 16)

        def taken(offset):
            slots = []
            for part in range(2):
                for k in range(half):
                    lanes = pl.ds(k * channels + offset, channels)
                    slots.append(spectra[pl.ds(at + part * height, 16), lanes])
            return jnp.stack(slots)

        mixed = jnp.swapaxes(taken(0).astype(BF), 0, 1)
        for r in range(16):
            send[n * group + r // rows, r % rows] = mixed[r]
        turned = jnp.swapaxes(taken(wide), 0, 1)
        for r in range(16):
            ar, ai = turned[r, :half], turned[r, half:]
            v = recv[n * group + r // rows, r % rows].astype(F32)
            br, bi = v[:half], v[half:]
            p1 = p1 + ar * br
            p2 = p2 + ai * bi
            p3 = p3 + (ai * br - ar * bi)
            both = [ar * coef[0] + ai * coef[2], ar * coef[1] + ai * coef[3]]
            send[n * group + r // rows, rows + r % rows] = jnp.concatenate(both, axis=0).astype(BF)
        return p1, p2, p3

    none = jnp.zeros((half, channels), F32)
    p1, p2, p3 = lax.fori_loop(0, height // 16, pack, (none, none, none))
    width = owners * per_owner
    kept = keep[0]
    twofold = (1.0 + kept) * (1.0 / width)
    qr = (p1 + kept * p2) * twofold
    qi = (kept * p3 + (1.0 - kept) * p2) * twofold
    rowp[...] = lax.dot_general(
        mine[...],
        jnp.concatenate([qr, qi], axis=0).astype(BF),
        (((0,), (0,)), ((), ())),
        preferred_element_type=F32,
    ).astype(BF)


def inverse_kernel(recv, mat, feat, cot, gated, first, middle, last):
    rows, width, channels = cot.shape
    for n in range(rows):
        spec = jnp.concatenate(
            [recv[:, 2 * n + e].reshape(width, channels) for e in range(2)], axis=1
        )
        back = jnp.dot(mat[...], spec, preferred_element_type=F32)
        for e in range(2):
            r = (2 * n + e) % rows
            value = back[:, e * channels : (e + 1) * channels]
            to, row = ((first, 0), *((middle, i) for i in range(rows - 2)), (last, 0))[r]
            if n < rows // 2:
                gated[r] = (feat[r].astype(F32) * value).astype(BF)
                to[row, :, pl.ds(0, channels)] = (cot[r].astype(F32) * value).astype(BF)
            else:
                to[row, :, pl.ds(channels, channels)] = value.astype(BF)


def spread_back(framed, kern, outs, width, channels):
    for branch in range(2):
        taps = taps_of(kern, branch, channels)

        def body(t, _, branch=branch, taps=taps):
            base = pl.multiple_of(t * STEP, STEP)
            done = [[] for _ in outs]
            for p in range(STEP // 8):
                acc = [None] * len(outs)
                needed = sorted({c + 1 - i for _, _, c in outs for i in range(3)})
                for r in needed:
                    for j in range(3):
                        v = framed[branch, r, pl.ds(base + 8 * p + EDGE + 1 - j, 8), :]
                        for n, (_, _, c) in enumerate(outs):
                            i = c + 1 - r
                            if 0 <= i < 3:
                                term = taps[i * 3 + j] * v
                                acc[n] = term if acc[n] is None else acc[n] + term
                for n in range(len(outs)):
                    done[n].append(acc[n])
            for n, (ref, row, _) in enumerate(outs):
                value = jnp.concatenate(done[n], axis=0).astype(BF)
                ref[row, pl.ds(base, STEP), pl.ds(branch * channels, channels)] = value
            return 0

        lax.fori_loop(0, width // STEP, body, 0)


def shares(back, w_turned, p0, p1, p2, p3):
    tokens = back.shape[0] * back.shape[1]
    channels = p0.shape[1]
    total = jnp.dot(
        back[...].reshape(tokens, back.shape[2]), w_turned[...], preferred_element_type=F32
    )
    for k, p in enumerate((p0, p1, p2, p3)):
        p[...] = total[:, k * channels : (k + 1) * channels].astype(p.dtype)


def backward_mid_kernel(gfirst, gmiddle, glast, kern, w_turned, back, p0, p1, p2, p3, gframed):
    width = gfirst.shape[1]
    channels = kern.shape[1]
    inner = gmiddle.shape[0]
    fill_framed(
        gframed, [(gfirst, 0), *((gmiddle, r) for r in range(inner)), (glast, 0)], channels
    )
    spread_back(gframed, kern, [(back, r, r + 1) for r in range(inner)], width, channels)
    shares(back, w_turned, p0, p1, p2, p3)


def short_kernel(up, first, middle, last, down, gfirst, gmiddle, glast, short, framed, *, branch):
    width = first.shape[1]
    channels = short.shape[1]
    inner = middle.shape[0]
    rows = inner + 2
    lanes = pl.ds(branch * channels, channels)
    tokens = [(up, 0), (first, 0), *((middle, r) for r in range(inner)), (last, 0), (down, 0)]
    grads = [(gfirst, 0), *((gmiddle, r) for r in range(inner)), (glast, 0)]
    zeros = jnp.zeros((EDGE, channels), F32)
    for r in range(rows + 2):
        framed[r, pl.ds(0, EDGE), :] = zeros
        framed[r, pl.ds(EDGE + width, EDGE), :] = zeros

    def fill(t, _):
        at = pl.multiple_of(t * 32, 32)
        for r, (ref, row) in enumerate(tokens):
            framed[r, pl.ds(EDGE + at, 32), :] = ref[row, pl.ds(at, 32), lanes].astype(F32)
        return 0

    lax.fori_loop(0, width // 32, fill, 0)

    def terms(t, sums):
        base = pl.multiple_of(t * 16, 16)
        sums = list(sums)
        both = [ref[row, pl.ds(base, 16), lanes].astype(F32) for ref, row in grads]
        for p in range(2):
            at = base + 8 * p + EDGE
            g = [v[8 * p : 8 * p + 8] for v in both]
            for r in range(rows + 2):
                for j in range(3):
                    v = framed[r, pl.ds(at + j - 1, 8), :]
                    for i in range(3):
                        o = r - i
                        if 0 <= o < rows:
                            sums[i * 3 + j] = sums[i * 3 + j] + g[o] * v
        return tuple(sums)

    sums = lax.fori_loop(
        0, width // 16, terms, tuple(jnp.zeros((8, channels), F32) for _ in range(9))
    )
    for k in range(9):
        short[pl.ds(k, 1), :] = jnp.sum(sums[k], axis=0, keepdims=True)


def backward_edge_kernel(
    gup, gfirst, gmiddle, glast, gdown, kern, w_turned, back, p0, p1, p2, p3, gframed
):
    width = gfirst.shape[1]
    channels = kern.shape[1]
    inner = gmiddle.shape[0]
    fill_framed(
        gframed,
        [(gup, 0), (gfirst, 0), (gmiddle, 0), (gmiddle, inner - 1), (glast, 0), (gdown, 0)],
        channels,
    )
    spread_back(gframed, kern, [(back, 0, 1), (back, 1, 4)], width, channels)
    shares(back, w_turned, p0, p1, p2, p3)


def finish_mid_kernel(own, beside, across, grad, rows, sem):
    inner = grad.shape[0] - 2
    total = own[...] + beside[...].astype(F32) + across[...].astype(F32)
    rows[...] = total.astype(BF).reshape(rows.shape)
    copy = pltpu.make_async_copy(rows, grad.at[pl.ds(1, inner)], sem)
    copy.start()
    copy.wait()


def finish_edge_kernel(own, beside, across, middle, grad, rows, sems):
    width = grad.shape[1]
    copies = []
    for r in range(2):
        at = pl.ds(r * width, width)
        total = own[at, :] + beside[at, :].astype(F32) + across[at, :].astype(F32)
        rows[r] = total.astype(BF)
        to = r * (grad.shape[0] - 1)
        copies.append(pltpu.make_async_copy(rows.at[r], grad.at[to], sems.at[r]))
        copies[r].start()
    for copy in copies:
        copy.wait()


def sum_kernel(parts, *outs, scale):
    total = parts[0].astype(F32)
    for n in range(1, parts.shape[0]):
        total = total + parts[n].astype(F32)
    total = total * scale
    at = 0
    for out in outs[:-1]:
        out[...] = total[at : at + out.shape[0]]
        at += out.shape[0]
    short = outs[-1]
    for b in range(2):
        for k in range(9):
            row = at + 9 * b + k
            short[k // 3, k % 3, pl.ds(b, 1), :] = total[row : row + 1]


def pack_kernel(ch, grad_w, row_part, small, out, packed, sem):
    owners, _, channels = packed.shape
    parts = 4
    size = grad_w.shape[0] // parts
    each = owners // parts
    deep = size // each
    for k in range(parts):
        at = pl.ds((ch[0] ^ k) * each, each)
        for branch in range(2):
            v = grad_w[pl.ds(k * size, size), pl.ds(branch * channels, channels)].astype(BF)
            packed[at, pl.ds(branch * deep, deep), :] = v.reshape(each, deep, channels)
    per_owner = row_part.shape[0] // owners
    packed[:, pl.ds(2 * deep, per_owner), :] = row_part[...].reshape(owners, per_owner, channels)
    packed[:, pl.ds(2 * deep + per_owner, small.shape[1]), :] = small[...]
    copy = pltpu.make_async_copy(packed, out, sem)
    copy.start()
    copy.wait()


def kernel_call(
    body, outs, scratch, limit, scalars=0, operands=0, free=False, alias=None, sems=None
):
    specs = {}
    if scalars or alias is not None:
        whole = [pl.BlockSpec(memory_space=pltpu.SMEM)] * scalars
        whole += [pl.BlockSpec(memory_space=pltpu.VMEM)] * operands
        if alias is not None:
            whole += [pl.BlockSpec(memory_space=pltpu.HBM)]
            specs["input_output_aliases"] = {alias: 0}
        specs["in_specs"] = whole
    if free:
        specs["out_specs"] = [pl.BlockSpec(memory_space=pltpu.HBM)] * len(outs)
    semaphores = [] if sems is None else [pltpu.SemaphoreType.DMA(sems)]
    return pl.pallas_call(
        body,
        out_shape=[(pltpu.HBM if free else jax.ShapeDtypeStruct)(s, d) for s, d in outs],
        scratch_shapes=[pltpu.VMEM(s, d) for s, d in scratch] + semaphores,
        compiler_params=pltpu.CompilerParams(vmem_limit_bytes=limit << 20),
        **specs,
    )


def local(inputs, w_gate, w_value, short_filter, row_filter, column_filter, cotangent):
    rows, width, channels = inputs.shape
    owners = lax.axis_size("grid")
    parts = lax.axis_size("ch")
    height = column_filter.shape[0]
    per_owner = width // owners
    half = per_owner // 2
    inner = rows - 2
    scale = 1.0 / math.sqrt(height * width)
    ch = lax.axis_index("ch")
    place = lax.axis_index("grid")

    def flipped(value, bit):
        return lax.ppermute(value, "ch", [(i, i ^ bit) for i in range(parts)])

    def halos(first, last):
        up = lax.ppermute(last, "grid", [(i, i + 1) for i in range(owners - 1)])
        down = lax.ppermute(first, "grid", [(i + 1, i) for i in range(owners - 1)])
        return up, down

    edge = jnp.concatenate([inputs[0], inputs[rows - 1]], axis=0)
    mid = inputs[1 : rows - 1].reshape(inner * width, channels)
    edge_across = flipped(edge, 2)
    mid_across = flipped(mid, 2)
    edge_beside = flipped(edge, 1)
    mid_beside = flipped(mid, 1)
    edge_corner = flipped(edge_across, 1)

    (mat, mat_t, mine, fwd, inv, coef, keep, colr, coli, kern, w_all, w_turned) = kernel_call(
        tables_kernel,
        [
            ((width, width), BF),
            ((width, width), BF),
            ((per_owner, width), BF),
            ((2 * height, 2 * height), BF),
            ((2 * height, 2 * height), BF),
            ((4, half, channels), F32),
            ((1, half, channels), F32),
            ((height, channels), F32),
            ((height, channels), F32),
            ((18, channels), F32),
            ((parts * channels, 2 * channels), BF),
            ((2 * channels, parts * channels), BF),
        ],
        [],
        12,
        scalars=1,
        operands=5,
    )(jnp.stack([ch, place]), w_gate, w_value, short_filter, row_filter, column_filter)

    line = ((1, width, 2 * channels), BF)
    lines = ((inner, width, 2 * channels), BF)
    edge_blocks = (edge, edge_beside, edge_across, edge_corner)
    first, last = kernel_call(project_edge_kernel, [line, line], [], 12)(*edge_blocks, w_all)
    up, down = halos(first, last)
    mid_corner = flipped(mid_across, 1)
    mid_blocks = (mid, mid_beside, mid_across, mid_corner)
    middle = kernel_call(project_mid_kernel, [lines], [], 12)(*mid_blocks, w_all)[0]
    middle, edge_blocks, mid_blocks = lax.optimization_barrier((middle, edge_blocks, mid_blocks))
    gathered_edge = jnp.concatenate(edge_blocks, axis=1)
    gathered_mid = jnp.concatenate(mid_blocks, axis=1)

    def framed(count):
        return ((2, count, width + 2 * EDGE, channels), F32)

    spread = ((owners, 2 * rows, per_owner, channels), BF)
    tile = ((rows, width, channels), BF)
    send, feat = kernel_call(
        forward_kernel, [spread, tile], [framed(rows + 2), ((width, 2 * rows * channels), BF)], 24
    )(up, first, middle, last, down, cotangent, kern, mat)
    recv = lax.all_to_all(send, "grid", split_axis=0, concat_axis=0, tiled=True)
    tall = (2 * height, 2 * half * channels)
    turned, row_part, colp = kernel_call(
        column_kernel,
        [spread, ((width, channels), BF), ((height, channels), F32)],
        [(tall, BF), (tall, F32), ((height, channels), F32), ((height, channels), F32)],
        20,
    )(recv, coef, keep, colr, coli, fwd, inv, mine)
    returned = lax.all_to_all(turned, "grid", split_axis=0, concat_axis=0, tiled=True)
    gated, gfirst, gmiddle, glast = kernel_call(
        inverse_kernel, [tile, line, lines, line], [], 20
    )(returned, mat_t, feat, cotangent)
    gup, gdown = halos(gfirst, glast)
    share = (2 * width, channels)
    share_outs = [(share, F32), (share, BF), (share, F32), (share, BF)]
    back_mid, *shares_mid = kernel_call(
        backward_mid_kernel, [lines, *share_outs], [framed(rows)], 20
    )(gfirst, gmiddle, glast, kern, w_turned)
    shorts = [
        kernel_call(
            functools.partial(short_kernel, branch=n),
            [((9, channels), F32)],
            [((rows + 2, width + 2 * EDGE, channels), F32)],
            12,
        )(up, first, middle, last, down, gfirst, gmiddle, glast)[0]
        for n in range(2)
    ]
    back_edge, *shares_edge = kernel_call(
        backward_edge_kernel, [lines, *share_outs], [framed(6)], 22
    )(gup, gfirst, gmiddle, glast, gdown, kern, w_turned)

    over_tokens = (((0,), (0,)), ((), ()))

    def collected(p0, p1, p2, p3):
        beside = flipped(p3, 1)
        theirs = (p2 + beside.astype(F32)).astype(BF)
        across = flipped(theirs, 2)
        kept = flipped(p1, 1)
        return p0, kept, across

    back_mid = back_mid.reshape(inner * width, 2 * channels)
    back_edge = back_edge.reshape(2 * width, 2 * channels)
    mid_parts = collected(*shares_mid)
    edge_parts = collected(*shares_edge)
    begun = kernel_call(
        finish_mid_kernel, [tile], [((inner, width, channels), BF)], 10,
        free=True, sems=(),
    )(*mid_parts)[0]
    input_grad = kernel_call(
        finish_edge_kernel, [tile], [((2, width, channels), BF)], 10,
        operands=3, free=True, alias=3, sems=(2,),
    )(*edge_parts, begun)[0]

    grad_w = lax.dot_general(gathered_mid, back_mid, over_tokens, preferred_element_type=F32)
    grad_w = lax.optimization_barrier(grad_w)
    grad_w = grad_w + lax.dot_general(
        gathered_edge, back_edge, over_tokens, preferred_element_type=F32
    )
    small = jnp.concatenate(
        [
            colp.astype(BF).reshape(owners, -1, channels),
            *(jnp.broadcast_to(v.astype(BF), (owners, 9, channels)) for v in shorts),
            jnp.zeros((owners, 2, channels), BF),
        ],
        axis=1,
    )
    small = lax.optimization_barrier(small)
    deep = parts * channels // owners
    packed = kernel_call(
        pack_kernel,
        [((owners, 2 * deep + per_owner + small.shape[1], channels), BF)],
        [((owners, 2 * deep + per_owner + small.shape[1], channels), BF)],
        16,
        scalars=1,
        operands=3,
        free=True,
        sems=(),
    )(ch.reshape(1), grad_w, row_part, small)[0]
    total = lax.all_to_all(packed, "grid", split_axis=0, concat_axis=0, tiled=True)
    sizes = (deep, deep, per_owner, height // owners)
    gate_grad, value_grad, row_share, col_share, short_sum = kernel_call(
        functools.partial(sum_kernel, scale=scale),
        [((size, channels), F32) for size in sizes] + [((3, 3, 2, channels), F32)],
        [],
        12,
    )(total)
    short_grad = short_sum.transpose(2, 0, 1, 3)
    return (gated, input_grad, gate_grad, value_grad, short_grad, row_share, col_share)


def solution(mesh):
    return jax.shard_map(
        local,
        mesh=mesh,
        in_specs=(
            P("grid", None, "ch"),
            P(None, "ch"),
            P(None, "ch"),
            P(None, None, None, "ch"),
            P(None, "ch"),
            P(None, "ch"),
            P("grid", None, "ch"),
        ),
        out_specs=(
            P("grid", None, "ch"),
            P("grid", None, "ch"),
            P("grid", "ch"),
            P("grid", "ch"),
            P(None, None, None, "ch"),
            P("grid", "ch"),
            P("grid", "ch"),
        ),
        check_vma=False,
    )
```

```python
import functools
import math

import jax
import jax.numpy as jnp
from jax import lax
from jax.experimental import pallas as pl
from jax.experimental.pallas import tpu as pltpu
from jax.sharding import PartitionSpec as P


BF = jnp.bfloat16
F32 = jnp.float32
EDGE = 8
STEP = 128


def cosine(phase, period):
    folded = phase & (period - 1)
    folded = jnp.minimum(folded, period - folded)
    y = (folded - period // 4).astype(F32) * (2.0 * math.pi / period)
    z = y * y
    series = 1.0 + z * (-1 / 6 + z * (1 / 120 + z * (-1 / 5040 + z * (1 / 362880 - z / 39916800))))
    return -(y * series)


def frequencies(slots, width, owners):
    per_owner = width // owners
    half = per_owner // 2
    place = slots & (per_owner - 1)
    top = slots == half
    freq = (slots // per_owner) * half + (place & (half - 1))
    freq = jnp.where(top, width // 2, freq)
    offset = jnp.where((place >= half) & ~top, width // 4, 0)
    return freq, offset


def turning(store, phase, step, period, count):
    quarter = period - period // 4
    c, s = cosine(phase, period), cosine(phase + quarter, period)
    dc, ds = cosine(step, period), cosine(step + quarter, period)
    for n in range(count):
        store(n, c)
        c, s = c * dc - s * ds, s * dc + c * ds


def column_matrix(height, sign):
    shape = (2 * height, 2 * height)
    i = lax.broadcasted_iota(jnp.int32, shape, 0)
    j = lax.broadcasted_iota(jnp.int32, shape, 1)
    turn = (jnp.where(j >= height, 1, 0) - jnp.where(i >= height, 1, 0)) * (-sign * (height // 4))
    return cosine((i & (height - 1)) * (j & (height - 1)) + turn + height, height)


def tables_kernel(
    where, w_gate, w_value, short_filter, row_filter, column_filter,
    mat, mat_t, mine, fwd, inv, coef, keep, colr, coli, kern, w_all, w_turned,
):
    ch, place = where[0], where[1]
    width, channels = row_filter.shape
    height = column_filter.shape[0]
    _, half, _ = coef.shape
    per_owner = 2 * half
    owners = width // per_owner
    shape = (16, 128)
    lane = lax.broadcasted_iota(jnp.int32, shape, 1)
    row = lax.broadcasted_iota(jnp.int32, shape, 0)

    def build(n, _):
        at = pl.multiple_of(n * 16, 16)
        freq, offset = frequencies(row + at, width, owners)

        def along(m, value):
            mat[pl.ds(at, 16), pl.ds(m * 128, 128)] = value.astype(BF)

        turning(along, freq * lane + offset, freq * 128, width, width // 128)
        token = row + at
        per_block = 128 // per_owner * half
        freq, offset = frequencies(lane + 128, width, owners)
        freq = freq - per_block
        highest = 1.0 - 2.0 * (token & 1).astype(F32)

        def across(m, value):
            if m == 0:
                value = jnp.where(lane == half, highest, value)
            mat_t[pl.ds(at, 16), pl.ds(m * 128, 128)] = value.astype(BF)

        turning(across, freq * token + offset, token * per_block, width, width // 128)
        return 0

    lax.fori_loop(0, width // 16, build, 0)
    fwd[...] = column_matrix(height, 1).astype(BF)
    inv[...] = column_matrix(height, -1).astype(BF)
    mine[...] = mat[pl.ds(pl.multiple_of(place * per_owner, per_owner), per_owner), :]
    rspec = jnp.dot(mine[...], row_filter[...], preferred_element_type=F32)
    first = lax.broadcasted_iota(jnp.int32, (half, channels), 0) == 0
    top = jnp.where(first, jnp.where(place == 0, 1.0, 0.0), 0.0)
    weight = (2.0 - top) * (1.0 / width)
    rre, rim = rspec[:half] * weight, rspec[half:] * weight
    rest = 1.0 - top
    coef[0] = rre
    coef[1] = -rim * rest
    coef[2] = rim * rest
    coef[3] = rre * rest + rim * top
    keep[0] = rest
    cspec = jnp.dot(fwd[:, pl.ds(0, height)], column_filter[...], preferred_element_type=F32)
    cspec = cspec * (1.0 / height)
    colr[...] = cspec[:height]
    coli[...] = cspec[height:]
    for b in range(2):
        for i in range(3):
            kern[pl.ds(b * 9 + i * 3, 3), :] = short_filter[b, i].astype(F32)
    parts = w_gate.shape[0] // channels
    for k in range(parts):
        at = pl.ds(pl.multiple_of((ch ^ k) * channels, channels), channels)
        to = pl.ds(k * channels, channels)
        w_all[to, pl.ds(0, channels)] = w_gate[at, :]
        w_all[to, pl.ds(channels, channels)] = w_value[at, :]
    w_turned[...] = w_all[...].astype(F32).T.astype(BF)


def fill_framed(framed, rows_of, channels):
    width = rows_of[0][0].shape[1]
    zeros = jnp.zeros((EDGE, channels), F32)
    for branch in range(2):
        for r in range(len(rows_of)):
            framed[branch, r, pl.ds(0, EDGE), :] = zeros
            framed[branch, r, pl.ds(EDGE + width, EDGE), :] = zeros

    def body(t, _):
        at = pl.multiple_of(t * 32, 32)
        for r, (ref, row) in enumerate(rows_of):
            for branch in range(2):
                v = ref[row, pl.ds(at, 32), pl.ds(branch * channels, channels)]
                framed[branch, r, pl.ds(EDGE + at, 32), :] = v.astype(F32)
        return 0

    lax.fori_loop(0, width // 32, body, 0)


def taps_of(kern, branch, channels):
    return [jnp.broadcast_to(kern[pl.ds(branch * 9 + k, 1), :], (8, channels)) for k in range(9)]


def projected(xs, w):
    size = 2 * xs[0].shape[1]
    total = None
    for n in range(len(xs) // 2):
        pair = jnp.concatenate([xs[2 * n][...], xs[2 * n + 1][...]], axis=1)
        part = jnp.dot(pair, w[pl.ds(n * size, size), :], preferred_element_type=F32)
        total = part if total is None else total + part
    return total.astype(BF)


def project_edge_kernel(x0, x1, x2, x3, w, first, last):
    width = first.shape[1]
    both = projected((x0, x1, x2, x3), w)
    first[0] = both[:width]
    last[0] = both[width:]


def project_mid_kernel(x0, x1, x2, x3, w, middle):
    middle[...] = projected((x0, x1, x2, x3), w).reshape(middle.shape)


def forward_kernel(up, first, middle, last, down, cot, kern, mat, send, feat, framed, cols):
    rows, width, channels = cot.shape
    owners, _, per_owner, _ = send.shape
    inner = [(middle, r) for r in range(rows - 2)]
    fill_framed(framed, [(up, 0), (first, 0), *inner, (last, 0), (down, 0)], channels)
    for branch in range(2):
        taps = taps_of(kern, branch, channels)

        def body(t, _, branch=branch, taps=taps):
            base = pl.multiple_of(t * STEP, STEP)
            done = [[] for _ in range(rows)]
            for p in range(STEP // 8):
                acc = [None] * rows
                for r in range(rows + 2):
                    for j in range(3):
                        v = framed[branch, r, pl.ds(base + 8 * p + EDGE + j - 1, 8), :]
                        for i in range(3):
                            o = r - i
                            if 0 <= o < rows:
                                term = taps[i * 3 + j] * v
                                acc[o] = term if acc[o] is None else acc[o] + term
                for o in range(rows):
                    done[o].append(acc[o])
            for o in range(rows):
                f = jnp.concatenate(done[o], axis=0).astype(BF)
                if branch == 0:
                    feat[o, pl.ds(base, STEP), :] = f
                    g = cot[o, pl.ds(base, STEP), :].astype(F32) * f.astype(F32)
                    cols[pl.ds(base, STEP), pl.ds((rows + o) * channels, channels)] = g.astype(BF)
                else:
                    cols[pl.ds(base, STEP), pl.ds(o * channels, channels)] = f
            return 0

        lax.fori_loop(0, width // STEP, body, 0)
    for n in range(rows):
        spec = jnp.dot(
            mat[...], cols[:, pl.ds(2 * n * channels, 2 * channels)], preferred_element_type=F32
        ).astype(BF)
        for e in range(2):
            send[:, 2 * n + e] = spec[:, e * channels : (e + 1) * channels].reshape(
                owners, per_owner, channels
            )


def column_kernel(
    recv, coef, keep, colr, coli, fwd, inv, mine, send, rowp, colp, stacked, spectra, er, ei
):
    owners, twice, per_owner, channels = recv.shape
    rows = twice // 2
    height = owners * rows
    half = per_owner // 2
    wide = half * channels
    group = 16 // rows

    def place(value, at, offset):
        turned = jnp.swapaxes(value, 0, 1)
        for k in range(half):
            lanes = pl.ds(k * channels + offset, channels)
            stacked[pl.ds(at, 16), lanes] = turned[k]
            stacked[pl.ds(at + height, 16), lanes] = turned[k + half]

    def unpack(n, _):
        at = pl.multiple_of(n * 16, 16)
        mixed = []
        for r in range(16):
            v = recv[n * group + r // rows, r % rows].astype(F32)
            br, bi = v[:half], v[half:]
            both = [br * coef[0] + bi * coef[1], br * coef[2] + bi * coef[3]]
            mixed.append(jnp.concatenate(both, axis=0).astype(BF))
        place(jnp.stack(mixed), at, 0)
        raw = [recv[n * group + r // rows, rows + r % rows] for r in range(16)]
        place(jnp.stack(raw), at, wide)
        return 0

    lax.fori_loop(0, height // 16, unpack, 0)
    several = 4

    def transform(matrix, n):
        for offset in (0, wide):
            lanes = pl.ds(n * several * channels + offset, several * channels)
            spectra[:, lanes] = jnp.dot(matrix[...], stacked[:, lanes], preferred_element_type=F32)

    def products(n):
        for at in range(0, height, 16):
            low, high = pl.ds(at, 16), pl.ds(at + height, 16)
            cr, ci = colr[low, :], coli[low, :]
            sr = si = None
            for k in range(n * several, (n + 1) * several):
                lanes = pl.ds(k * channels, channels)
                more = pl.ds(k * channels + wide, channels)
                tr, ti = spectra[low, lanes], spectra[high, lanes]
                fr, fi = spectra[low, more], spectra[high, more]
                pr, pi = fr * tr + fi * ti, fi * tr - fr * ti
                sr = pr if sr is None else sr + pr
                si = pi if si is None else si + pi
                stacked[low, lanes] = (tr * cr - ti * ci).astype(BF)
                stacked[high, lanes] = (tr * ci + ti * cr).astype(BF)
                stacked[low, more] = (fr * cr + fi * ci).astype(BF)
                stacked[high, more] = (fi * cr - fr * ci).astype(BF)
            er[low, :] = sr if n == 0 else er[low, :] + sr
            ei[low, :] = si if n == 0 else ei[low, :] + si

    steps = half // several
    transform(fwd, 0)
    for n in range(steps):
        if n + 1 < steps:
            transform(fwd, n + 1)
        products(n)
        transform(inv, n)

    e = jnp.concatenate([er[...], ei[...]], axis=0) * (1.0 / height)
    high = e.astype(BF)
    low = (e - high.astype(F32)).astype(BF)
    top = inv[pl.ds(0, height), :]
    colp[...] = jnp.dot(top, high, preferred_element_type=F32) + jnp.dot(
        top, low, preferred_element_type=F32
    )

    def pack(n, sums):
        p1, p2, p3 = sums
        at = pl.multiple_of(n * 16, 16)

        def taken(offset):
            slots = []
            for part in range(2):
                for k in range(half):
                    lanes = pl.ds(k * channels + offset, channels)
                    slots.append(spectra[pl.ds(at + part * height, 16), lanes])
            return jnp.stack(slots)

        mixed = jnp.swapaxes(taken(0).astype(BF), 0, 1)
        for r in range(16):
            send[n * group + r // rows, r % rows] = mixed[r]
        turned = jnp.swapaxes(taken(wide), 0, 1)
        for r in range(16):
            ar, ai = turned[r, :half], turned[r, half:]
            v = recv[n * group + r // rows, r % rows].astype(F32)
            br, bi = v[:half], v[half:]
            p1 = p1 + ar * br
            p2 = p2 + ai * bi
            p3 = p3 + (ai * br - ar * bi)
            both = [ar * coef[0] + ai * coef[2], ar * coef[1] + ai * coef[3]]
            send[n * group + r // rows, rows + r % rows] = jnp.concatenate(both, axis=0).astype(BF)
        return p1, p2, p3

    none = jnp.zeros((half, channels), F32)
    p1, p2, p3 = lax.fori_loop(0, height // 16, pack, (none, none, none))
    width = owners * per_owner
    kept = keep[0]
    twofold = (1.0 + kept) * (1.0 / width)
    qr = (p1 + kept * p2) * twofold
    qi = (kept * p3 + (1.0 - kept) * p2) * twofold
    rowp[...] = lax.dot_general(
        mine[...],
        jnp.concatenate([qr, qi], axis=0).astype(BF),
        (((0,), (0,)), ((), ())),
        preferred_element_type=F32,
    ).astype(BF)


def inverse_kernel(recv, mat, feat, cot, gated, first, middle, last):
    rows, width, channels = cot.shape
    for n in range(rows):
        spec = jnp.concatenate(
            [recv[:, 2 * n + e].reshape(width, channels) for e in range(2)], axis=1
        )
        back = jnp.dot(mat[...], spec, preferred_element_type=F32)
        for e in range(2):
            r = (2 * n + e) % rows
            value = back[:, e * channels : (e + 1) * channels]
            to, row = ((first, 0), *((middle, i) for i in range(rows - 2)), (last, 0))[r]
            if n < rows // 2:
                gated[r] = (feat[r].astype(F32) * value).astype(BF)
                to[row, :, pl.ds(0, channels)] = (cot[r].astype(F32) * value).astype(BF)
            else:
                to[row, :, pl.ds(channels, channels)] = value.astype(BF)


def spread_back(framed, kern, outs, width, channels):
    for branch in range(2):
        taps = taps_of(kern, branch, channels)

        def body(t, _, branch=branch, taps=taps):
            base = pl.multiple_of(t * STEP, STEP)
            done = [[] for _ in outs]
            for p in range(STEP // 8):
                acc = [None] * len(outs)
                needed = sorted({c + 1 - i for _, _, c in outs for i in range(3)})
                for r in needed:
                    for j in range(3):
                        v = framed[branch, r, pl.ds(base + 8 * p + EDGE + 1 - j, 8), :]
                        for n, (_, _, c) in enumerate(outs):
                            i = c + 1 - r
                            if 0 <= i < 3:
                                term = taps[i * 3 + j] * v
                                acc[n] = term if acc[n] is None else acc[n] + term
                for n in range(len(outs)):
                    done[n].append(acc[n])
            for n, (ref, row, _) in enumerate(outs):
                value = jnp.concatenate(done[n], axis=0).astype(BF)
                ref[row, pl.ds(base, STEP), pl.ds(branch * channels, channels)] = value
            return 0

        lax.fori_loop(0, width // STEP, body, 0)


def shares(back, w_turned, p0, p1, p2, p3):
    tokens = back.shape[0] * back.shape[1]
    channels = p0.shape[1]
    total = jnp.dot(
        back[...].reshape(tokens, back.shape[2]), w_turned[...], preferred_element_type=F32
    )
    for k, p in enumerate((p0, p1, p2, p3)):
        p[...] = total[:, k * channels : (k + 1) * channels].astype(p.dtype)


def backward_mid_kernel(gfirst, gmiddle, glast, kern, w_turned, back, p0, p1, p2, p3, gframed):
    width = gfirst.shape[1]
    channels = kern.shape[1]
    inner = gmiddle.shape[0]
    fill_framed(
        gframed, [(gfirst, 0), *((gmiddle, r) for r in range(inner)), (glast, 0)], channels
    )
    spread_back(gframed, kern, [(back, r, r + 1) for r in range(inner)], width, channels)
    shares(back, w_turned, p0, p1, p2, p3)


def short_kernel(up, first, middle, last, down, gfirst, gmiddle, glast, short, framed, *, branch):
    width = first.shape[1]
    channels = short.shape[1]
    inner = middle.shape[0]
    rows = inner + 2
    lanes = pl.ds(branch * channels, channels)
    tokens = [(up, 0), (first, 0), *((middle, r) for r in range(inner)), (last, 0), (down, 0)]
    grads = [(gfirst, 0), *((gmiddle, r) for r in range(inner)), (glast, 0)]
    zeros = jnp.zeros((EDGE, channels), F32)
    for r in range(rows + 2):
        framed[r, pl.ds(0, EDGE), :] = zeros
        framed[r, pl.ds(EDGE + width, EDGE), :] = zeros

    def fill(t, _):
        at = pl.multiple_of(t * 32, 32)
        for r, (ref, row) in enumerate(tokens):
            framed[r, pl.ds(EDGE + at, 32), :] = ref[row, pl.ds(at, 32), lanes].astype(F32)
        return 0

    lax.fori_loop(0, width // 32, fill, 0)

    def terms(t, sums):
        base = pl.multiple_of(t * 16, 16)
        sums = list(sums)
        both = [ref[row, pl.ds(base, 16), lanes].astype(F32) for ref, row in grads]
        for p in range(2):
            at = base + 8 * p + EDGE
            g = [v[8 * p : 8 * p + 8] for v in both]
            for r in range(rows + 2):
                for j in range(3):
                    v = framed[r, pl.ds(at + j - 1, 8), :]
                    for i in range(3):
                        o = r - i
                        if 0 <= o < rows:
                            sums[i * 3 + j] = sums[i * 3 + j] + g[o] * v
        return tuple(sums)

    sums = lax.fori_loop(
        0, width // 16, terms, tuple(jnp.zeros((8, channels), F32) for _ in range(9))
    )
    for k in range(9):
        short[pl.ds(k, 1), :] = jnp.sum(sums[k], axis=0, keepdims=True)


def backward_edge_kernel(
    gup, gfirst, gmiddle, glast, gdown, kern, w_turned, back, p0, p1, p2, p3, gframed
):
    width = gfirst.shape[1]
    channels = kern.shape[1]
    inner = gmiddle.shape[0]
    fill_framed(
        gframed,
        [(gup, 0), (gfirst, 0), (gmiddle, 0), (gmiddle, inner - 1), (glast, 0), (gdown, 0)],
        channels,
    )
    spread_back(gframed, kern, [(back, 0, 1), (back, 1, 4)], width, channels)
    shares(back, w_turned, p0, p1, p2, p3)


def finish_mid_kernel(own, beside, across, grad, rows, sem):
    inner = grad.shape[0] - 2
    total = own[...] + beside[...].astype(F32) + across[...].astype(F32)
    rows[...] = total.astype(BF).reshape(rows.shape)
    copy = pltpu.make_async_copy(rows, grad.at[pl.ds(1, inner)], sem)
    copy.start()
    copy.wait()


def finish_edge_kernel(own, beside, across, middle, grad, rows, sems):
    width = grad.shape[1]
    copies = []
    for r in range(2):
        at = pl.ds(r * width, width)
        total = own[at, :] + beside[at, :].astype(F32) + across[at, :].astype(F32)
        rows[r] = total.astype(BF)
        to = r * (grad.shape[0] - 1)
        copies.append(pltpu.make_async_copy(rows.at[r], grad.at[to], sems.at[r]))
        copies[r].start()
    for copy in copies:
        copy.wait()


def sum_kernel(parts, *outs, scale):
    total = parts[0].astype(F32)
    for n in range(1, parts.shape[0]):
        total = total + parts[n].astype(F32)
    total = total * scale
    at = 0
    for out in outs[:-1]:
        out[...] = total[at : at + out.shape[0]]
        at += out.shape[0]
    short = outs[-1]
    for b in range(2):
        for k in range(9):
            row = at + 9 * b + k
            short[k // 3, k % 3, pl.ds(b, 1), :] = total[row : row + 1]


def pack_kernel(ch, grad_w, row_part, small, out, packed, sem):
    owners, _, channels = packed.shape
    parts = 4
    size = grad_w.shape[0] // parts
    each = owners // parts
    deep = size // each
    for k in range(parts):
        at = pl.ds((ch[0] ^ k) * each, each)
        for branch in range(2):
            v = grad_w[pl.ds(k * size, size), pl.ds(branch * channels, channels)].astype(BF)
            packed[at, pl.ds(branch * deep, deep), :] = v.reshape(each, deep, channels)
    per_owner = row_part.shape[0] // owners
    packed[:, pl.ds(2 * deep, per_owner), :] = row_part[...].reshape(owners, per_owner, channels)
    packed[:, pl.ds(2 * deep + per_owner, small.shape[1]), :] = small[...]
    copy = pltpu.make_async_copy(packed, out, sem)
    copy.start()
    copy.wait()


def kernel_call(
    body, outs, scratch, limit, scalars=0, operands=0, free=False, alias=None, sems=None
):
    specs = {}
    if scalars or alias is not None:
        whole = [pl.BlockSpec(memory_space=pltpu.SMEM)] * scalars
        whole += [pl.BlockSpec(memory_space=pltpu.VMEM)] * operands
        if alias is not None:
            whole += [pl.BlockSpec(memory_space=pltpu.HBM)]
            specs["input_output_aliases"] = {alias: 0}
        specs["in_specs"] = whole
    if free:
        specs["out_specs"] = [pl.BlockSpec(memory_space=pltpu.HBM)] * len(outs)
    semaphores = [] if sems is None else [pltpu.SemaphoreType.DMA(sems)]
    return pl.pallas_call(
        body,
        out_shape=[(pltpu.HBM if free else jax.ShapeDtypeStruct)(s, d) for s, d in outs],
        scratch_shapes=[pltpu.VMEM(s, d) for s, d in scratch] + semaphores,
        compiler_params=pltpu.CompilerParams(vmem_limit_bytes=limit << 20),
        **specs,
    )


def local(inputs, w_gate, w_value, short_filter, row_filter, column_filter, cotangent):
    rows, width, channels = inputs.shape
    owners = lax.axis_size("grid")
    parts = lax.axis_size("ch")
    height = column_filter.shape[0]
    per_owner = width // owners
    half = per_owner // 2
    inner = rows - 2
    scale = 1.0 / math.sqrt(height * width)
    ch = lax.axis_index("ch")
    place = lax.axis_index("grid")

    def flipped(value, bit):
        return lax.ppermute(value, "ch", [(i, i ^ bit) for i in range(parts)])

    def halos(first, last):
        up = lax.ppermute(last, "grid", [(i, i + 1) for i in range(owners - 1)])
        down = lax.ppermute(first, "grid", [(i + 1, i) for i in range(owners - 1)])
        return up, down

    edge = jnp.concatenate([inputs[0], inputs[rows - 1]], axis=0)
    mid = inputs[1 : rows - 1].reshape(inner * width, channels)
    edge_across = flipped(edge, 2)
    mid_across = flipped(mid, 2)
    edge_beside = flipped(edge, 1)
    mid_beside = flipped(mid, 1)
    edge_corner = flipped(edge_across, 1)

    (mat, mat_t, mine, fwd, inv, coef, keep, colr, coli, kern, w_all, w_turned) = kernel_call(
        tables_kernel,
        [
            ((width, width), BF),
            ((width, width), BF),
            ((per_owner, width), BF),
            ((2 * height, 2 * height), BF),
            ((2 * height, 2 * height), BF),
            ((4, half, channels), F32),
            ((1, half, channels), F32),
            ((height, channels), F32),
            ((height, channels), F32),
            ((18, channels), F32),
            ((parts * channels, 2 * channels), BF),
            ((2 * channels, parts * channels), BF),
        ],
        [],
        12,
        scalars=1,
        operands=5,
    )(jnp.stack([ch, place]), w_gate, w_value, short_filter, row_filter, column_filter)

    line = ((1, width, 2 * channels), BF)
    lines = ((inner, width, 2 * channels), BF)
    edge_blocks = (edge, edge_beside, edge_across, edge_corner)
    first, last = kernel_call(project_edge_kernel, [line, line], [], 12)(*edge_blocks, w_all)
    up, down = halos(first, last)
    mid_corner = flipped(mid_across, 1)
    mid_blocks = (mid, mid_beside, mid_across, mid_corner)
    middle = kernel_call(project_mid_kernel, [lines], [], 12)(*mid_blocks, w_all)[0]
    middle, edge_blocks, mid_blocks = lax.optimization_barrier((middle, edge_blocks, mid_blocks))
    gathered_edge = jnp.concatenate(edge_blocks, axis=1)
    gathered_mid = jnp.concatenate(mid_blocks, axis=1)

    def framed(count):
        return ((2, count, width + 2 * EDGE, channels), F32)

    spread = ((owners, 2 * rows, per_owner, channels), BF)
    tile = ((rows, width, channels), BF)
    send, feat = kernel_call(
        forward_kernel, [spread, tile], [framed(rows + 2), ((width, 2 * rows * channels), BF)], 24
    )(up, first, middle, last, down, cotangent, kern, mat)
    recv = lax.all_to_all(send, "grid", split_axis=0, concat_axis=0, tiled=True)
    tall = (2 * height, 2 * half * channels)
    turned, row_part, colp = kernel_call(
        column_kernel,
        [spread, ((width, channels), BF), ((height, channels), F32)],
        [(tall, BF), (tall, F32), ((height, channels), F32), ((height, channels), F32)],
        20,
    )(recv, coef, keep, colr, coli, fwd, inv, mine)
    returned = lax.all_to_all(turned, "grid", split_axis=0, concat_axis=0, tiled=True)
    gated, gfirst, gmiddle, glast = kernel_call(
        inverse_kernel, [tile, line, lines, line], [], 20
    )(returned, mat_t, feat, cotangent)
    gup, gdown = halos(gfirst, glast)
    share = (2 * width, channels)
    share_outs = [(share, F32), (share, BF), (share, F32), (share, BF)]
    back_mid, *shares_mid = kernel_call(
        backward_mid_kernel, [lines, *share_outs], [framed(rows)], 20
    )(gfirst, gmiddle, glast, kern, w_turned)
    shorts = [
        kernel_call(
            functools.partial(short_kernel, branch=n),
            [((9, channels), F32)],
            [((rows + 2, width + 2 * EDGE, channels), F32)],
            12,
        )(up, first, middle, last, down, gfirst, gmiddle, glast)[0]
        for n in range(2)
    ]
    back_edge, *shares_edge = kernel_call(
        backward_edge_kernel, [lines, *share_outs], [framed(6)], 22
    )(gup, gfirst, gmiddle, glast, gdown, kern, w_turned)

    over_tokens = (((0,), (0,)), ((), ()))

    def collected(p0, p1, p2, p3):
        beside = flipped(p3, 1)
        theirs = (p2 + beside.astype(F32)).astype(BF)
        across = flipped(theirs, 2)
        kept = flipped(p1, 1)
        return p0, kept, across

    back_mid = back_mid.reshape(inner * width, 2 * channels)
    back_edge = back_edge.reshape(2 * width, 2 * channels)
    mid_parts = collected(*shares_mid)
    edge_parts = collected(*shares_edge)
    begun = kernel_call(
        finish_mid_kernel, [tile], [((inner, width, channels), BF)], 10,
        free=True, sems=(),
    )(*mid_parts)[0]
    input_grad = kernel_call(
        finish_edge_kernel, [tile], [((2, width, channels), BF)], 10,
        operands=3, free=True, alias=3, sems=(2,),
    )(*edge_parts, begun)[0]

    grad_w = lax.dot_general(gathered_mid, back_mid, over_tokens, preferred_element_type=F32)
    grad_w = lax.optimization_barrier(grad_w)
    grad_w = grad_w + lax.dot_general(
        gathered_edge, back_edge, over_tokens, preferred_element_type=F32
    )
    small = jnp.concatenate(
        [
            colp.astype(BF).reshape(owners, -1, channels),
            *(jnp.broadcast_to(v.astype(BF), (owners, 9, channels)) for v in shorts),
            jnp.zeros((owners, 2, channels), BF),
        ],
        axis=1,
    )
    small = lax.optimization_barrier(small)
    deep = parts * channels // owners
    packed = kernel_call(
        pack_kernel,
        [((owners, 2 * deep + per_owner + small.shape[1], channels), BF)],
        [((owners, 2 * deep + per_owner + small.shape[1], channels), BF)],
        16,
        scalars=1,
        operands=3,
        free=True,
        sems=(),
    )(ch.reshape(1), grad_w, row_part, small)[0]
    total = lax.all_to_all(packed, "grid", split_axis=0, concat_axis=0, tiled=True)
    sizes = (deep, deep, per_owner, height // owners)
    gate_grad, value_grad, row_share, col_share, short_sum = kernel_call(
        functools.partial(sum_kernel, scale=scale),
        [((size, channels), F32) for size in sizes] + [((3, 3, 2, channels), F32)],
        [],
        12,
    )(total)
    short_grad = short_sum.transpose(2, 0, 1, 3)
    return (gated, input_grad, gate_grad, value_grad, short_grad, row_share, col_share)


def solution(mesh):
    return jax.shard_map(
        local,
        mesh=mesh,
        in_specs=(
            P("grid", None, "ch"),
            P(None, "ch"),
            P(None, "ch"),
            P(None, None, None, "ch"),
            P(None, "ch"),
            P(None, "ch"),
            P("grid", None, "ch"),
        ),
        out_specs=(
            P("grid", None, "ch"),
            P("grid", None, "ch"),
            P("grid", "ch"),
            P("grid", "ch"),
            P(None, None, None, "ch"),
            P("grid", "ch"),
            P("grid", "ch"),
        ),
        check_vma=False,
    )
```

```python
import functools
import math

import jax
import jax.numpy as jnp
from jax import lax
from jax.experimental import pallas as pl
from jax.experimental.pallas import tpu as pltpu
from jax.sharding import PartitionSpec as P


BF = jnp.bfloat16
F32 = jnp.float32
EDGE = 8
STEP = 128


def cosine(phase, period):
    folded = phase & (period - 1)
    folded = jnp.minimum(folded, period - folded)
    y = (folded - period // 4).astype(F32) * (2.0 * math.pi / period)
    z = y * y
    series = 1.0 + z * (-1 / 6 + z * (1 / 120 + z * (-1 / 5040 + z * (1 / 362880 - z / 39916800))))
    return -(y * series)


def frequencies(slots, width, owners):
    per_owner = width // owners
    half = per_owner // 2
    place = slots & (per_owner - 1)
    top = slots == half
    freq = (slots // per_owner) * half + (place & (half - 1))
    freq = jnp.where(top, width // 2, freq)
    offset = jnp.where((place >= half) & ~top, width // 4, 0)
    return freq, offset


def turning(store, phase, step, period, count):
    quarter = period - period // 4
    c, s = cosine(phase, period), cosine(phase + quarter, period)
    dc, ds = cosine(step, period), cosine(step + quarter, period)
    for n in range(count):
        store(n, c)
        c, s = c * dc - s * ds, s * dc + c * ds


def column_matrix(height, sign):
    shape = (2 * height, 2 * height)
    i = lax.broadcasted_iota(jnp.int32, shape, 0)
    j = lax.broadcasted_iota(jnp.int32, shape, 1)
    turn = (jnp.where(j >= height, 1, 0) - jnp.where(i >= height, 1, 0)) * (-sign * (height // 4))
    return cosine((i & (height - 1)) * (j & (height - 1)) + turn + height, height)


def tables_kernel(
    where, w_gate, w_value, short_filter, row_filter, column_filter,
    mat, mat_t, mine, fwd, inv, coef, keep, colr, coli, kern, w_all, w_turned,
):
    ch, place = where[0], where[1]
    width, channels = row_filter.shape
    height = column_filter.shape[0]
    _, half, _ = coef.shape
    per_owner = 2 * half
    owners = width // per_owner
    shape = (16, 128)
    lane = lax.broadcasted_iota(jnp.int32, shape, 1)
    row = lax.broadcasted_iota(jnp.int32, shape, 0)

    def build(n, _):
        at = pl.multiple_of(n * 16, 16)
        freq, offset = frequencies(row + at, width, owners)

        def along(m, value):
            mat[pl.ds(at, 16), pl.ds(m * 128, 128)] = value.astype(BF)

        turning(along, freq * lane + offset, freq * 128, width, width // 128)
        token = row + at
        per_block = 128 // per_owner * half
        freq, offset = frequencies(lane + 128, width, owners)
        freq = freq - per_block
        highest = 1.0 - 2.0 * (token & 1).astype(F32)

        def across(m, value):
            if m == 0:
                value = jnp.where(lane == half, highest, value)
            mat_t[pl.ds(at, 16), pl.ds(m * 128, 128)] = value.astype(BF)

        turning(across, freq * token + offset, token * per_block, width, width // 128)
        return 0

    lax.fori_loop(0, width // 16, build, 0)
    fwd[...] = column_matrix(height, 1).astype(BF)
    inv[...] = column_matrix(height, -1).astype(BF)
    mine[...] = mat[pl.ds(pl.multiple_of(place * per_owner, per_owner), per_owner), :]
    rspec = jnp.dot(mine[...], row_filter[...], preferred_element_type=F32)
    first = lax.broadcasted_iota(jnp.int32, (half, channels), 0) == 0
    top = jnp.where(first, jnp.where(place == 0, 1.0, 0.0), 0.0)
    weight = (2.0 - top) * (1.0 / width)
    rre, rim = rspec[:half] * weight, rspec[half:] * weight
    rest = 1.0 - top
    coef[0] = rre
    coef[1] = -rim * rest
    coef[2] = rim * rest
    coef[3] = rre * rest + rim * top
    keep[0] = rest
    cspec = jnp.dot(fwd[:, pl.ds(0, height)], column_filter[...], preferred_element_type=F32)
    cspec = cspec * (1.0 / height)
    colr[...] = cspec[:height]
    coli[...] = cspec[height:]
    for b in range(2):
        for i in range(3):
            kern[pl.ds(b * 9 + i * 3, 3), :] = short_filter[b, i].astype(F32)
    parts = w_gate.shape[0] // channels
    for k in range(parts):
        at = pl.ds(pl.multiple_of((ch ^ k) * channels, channels), channels)
        to = pl.ds(k * channels, channels)
        w_all[to, pl.ds(0, channels)] = w_gate[at, :]
        w_all[to, pl.ds(channels, channels)] = w_value[at, :]
    w_turned[...] = w_all[...].astype(F32).T.astype(BF)


def fill_framed(framed, rows_of, channels):
    width = rows_of[0][0].shape[1]
    zeros = jnp.zeros((EDGE, channels), F32)
    for branch in range(2):
        for r in range(len(rows_of)):
            framed[branch, r, pl.ds(0, EDGE), :] = zeros
            framed[branch, r, pl.ds(EDGE + width, EDGE), :] = zeros

    def body(t, _):
        at = pl.multiple_of(t * 32, 32)
        for r, (ref, row) in enumerate(rows_of):
            for branch in range(2):
                v = ref[row, pl.ds(at, 32), pl.ds(branch * channels, channels)]
                framed[branch, r, pl.ds(EDGE + at, 32), :] = v.astype(F32)
        return 0

    lax.fori_loop(0, width // 32, body, 0)


def taps_of(kern, branch, channels):
    return [jnp.broadcast_to(kern[pl.ds(branch * 9 + k, 1), :], (8, channels)) for k in range(9)]


def projected(xs, w):
    size = 2 * xs[0].shape[1]
    total = None
    for n in range(len(xs) // 2):
        pair = jnp.concatenate([xs[2 * n][...], xs[2 * n + 1][...]], axis=1)
        part = jnp.dot(pair, w[pl.ds(n * size, size), :], preferred_element_type=F32)
        total = part if total is None else total + part
    return total.astype(BF)


def project_edge_kernel(x0, x1, x2, x3, w, first, last):
    width = first.shape[1]
    both = projected((x0, x1, x2, x3), w)
    first[0] = both[:width]
    last[0] = both[width:]


def project_mid_kernel(x0, x1, x2, x3, w, middle):
    middle[...] = projected((x0, x1, x2, x3), w).reshape(middle.shape)


def forward_kernel(up, first, middle, last, down, cot, kern, mat, send, feat, framed, cols):
    rows, width, channels = cot.shape
    owners, _, per_owner, _ = send.shape
    inner = [(middle, r) for r in range(rows - 2)]
    fill_framed(framed, [(up, 0), (first, 0), *inner, (last, 0), (down, 0)], channels)
    for branch in range(2):
        taps = taps_of(kern, branch, channels)

        def body(t, _, branch=branch, taps=taps):
            base = pl.multiple_of(t * STEP, STEP)
            done = [[] for _ in range(rows)]
            for p in range(STEP // 8):
                acc = [None] * rows
                for r in range(rows + 2):
                    for j in range(3):
                        v = framed[branch, r, pl.ds(base + 8 * p + EDGE + j - 1, 8), :]
                        for i in range(3):
                            o = r - i
                            if 0 <= o < rows:
                                term = taps[i * 3 + j] * v
                                acc[o] = term if acc[o] is None else acc[o] + term
                for o in range(rows):
                    done[o].append(acc[o])
            for o in range(rows):
                f = jnp.concatenate(done[o], axis=0).astype(BF)
                if branch == 0:
                    feat[o, pl.ds(base, STEP), :] = f
                    g = cot[o, pl.ds(base, STEP), :].astype(F32) * f.astype(F32)
                    cols[pl.ds(base, STEP), pl.ds((rows + o) * channels, channels)] = g.astype(BF)
                else:
                    cols[pl.ds(base, STEP), pl.ds(o * channels, channels)] = f
            return 0

        lax.fori_loop(0, width // STEP, body, 0)
    for n in range(rows):
        spec = jnp.dot(
            mat[...], cols[:, pl.ds(2 * n * channels, 2 * channels)], preferred_element_type=F32
        ).astype(BF)
        for e in range(2):
            send[:, 2 * n + e] = spec[:, e * channels : (e + 1) * channels].reshape(
                owners, per_owner, channels
            )


def column_kernel(
    recv, coef, keep, colr, coli, fwd, inv, mine, send, rowp, colp, stacked, spectra, er, ei
):
    owners, twice, per_owner, channels = recv.shape
    rows = twice // 2
    height = owners * rows
    half = per_owner // 2
    wide = half * channels
    group = 16 // rows

    def place(value, at, offset):
        turned = jnp.swapaxes(value, 0, 1)
        for k in range(half):
            lanes = pl.ds(k * channels + offset, channels)
            stacked[pl.ds(at, 16), lanes] = turned[k]
            stacked[pl.ds(at + height, 16), lanes] = turned[k + half]

    def unpack(n, _):
        at = pl.multiple_of(n * 16, 16)
        mixed = []
        for r in range(16):
            v = recv[n * group + r // rows, r % rows].astype(F32)
            br, bi = v[:half], v[half:]
            both = [br * coef[0] + bi * coef[1], br * coef[2] + bi * coef[3]]
            mixed.append(jnp.concatenate(both, axis=0).astype(BF))
        place(jnp.stack(mixed), at, 0)
        raw = [recv[n * group + r // rows, rows + r % rows] for r in range(16)]
        place(jnp.stack(raw), at, wide)
        return 0

    lax.fori_loop(0, height // 16, unpack, 0)
    several = 4

    def transform(matrix, n):
        for offset in (0, wide):
            lanes = pl.ds(n * several * channels + offset, several * channels)
            spectra[:, lanes] = jnp.dot(matrix[...], stacked[:, lanes], preferred_element_type=F32)

    def products(n):
        for at in range(0, height, 16):
            low, high = pl.ds(at, 16), pl.ds(at + height, 16)
            cr, ci = colr[low, :], coli[low, :]
            sr = si = None
            for k in range(n * several, (n + 1) * several):
                lanes = pl.ds(k * channels, channels)
                more = pl.ds(k * channels + wide, channels)
                tr, ti = spectra[low, lanes], spectra[high, lanes]
                fr, fi = spectra[low, more], spectra[high, more]
                pr, pi = fr * tr + fi * ti, fi * tr - fr * ti
                sr = pr if sr is None else sr + pr
                si = pi if si is None else si + pi
                stacked[low, lanes] = (tr * cr - ti * ci).astype(BF)
                stacked[high, lanes] = (tr * ci + ti * cr).astype(BF)
                stacked[low, more] = (fr * cr + fi * ci).astype(BF)
                stacked[high, more] = (fi * cr - fr * ci).astype(BF)
            er[low, :] = sr if n == 0 else er[low, :] + sr
            ei[low, :] = si if n == 0 else ei[low, :] + si

    steps = half // several
    transform(fwd, 0)
    for n in range(steps):
        if n + 1 < steps:
            transform(fwd, n + 1)
        products(n)
        transform(inv, n)

    e = jnp.concatenate([er[...], ei[...]], axis=0) * (1.0 / height)
    high = e.astype(BF)
    low = (e - high.astype(F32)).astype(BF)
    top = inv[pl.ds(0, height), :]
    colp[...] = jnp.dot(top, high, preferred_element_type=F32) + jnp.dot(
        top, low, preferred_element_type=F32
    )

    def pack(n, sums):
        p1, p2, p3 = sums
        at = pl.multiple_of(n * 16, 16)

        def taken(offset):
            slots = []
            for part in range(2):
                for k in range(half):
                    lanes = pl.ds(k * channels + offset, channels)
                    slots.append(spectra[pl.ds(at + part * height, 16), lanes])
            return jnp.stack(slots)

        mixed = jnp.swapaxes(taken(0).astype(BF), 0, 1)
        for r in range(16):
            send[n * group + r // rows, r % rows] = mixed[r]
        turned = jnp.swapaxes(taken(wide), 0, 1)
        for r in range(16):
            ar, ai = turned[r, :half], turned[r, half:]
            v = recv[n * group + r // rows, r % rows].astype(F32)
            br, bi = v[:half], v[half:]
            p1 = p1 + ar * br
            p2 = p2 + ai * bi
            p3 = p3 + (ai * br - ar * bi)
            both = [ar * coef[0] + ai * coef[2], ar * coef[1] + ai * coef[3]]
            send[n * group + r // rows, rows + r % rows] = jnp.concatenate(both, axis=0).astype(BF)
        return p1, p2, p3

    none = jnp.zeros((half, channels), F32)
    p1, p2, p3 = lax.fori_loop(0, height // 16, pack, (none, none, none))
    width = owners * per_owner
    kept = keep[0]
    twofold = (1.0 + kept) * (1.0 / width)
    qr = (p1 + kept * p2) * twofold
    qi = (kept * p3 + (1.0 - kept) * p2) * twofold
    rowp[...] = lax.dot_general(
        mine[...],
        jnp.concatenate([qr, qi], axis=0).astype(BF),
        (((0,), (0,)), ((), ())),
        preferred_element_type=F32,
    ).astype(BF)


def inverse_kernel(recv, mat, feat, cot, gated, first, middle, last):
    rows, width, channels = cot.shape
    for n in range(rows):
        spec = jnp.concatenate(
            [recv[:, 2 * n + e].reshape(width, channels) for e in range(2)], axis=1
        )
        back = jnp.dot(mat[...], spec, preferred_element_type=F32)
        for e in range(2):
            r = (2 * n + e) % rows
            value = back[:, e * channels : (e + 1) * channels]
            to, row = ((first, 0), *((middle, i) for i in range(rows - 2)), (last, 0))[r]
            if n < rows // 2:
                gated[r] = (feat[r].astype(F32) * value).astype(BF)
                to[row, :, pl.ds(0, channels)] = (cot[r].astype(F32) * value).astype(BF)
            else:
                to[row, :, pl.ds(channels, channels)] = value.astype(BF)


def spread_back(rows_at, kern, outs, width, channels):
    for branch in range(2):
        taps = taps_of(kern, branch, channels)

        def body(t, _, branch=branch, taps=taps):
            base = pl.multiple_of(t * STEP, STEP)
            done = [[] for _ in outs]
            for p in range(STEP // 8):
                acc = [None] * len(outs)
                needed = sorted({c + 1 - i for _, _, c in outs for i in range(3)})
                for r in needed:
                    for j in range(3):
                        ref, row = rows_at[r]
                        v = ref[branch, row, pl.ds(base + 8 * p + EDGE + 1 - j, 8), :]
                        for n, (_, _, c) in enumerate(outs):
                            i = c + 1 - r
                            if 0 <= i < 3:
                                term = taps[i * 3 + j] * v
                                acc[n] = term if acc[n] is None else acc[n] + term
                for n in range(len(outs)):
                    done[n].append(acc[n])
            for n, (ref, row, _) in enumerate(outs):
                value = jnp.concatenate(done[n], axis=0).astype(BF)
                ref[row, pl.ds(base, STEP), pl.ds(branch * channels, channels)] = value
            return 0

        lax.fori_loop(0, width // STEP, body, 0)


def shares(back, w_turned, p0, p1, p2, p3):
    tokens = back.shape[0] * back.shape[1]
    channels = p0.shape[1]
    total = jnp.dot(
        back[...].reshape(tokens, back.shape[2]), w_turned[...], preferred_element_type=F32
    )
    for k, p in enumerate((p0, p1, p2, p3)):
        p[...] = total[:, k * channels : (k + 1) * channels].astype(p.dtype)


def backward_mid_kernel(gfirst, gmiddle, glast, kern, w_turned, back, p0, p1, p2, p3, gframed):
    width = gfirst.shape[1]
    channels = kern.shape[1]
    inner = gmiddle.shape[0]
    fill_framed(
        gframed, [(gfirst, 0), *((gmiddle, r) for r in range(inner)), (glast, 0)], channels
    )
    rows_at = [(gframed, r) for r in range(inner + 2)]
    spread_back(rows_at, kern, [(back, r, r + 1) for r in range(inner)], width, channels)
    shares(back, w_turned, p0, p1, p2, p3)


def short_kernel(up, first, middle, last, down, gfirst, gmiddle, glast, short, framed, *, branch):
    width = first.shape[1]
    channels = short.shape[1]
    inner = middle.shape[0]
    rows = inner + 2
    lanes = pl.ds(branch * channels, channels)
    tokens = [(up, 0), (first, 0), *((middle, r) for r in range(inner)), (last, 0), (down, 0)]
    grads = [(gfirst, 0), *((gmiddle, r) for r in range(inner)), (glast, 0)]
    zeros = jnp.zeros((EDGE, channels), F32)
    for r in range(rows + 2):
        framed[r, pl.ds(0, EDGE), :] = zeros
        framed[r, pl.ds(EDGE + width, EDGE), :] = zeros

    def fill(t, _):
        at = pl.multiple_of(t * 32, 32)
        for r, (ref, row) in enumerate(tokens):
            framed[r, pl.ds(EDGE + at, 32), :] = ref[row, pl.ds(at, 32), lanes].astype(F32)
        return 0

    lax.fori_loop(0, width // 32, fill, 0)

    def terms(t, sums):
        base = pl.multiple_of(t * 16, 16)
        sums = list(sums)
        both = [ref[row, pl.ds(base, 16), lanes].astype(F32) for ref, row in grads]
        for p in range(2):
            at = base + 8 * p + EDGE
            g = [v[8 * p : 8 * p + 8] for v in both]
            for r in range(rows + 2):
                for j in range(3):
                    v = framed[r, pl.ds(at + j - 1, 8), :]
                    for i in range(3):
                        o = r - i
                        if 0 <= o < rows:
                            sums[i * 3 + j] = sums[i * 3 + j] + g[o] * v
        return tuple(sums)

    sums = lax.fori_loop(
        0, width // 16, terms, tuple(jnp.zeros((8, channels), F32) for _ in range(9))
    )
    for k in range(9):
        short[pl.ds(k, 1), :] = jnp.sum(sums[k], axis=0, keepdims=True)


def backward_edge_kernel(
    gup, gdown, gframed, kern, w_turned, back, p0, p1, p2, p3, around
):
    width = gup.shape[1]
    channels = kern.shape[1]
    last = gframed.shape[1] - 1
    fill_framed(around, [(gup, 0), (gdown, 0)], channels)
    own = [(gframed, r) for r in (0, 1, last - 1, last)]
    rows_at = [(around, 0), *own, (around, 1)]
    spread_back(rows_at, kern, [(back, 0, 1), (back, 1, 4)], width, channels)
    shares(back, w_turned, p0, p1, p2, p3)


def finish_mid_kernel(own, beside, across, grad, rows, sem):
    inner = grad.shape[0] - 2
    total = own[...] + beside[...].astype(F32) + across[...].astype(F32)
    rows[...] = total.astype(BF).reshape(rows.shape)
    copy = pltpu.make_async_copy(rows, grad.at[pl.ds(1, inner)], sem)
    copy.start()
    copy.wait()


def finish_edge_kernel(own, beside, across, middle, grad, rows, sems):
    width = grad.shape[1]
    copies = []
    for r in range(2):
        at = pl.ds(r * width, width)
        total = own[at, :] + beside[at, :].astype(F32) + across[at, :].astype(F32)
        rows[r] = total.astype(BF)
        to = r * (grad.shape[0] - 1)
        copies.append(pltpu.make_async_copy(rows.at[r], grad.at[to], sems.at[r]))
        copies[r].start()
    for copy in copies:
        copy.wait()


def sum_kernel(parts, *outs, scale):
    total = parts[0].astype(F32)
    for n in range(1, parts.shape[0]):
        total = total + parts[n].astype(F32)
    total = total * scale
    at = 0
    for out in outs[:-1]:
        out[...] = total[at : at + out.shape[0]]
        at += out.shape[0]
    short = outs[-1]
    for b in range(2):
        for k in range(9):
            row = at + 9 * b + k
            short[k // 3, k % 3, pl.ds(b, 1), :] = total[row : row + 1]


def pack_kernel(ch, grad_w, row_part, small, out, packed, sem):
    owners, _, channels = packed.shape
    parts = 4
    size = grad_w.shape[0] // parts
    each = owners // parts
    deep = size // each
    for k in range(parts):
        at = pl.ds((ch[0] ^ k) * each, each)
        for branch in range(2):
            v = grad_w[pl.ds(k * size, size), pl.ds(branch * channels, channels)].astype(BF)
            packed[at, pl.ds(branch * deep, deep), :] = v.reshape(each, deep, channels)
    per_owner = row_part.shape[0] // owners
    packed[:, pl.ds(2 * deep, per_owner), :] = row_part[...].reshape(owners, per_owner, channels)
    packed[:, pl.ds(2 * deep + per_owner, small.shape[1]), :] = small[...]
    copy = pltpu.make_async_copy(packed, out, sem)
    copy.start()
    copy.wait()


def kernel_call(
    body, outs, scratch, limit, scalars=0, operands=0, free=False, alias=None, sems=None
):
    specs = {}
    if scalars or alias is not None:
        whole = [pl.BlockSpec(memory_space=pltpu.SMEM)] * scalars
        whole += [pl.BlockSpec(memory_space=pltpu.VMEM)] * operands
        if alias is not None:
            whole += [pl.BlockSpec(memory_space=pltpu.HBM)]
            specs["input_output_aliases"] = {alias: 0}
        specs["in_specs"] = whole
    if free:
        specs["out_specs"] = [pl.BlockSpec(memory_space=pltpu.HBM)] * len(outs)
    semaphores = [] if sems is None else [pltpu.SemaphoreType.DMA(sems)]
    return pl.pallas_call(
        body,
        out_shape=[(pltpu.HBM if free else jax.ShapeDtypeStruct)(s, d) for s, d in outs],
        scratch_shapes=[pltpu.VMEM(s, d) for s, d in scratch] + semaphores,
        compiler_params=pltpu.CompilerParams(vmem_limit_bytes=limit << 20),
        **specs,
    )


def local(inputs, w_gate, w_value, short_filter, row_filter, column_filter, cotangent):
    rows, width, channels = inputs.shape
    owners = lax.axis_size("grid")
    parts = lax.axis_size("ch")
    height = column_filter.shape[0]
    per_owner = width // owners
    half = per_owner // 2
    inner = rows - 2
    scale = 1.0 / math.sqrt(height * width)
    ch = lax.axis_index("ch")
    place = lax.axis_index("grid")

    def flipped(value, bit):
        return lax.ppermute(value, "ch", [(i, i ^ bit) for i in range(parts)])

    def halos(first, last):
        up = lax.ppermute(last, "grid", [(i, i + 1) for i in range(owners - 1)])
        down = lax.ppermute(first, "grid", [(i + 1, i) for i in range(owners - 1)])
        return up, down

    edge = jnp.concatenate([inputs[0], inputs[rows - 1]], axis=0)
    mid = inputs[1 : rows - 1].reshape(inner * width, channels)
    edge_across = flipped(edge, 2)
    mid_across = flipped(mid, 2)
    edge_beside = flipped(edge, 1)
    mid_beside = flipped(mid, 1)
    edge_corner = flipped(edge_across, 1)

    (mat, mat_t, mine, fwd, inv, coef, keep, colr, coli, kern, w_all, w_turned) = kernel_call(
        tables_kernel,
        [
            ((width, width), BF),
            ((width, width), BF),
            ((per_owner, width), BF),
            ((2 * height, 2 * height), BF),
            ((2 * height, 2 * height), BF),
            ((4, half, channels), F32),
            ((1, half, channels), F32),
            ((height, channels), F32),
            ((height, channels), F32),
            ((18, channels), F32),
            ((parts * channels, 2 * channels), BF),
            ((2 * channels, parts * channels), BF),
        ],
        [],
        12,
        scalars=1,
        operands=5,
    )(jnp.stack([ch, place]), w_gate, w_value, short_filter, row_filter, column_filter)

    line = ((1, width, 2 * channels), BF)
    lines = ((inner, width, 2 * channels), BF)
    edge_blocks = (edge, edge_beside, edge_across, edge_corner)
    first, last = kernel_call(project_edge_kernel, [line, line], [], 12)(*edge_blocks, w_all)
    up, down = halos(first, last)
    mid_corner = flipped(mid_across, 1)
    mid_blocks = (mid, mid_beside, mid_across, mid_corner)
    middle = kernel_call(project_mid_kernel, [lines], [], 12)(*mid_blocks, w_all)[0]
    middle, edge_blocks, mid_blocks = lax.optimization_barrier((middle, edge_blocks, mid_blocks))
    gathered_edge = jnp.concatenate(edge_blocks, axis=1)
    gathered_mid = jnp.concatenate(mid_blocks, axis=1)

    def framed(count):
        return ((2, count, width + 2 * EDGE, channels), F32)

    spread = ((owners, 2 * rows, per_owner, channels), BF)
    tile = ((rows, width, channels), BF)
    send, feat = kernel_call(
        forward_kernel, [spread, tile], [framed(rows + 2), ((width, 2 * rows * channels), BF)], 24
    )(up, first, middle, last, down, cotangent, kern, mat)
    recv = lax.all_to_all(send, "grid", split_axis=0, concat_axis=0, tiled=True)
    tall = (2 * height, 2 * half * channels)
    turned, row_part, colp = kernel_call(
        column_kernel,
        [spread, ((width, channels), BF), ((height, channels), F32)],
        [(tall, BF), (tall, F32), ((height, channels), F32), ((height, channels), F32)],
        20,
    )(recv, coef, keep, colr, coli, fwd, inv, mine)
    returned = lax.all_to_all(turned, "grid", split_axis=0, concat_axis=0, tiled=True)
    gated, gfirst, gmiddle, glast = kernel_call(
        inverse_kernel, [tile, line, lines, line], [], 20
    )(returned, mat_t, feat, cotangent)
    gup, gdown = halos(gfirst, glast)
    share = (2 * width, channels)
    share_outs = [(share, F32), (share, BF), (share, BF), (share, BF)]
    back_mid, *shares_mid, gframed = kernel_call(
        backward_mid_kernel, [lines, *share_outs, framed(rows)], [], 20
    )(gfirst, gmiddle, glast, kern, w_turned)
    shorts = [
        kernel_call(
            functools.partial(short_kernel, branch=n),
            [((9, channels), F32)],
            [((rows + 2, width + 2 * EDGE, channels), F32)],
            12,
        )(up, first, middle, last, down, gfirst, gmiddle, glast)[0]
        for n in range(2)
    ]
    back_edge, *shares_edge = kernel_call(
        backward_edge_kernel, [lines, *share_outs], [framed(2)], 20
    )(gup, gdown, gframed, kern, w_turned)

    over_tokens = (((0,), (0,)), ((), ()))

    def collected(p0, p1, p2, p3):
        beside = flipped(p3, 1)
        theirs = (p2.astype(F32) + beside.astype(F32)).astype(BF)
        across = flipped(theirs, 2)
        kept = flipped(p1, 1)
        return p0, kept, across

    back_mid = back_mid.reshape(inner * width, 2 * channels)
    back_edge = back_edge.reshape(2 * width, 2 * channels)
    mid_parts = collected(*shares_mid)
    edge_parts = collected(*shares_edge)
    begun = kernel_call(
        finish_mid_kernel, [tile], [((inner, width, channels), BF)], 10,
        free=True, sems=(),
    )(*mid_parts)[0]
    input_grad = kernel_call(
        finish_edge_kernel, [tile], [((2, width, channels), BF)], 10,
        operands=3, free=True, alias=3, sems=(2,),
    )(*edge_parts, begun)[0]

    grad_w = lax.dot_general(gathered_mid, back_mid, over_tokens, preferred_element_type=F32)
    grad_w = lax.optimization_barrier(grad_w)
    grad_w = grad_w + lax.dot_general(
        gathered_edge, back_edge, over_tokens, preferred_element_type=F32
    )
    small = jnp.concatenate(
        [
            colp.astype(BF).reshape(owners, -1, channels),
            *(jnp.broadcast_to(v.astype(BF), (owners, 9, channels)) for v in shorts),
            jnp.zeros((owners, 2, channels), BF),
        ],
        axis=1,
    )
    small = lax.optimization_barrier(small)
    deep = parts * channels // owners
    packed = kernel_call(
        pack_kernel,
        [((owners, 2 * deep + per_owner + small.shape[1], channels), BF)],
        [((owners, 2 * deep + per_owner + small.shape[1], channels), BF)],
        16,
        scalars=1,
        operands=3,
        free=True,
        sems=(),
    )(ch.reshape(1), grad_w, row_part, small)[0]
    total = lax.all_to_all(packed, "grid", split_axis=0, concat_axis=0, tiled=True)
    sizes = (deep, deep, per_owner, height // owners)
    gate_grad, value_grad, row_share, col_share, short_sum = kernel_call(
        functools.partial(sum_kernel, scale=scale),
        [((size, channels), F32) for size in sizes] + [((3, 3, 2, channels), F32)],
        [],
        12,
    )(total)
    short_grad = short_sum.transpose(2, 0, 1, 3)
    return (gated, input_grad, gate_grad, value_grad, short_grad, row_share, col_share)


def solution(mesh):
    return jax.shard_map(
        local,
        mesh=mesh,
        in_specs=(
            P("grid", None, "ch"),
            P(None, "ch"),
            P(None, "ch"),
            P(None, None, None, "ch"),
            P(None, "ch"),
            P(None, "ch"),
            P("grid", None, "ch"),
        ),
        out_specs=(
            P("grid", None, "ch"),
            P("grid", None, "ch"),
            P("grid", "ch"),
            P("grid", "ch"),
            P(None, None, None, "ch"),
            P("grid", "ch"),
            P("grid", "ch"),
        ),
        check_vma=False,
    )
```
